256 devices in a mesh: dp: 32 (over x, z), tensor: 8 (over y, core).
Axes of the slice: x: 4, y: 4, z: 8, core: 2. Of those that a mesh axis runs over, the one named last changes fastest.
Arguments:
- hidden: bfloat16 [8192, 8192], P(('dp', 'tensor')), may hold values from -6 to 6
- cotangent: bfloat16 [8192, 2048], P('dp', 'tensor'), may hold values from -6 to 6
- frozen_key_value: bfloat16 [8192, 2048], P(None, 'tensor'), may hold values from -0.0625 to 0.0625
- adapter_down_factors: bfloat16 [8192, 2048], P('tensor'), may hold values from -0.0625 to 0.0625
- adapter_up_factors: bfloat16 [2048, 2048], P(None, 'tensor'), may hold values from -0.75 to 0.75
- down_master_copy: float32 [8192, 2048], P('tensor', 'dp'), may hold values from -0.0625 to 0.0625
- down_first_moment: float32 [8192, 2048], P('tensor', 'dp'), may hold values from -1.5 to 1.5
- down_second_moment: float32 [8192, 2048], P('tensor', 'dp'), may hold values from 0.001 to 0.05
- up_master_copy: float32 [2048, 2048], P('dp', 'tensor'), may hold values from -0.75 to 0.75
- up_first_moment: float32 [2048, 2048], P('dp', 'tensor'), may hold values from -0.3125 to 0.3125
- up_second_moment: float32 [2048, 2048], P('dp', 'tensor'), may hold values from 1e-05 to 0.001
- adapter_of_token: int32 [8192, 1], P('dp'), may hold values from 0 to 31; in each aligned block of 256 rows (0 to 255, 256 to 511, ...) at most 16 rows name the same one
- adapter_rank_bucket: int32 [32], replicated, may hold values from 0 to 3
- adapter_owner_slot: int32 [32], replicated, may hold values from 0 to 31, each once
- live_token_counts: int32 [32], replicated, may hold values from 64 to 256, as said below
Outputs:
- hidden_gradient: bfloat16 [8192, 8192], P(('dp', 'tensor'))
- new_down_master: float32 [8192, 2048], P('tensor', 'dp')
- new_down_moment: float32 [8192, 2048], P('tensor', 'dp')
- new_down_second: float32 [8192, 2048], P('tensor', 'dp')
- new_up_master: float32 [2048, 2048], P('dp', 'tensor')
- new_up_moment: float32 [2048, 2048], P('dp', 'tensor')
- new_up_second: float32 [2048, 2048], P('dp', 'tensor')
The draws below stay inside these ranges and needn't reach their ends.
Inputs may be any that keep to these rules, and one draw needn't show every extreme that they name: `adapter_of_token`: in the rows of one index of dp (aligned blocks of 256 rows) no adapter is named by more than 16 rows, and some adapter reaches 16; every adapter is named somewhere. `adapter_owner_slot`: each slot once. `live_token_counts`: some shard is full.
All inputs are finite; a program needn't handle non-finite values.
Results may differ from the reference program's by a relative error of at most 0.0034.
Values may be sent and summed in bfloat16 or wider, within the bound.
No kernel may reach another device: no remote copies, remote signals or barrier semaphores. Data moves between devices by JAX's collectives and lax.ppermute only.
A program may use at most 128 MiB of HBM per device.

```python
import math
import jax
import jax.numpy as jnp
import numpy as np
from jax import lax

MODEL_WIDTH = 8192
KEY_VALUE_WIDTH = 2048
TOK_DEV = 256
RMIN = 8
PADDED_RANK = 64
ADAPTER_COUNT = 32
SHARDS = 32
TOKEN_SLOTS = 8192
CAP = 16


def draw_live_token_counts(key, part):
    first_key = jax.random.fold_in(key, 11)
    second_key = jax.random.fold_in(key, 12)
    counts_all = jax.random.randint(first_key, (SHARDS,), TOK_DEV // 4, TOK_DEV + 1)
    full_shard = jax.random.randint(second_key, (), 0, SHARDS)
    return jnp.where(jnp.arange(SHARDS) == full_shard, TOK_DEV, counts_all).astype(jnp.int32)


def set_ends(result, own_key, low, top_value):
    longest = result.shape.index(max(result.shape))
    spots = []
    for shift in (0, 1):
        where = [jax.random.randint(jax.random.fold_in(own_key, axis), (), 0, length) for axis, length in enumerate(result.shape)]
        where[longest] = (where[longest] + shift) % result.shape[longest]
        spots.append(tuple(where))
    return result.at[spots[0]].set(low).at[spots[1]].set(top_value)


def block_levels(key, dims, split, least, top_value):
    loudness = 1.0
    for dim, shards_of in split:
        heights = jax.random.uniform(jax.random.fold_in(jax.random.fold_in(key, 6), dim), (shards_of,), jnp.float32, least / len(split), top_value / len(split))
        loudness = loudness * jnp.repeat(jnp.exp(heights), dims[dim] // shards_of).reshape((-1,) + (1,) * (len(dims) - 1 - dim))
    return loudness


def shared_out(key, own, number, rows, number_of, top, bound, lean):
    ranking = jax.random.permutation(key, number_of)
    packed, ordinary = portions_of(number_of, rows * top, bound, lean, True), portions_of(number_of, rows * top, bound, lean, False)
    places = jnp.arange(number_of)

    def named(lengths, offset_by):
        used = int((lengths > 0).sum())
        fixed = max(1, used // 4)
        moved = fixed + (places - fixed + offset_by * (used - fixed)) % max(1, number_of - fixed)
        return jnp.zeros((number_of,), jnp.int32).at[ranking[jnp.where(places < fixed, places, moved)]].set(jnp.asarray(lengths, jnp.int32))

    lengths = jnp.where(number % 4 == 0, named(packed, number // 4), named(ordinary, number - number // 4 - 1))
    mixed = jax.random.permutation(jax.random.fold_in(own, 3), number_of)
    donor, taker = mixed[0:number_of // 2 * 2:2], mixed[1:number_of // 2 * 2:2]
    margin = jnp.minimum(lengths[donor] - 1, bound - lengths[taker]) // 2
    margin = jnp.where((donor == ranking[0]) | (taker == ranking[0]) | (lengths[taker] == 0), 0, jnp.maximum(margin, 0))
    moved = jax.random.randint(jax.random.fold_in(own, 4), (number_of // 2,), 0, 1 << 20) % (margin + 1)
    lengths = lengths.at[donor].add(-moved).at[taker].add(moved)
    labels = jnp.searchsorted(jnp.cumsum(lengths), jnp.arange(rows * top), side="right").astype(jnp.int32)
    listing = labels.reshape(top, rows).T
    listing = listing[jax.random.permutation(jax.random.fold_in(own, 1), rows)]
    offset_by = jax.random.randint(jax.random.fold_in(own, 2), (rows, 1), 0, top)
    return jnp.take_along_axis(listing, (jnp.arange(top)[None, :] + offset_by) % top, axis=1)


def portions_of(count, total, limit, lean, full):
    weights = [(1 << 20) // math.isqrt(standing ** lean) + 1 for standing in range(1, count + 1)]
    largest = limit if full else min(limit, max(-(-total // count), total * weights[0] // sum(weights)))
    least = 1 if total - largest >= count - 1 else 0
    counts, spare = [largest] + [least] * (count - 1), total - largest - least * (count - 1)
    while spare > 0:
        candidates = [i for i in range(1, count) if counts[i] < largest] or [i for i in range(1, count) if counts[i] < limit]
        whole, left = sum([weights[i] for i in candidates]), spare
        for i in candidates:
            more = min(limit - counts[i], max(1, left * weights[i] // whole), spare)
            counts[i] = counts[i] + more
            spare = spare - more
    return np.array(counts)


def scatter_about(stream_key, dims, spread, reach, pieces=(), kind=jnp.bfloat16):
    entries = jax.random.normal(stream_key, dims, jnp.float32) * spread
    if len(pieces) > 0:
        entries = block_levels(stream_key, dims, pieces, -0.22, 0.18) * entries
    return jnp.clip(entries, min=-reach, max=reach).astype(kind)


def setup_inputs(seed: int = 0) -> dict:
    key_of = jax.random.split(jax.random.key(seed), 16)
    hidden = scatter_about(key_of[0], (TOKEN_SLOTS, MODEL_WIDTH), 1.0, 6.0, ((0, 256),))
    cotangent = scatter_about(key_of[1], (TOKEN_SLOTS, KEY_VALUE_WIDTH), 1.0, 6.0, ((0, 32), (1, 8)))
    frozen_key_value = scatter_about(key_of[2], (MODEL_WIDTH, KEY_VALUE_WIDTH), MODEL_WIDTH ** -0.5, 0.0625, ((1, 8),))
    adapter_down_factors = scatter_about(key_of[3], (MODEL_WIDTH, ADAPTER_COUNT * PADDED_RANK), MODEL_WIDTH ** -0.5, 0.0625, ((0, 8),))
    adapter_up_factors = scatter_about(key_of[4], (ADAPTER_COUNT * PADDED_RANK, KEY_VALUE_WIDTH), PADDED_RANK ** -0.5, 0.75, ((1, 8),))
    down_master_copy = scatter_about(key_of[5], (MODEL_WIDTH, ADAPTER_COUNT * PADDED_RANK), MODEL_WIDTH ** -0.5, 0.0625, ((0, 8), (1, 32)), jnp.float32)
    down_first_moment = scatter_about(key_of[6], (MODEL_WIDTH, ADAPTER_COUNT * PADDED_RANK), 0.1, 1.5, ((0, 8), (1, 32)), jnp.float32)
    down_second_moment = jnp.clip(jnp.exp(math.log(0.05) - 3.912023 * jax.random.uniform(key_of[7], (MODEL_WIDTH, ADAPTER_COUNT * PADDED_RANK), jnp.float32) ** block_levels(key_of[7], (MODEL_WIDTH, ADAPTER_COUNT * PADDED_RANK), ((0, 8), (1, 32)), -0.2, 0.2)), 0.001, 0.05)
    up_master_copy = scatter_about(key_of[8], (ADAPTER_COUNT * PADDED_RANK, KEY_VALUE_WIDTH), PADDED_RANK ** -0.5, 0.75, ((0, 32), (1, 8)), jnp.float32)
    up_first_moment = scatter_about(key_of[9], (ADAPTER_COUNT * PADDED_RANK, KEY_VALUE_WIDTH), 0.02, 0.3125, ((0, 32), (1, 8)), jnp.float32)
    up_second_moment = jnp.clip(jnp.exp(math.log(0.001) - 4.6051703 * jax.random.uniform(key_of[10], (ADAPTER_COUNT * PADDED_RANK, KEY_VALUE_WIDTH), jnp.float32) ** block_levels(key_of[10], (ADAPTER_COUNT * PADDED_RANK, KEY_VALUE_WIDTH), ((0, 32), (1, 8)), -0.2, 0.2)), 9.999999747378752e-06, 0.001)
    adapter_of_token_keys = jax.random.split(jax.random.fold_in(key_of[11], 1), TOKEN_SLOTS // TOK_DEV)
    adapter_of_token_turns = jax.random.permutation(jax.random.fold_in(key_of[11], 3), TOKEN_SLOTS // TOK_DEV)
    adapter_of_token = jax.vmap(lambda own, number: shared_out(jax.random.fold_in(key_of[11], 2), own, number, TOK_DEV, ADAPTER_COUNT, 1, CAP, 2))(adapter_of_token_keys, adapter_of_token_turns).reshape((TOKEN_SLOTS, 1))
    adapter_rank_bucket = set_ends(jax.random.randint(key_of[12], (ADAPTER_COUNT,), 0, 4), jax.random.fold_in(key_of[12], 1), 0, 3).astype(jnp.int32)
    adapter_owner_slot = jax.random.permutation(key_of[13], ADAPTER_COUNT).astype(jnp.int32)
    live_token_counts = draw_live_token_counts(jax.random.fold_in(key_of[15], 71), 0)
    return dict(hidden=hidden, cotangent=cotangent, frozen_key_value=frozen_key_value, adapter_down_factors=adapter_down_factors, adapter_up_factors=adapter_up_factors, down_master_copy=down_master_copy, down_first_moment=down_first_moment, down_second_moment=down_second_moment, up_master_copy=up_master_copy, up_first_moment=up_first_moment, up_second_moment=up_second_moment, adapter_of_token=adapter_of_token, adapter_rank_bucket=adapter_rank_bucket, adapter_owner_slot=adapter_owner_slot, live_token_counts=live_token_counts)


adapter_alpha_scale = 16.0
beta_one = 0.9
beta_two = 0.999
adam_eps = 1e-08
learn_rate = 0.0002
weight_decay = 0.1
first_fix = 0.9999734386011124
second_fix = 0.09520785288629038

def adapter_tables(adapter_of_token, adapter_rank_bucket, adapter_owner_slot):
    adapter = adapter_of_token[:, 0]
    idents = jnp.arange(adapter_owner_slot.shape[0], dtype=jnp.int32)
    slot_hit = (adapter[:, None] == idents[None, :]).astype(jnp.int32)
    slot_of = lax.optimization_barrier(jnp.sum(slot_hit * adapter_owner_slot[None, :], axis=1))
    bucket = lax.optimization_barrier(jnp.sum(slot_hit * adapter_rank_bucket[None, :], axis=1))
    steps_up = 1 + (bucket >= 1).astype(jnp.int32) + 2 * (bucket >= 2).astype(jnp.int32) + 4 * (bucket >= 3).astype(jnp.int32)
    return (slot_of, RMIN * steps_up)

def adamw(master, moment, second, grad):
    new_moment = beta_one * moment + (1.0 - beta_one) * grad
    new_second = beta_two * second + (1.0 - beta_two) * grad * grad
    update = new_moment / first_fix / (jnp.sqrt(new_second / second_fix) + adam_eps)
    new_master = master - learn_rate * (update + weight_decay * master)
    return (new_master, new_moment, new_second)

def reference(hidden, cotangent, frozen_key_value, adapter_down_factors, adapter_up_factors, down_master_copy, down_first_moment, down_second_moment, up_master_copy, up_first_moment, up_second_moment, adapter_of_token, adapter_rank_bucket, adapter_owner_slot, live_token_counts):
    rows_all = jnp.arange(TOKEN_SLOTS, dtype=jnp.int32)
    row_limit = jnp.take(live_token_counts, rows_all // TOK_DEV)
    is_valid = rows_all % TOK_DEV < row_limit
    masked_cotangent = jnp.where(is_valid[:, None], cotangent, jnp.zeros_like(cotangent))
    slot_of, rank_lookup = adapter_tables(adapter_of_token, adapter_rank_bucket, adapter_owner_slot)
    kept_cols = jnp.arange(PADDED_RANK, dtype=jnp.int32)[None, :] < rank_lookup[:, None]
    alpha_rank_ratio = (adapter_alpha_scale / rank_lookup.astype(jnp.float32))[:, None]
    factor = jnp.where(kept_cols, alpha_rank_ratio, jnp.zeros_like(alpha_rank_ratio))
    down_three_dimensional = adapter_down_factors.reshape(MODEL_WIDTH, ADAPTER_COUNT, PADDED_RANK)
    up_three_dimensional = adapter_up_factors.reshape(ADAPTER_COUNT, PADDED_RANK, KEY_VALUE_WIDTH)
    block = 64
    blocks_n = TOKEN_SLOTS // block

    def per_block(loop_carried, block_items):
        x_block, c_block, s_block, f_block = block_items
        adapter_per_token = jnp.take(down_three_dimensional, s_block, axis=1).astype(jnp.float32)
        b_tok = jnp.take(up_three_dimensional, s_block, axis=0).astype(jnp.float32)
        low_down = jnp.einsum('td,dtk->tk', x_block.astype(jnp.float32), adapter_per_token)
        low_up = jnp.einsum('tc,tkc->tk', c_block.astype(jnp.float32), b_tok)
        down_weight = (low_down * f_block).astype(jnp.bfloat16)
        up_weight = (low_up * f_block).astype(jnp.bfloat16)
        adapter_extra_output = jnp.einsum('wg,uwg->wu', up_weight.astype(jnp.float32), adapter_per_token)
        outer = jnp.einsum('td,tk->dtk', x_block.astype(jnp.float32), up_weight.astype(jnp.float32))
        loop_carried = loop_carried.at[:, s_block, :].add(outer)
        return (loop_carried, (down_weight, adapter_extra_output))
    start_grad = jnp.zeros((MODEL_WIDTH, ADAPTER_COUNT, PADDED_RANK), jnp.float32)
    block_items = (hidden.reshape(blocks_n, block, MODEL_WIDTH), masked_cotangent.reshape(blocks_n, block, KEY_VALUE_WIDTH), slot_of.reshape(blocks_n, block), factor.reshape(blocks_n, block, PADDED_RANK))
    grad_three, output_values = lax.scan(per_block, start_grad, block_items)
    down_weight = output_values[0].reshape(TOKEN_SLOTS, PADDED_RANK)
    adapter_extra_output = output_values[1].reshape(TOKEN_SLOTS, MODEL_WIDTH)
    frozen_input_term = lax.dot_general(masked_cotangent, frozen_key_value, (((1,), (1,)), ((), ())), preferred_element_type=jnp.float32)
    hidden_gradient = (frozen_input_term + adapter_extra_output).astype(jnp.bfloat16)
    idents = jnp.arange(ADAPTER_COUNT, dtype=jnp.int32)
    slot_hit = (slot_of[:, None] == idents[None, :]).astype(jnp.bfloat16)
    placed_down = (down_weight[:, None, :] * slot_hit[:, :, None]).reshape(TOKEN_SLOTS, ADAPTER_COUNT * PADDED_RANK)
    grad_up = lax.dot_general(placed_down, masked_cotangent, (((0,), (0,)), ((), ())), preferred_element_type=jnp.float32) / TOK_DEV
    grad_down = grad_three.reshape(MODEL_WIDTH, ADAPTER_COUNT * PADDED_RANK) / TOK_DEV
    new_dm, new_dmo, new_ds = adamw(down_master_copy, down_first_moment, down_second_moment, grad_down)
    new_um, new_umo, new_us = adamw(up_master_copy, up_first_moment, up_second_moment, grad_up)
    return (hidden_gradient, new_dm, new_dmo, new_ds, new_um, new_umo, new_us)
```

```python
import jax
import jax.numpy as jnp
from jax import lax
from jax.sharding import PartitionSpec as P

RMIN = 8
PADDED_RANK = 64
CAP = 16


adapter_alpha_scale = 16.0
beta_one = 0.9
beta_two = 0.999
adam_eps = 1e-08
learn_rate = 0.0002
weight_decay = 0.1
first_fix = 0.9999734386011124
second_fix = 0.09520785288629038


def adapter_tables(adapter_of_token, adapter_rank_bucket, adapter_owner_slot):
    adapter = adapter_of_token[:, 0]
    idents = jnp.arange(adapter_owner_slot.shape[0], dtype=jnp.int32)
    slot_hit = (adapter[:, None] == idents[None, :]).astype(jnp.int32)
    slot_of = jnp.sum(slot_hit * adapter_owner_slot[None, :], axis=1)
    bucket = jnp.sum(slot_hit * adapter_rank_bucket[None, :], axis=1)
    steps_up = (
        1
        + (bucket >= 1).astype(jnp.int32)
        + 2 * (bucket >= 2).astype(jnp.int32)
        + 4 * (bucket >= 3).astype(jnp.int32)
    )
    return (slot_of, RMIN * steps_up)


def adamw(master, moment, second, grad):
    new_moment = beta_one * moment + (1.0 - beta_one) * grad
    new_second = beta_two * second + (1.0 - beta_two) * grad * grad
    update = new_moment / first_fix / (jnp.sqrt(new_second / second_fix) + adam_eps)
    new_master = master - learn_rate * (update + weight_decay * master)
    return (new_master, new_moment, new_second)


def contract_helper(left, right, left_dim, right_dim):
    return lax.dot_general(
        left, right, (((left_dim,), (right_dim,)), ((), ())), preferred_element_type=jnp.float32
    )


def swap(value, mask, count):
    return lax.ppermute(value, "tensor", [(i, i ^ mask) for i in range(count)])


def sum_over_tensor(value, count):
    mask = 1
    while mask < count:
        value = value + swap(value, mask, count)
        mask *= 2
    return value


def local(
    hidden,
    cotangent,
    frozen_key_value,
    adapter_down_factors,
    adapter_up_factors,
    down_master_copy,
    down_first_moment,
    down_second_moment,
    up_master_copy,
    up_first_moment,
    up_second_moment,
    adapter_of_token,
    adapter_rank_bucket,
    adapter_owner_slot,
    live_token_counts,
):
    n_tensor = lax.axis_size("tensor")
    n_chip = n_tensor // 2
    tokens = cotangent.shape[0]
    width = hidden.shape[1]
    rows_own = hidden.shape[0]
    columns = width // n_tensor
    n_slot = adapter_owner_slot.shape[0]
    position = lax.axis_index("tensor")
    chip, core = position // 2, position % 2

    blocks = hidden.reshape(rows_own, n_tensor, columns).transpose(1, 0, 2)
    hidden_columns = lax.all_to_all(blocks, "tensor", 0, 0, tiled=True).reshape(tokens, columns)

    row_limit = lax.dynamic_index_in_dim(live_token_counts, lax.axis_index("dp"), 0, keepdims=False)
    is_valid = jnp.arange(tokens, dtype=jnp.int32) < row_limit
    masked_cotangent = jnp.where(is_valid[:, None], cotangent, jnp.zeros_like(cotangent))
    slot_of, rank_lookup = adapter_tables(adapter_of_token, adapter_rank_bucket, adapter_owner_slot)
    idents = jnp.arange(n_slot, dtype=jnp.int32)
    slot_hit = (slot_of[:, None] == idents[None, :]).astype(jnp.float32)
    hit_half = slot_hit.astype(jnp.bfloat16)
    kept_cols = jnp.arange(PADDED_RANK, dtype=jnp.int32)[None, :] < rank_lookup[:, None]
    alpha_rank_ratio = (adapter_alpha_scale / rank_lookup.astype(jnp.float32))[:, None]
    factor = jnp.where(kept_cols, alpha_rank_ratio, jnp.zeros_like(alpha_rank_ratio))

    order = jnp.arange(tokens, dtype=jnp.int32)
    earlier = (slot_of[:, None] == slot_of[None, :]) & (order[:, None] < order[None, :])
    rank_in_slot = jnp.sum(earlier.astype(jnp.int32), axis=0)
    packed_row = slot_of * CAP + rank_in_slot
    pack = (
        jnp.arange(n_slot * CAP, dtype=jnp.int32)[:, None] == packed_row[None, :]
    ).astype(jnp.bfloat16)

    by_core = masked_cotangent.reshape(n_chip, 2, rows_own, cotangent.shape[1])
    theirs = lax.dynamic_index_in_dim(by_core, 1 - core, 1, keepdims=False).reshape(
        tokens // 2, -1
    )
    ours = lax.dynamic_index_in_dim(by_core, core, 1, keepdims=False).reshape(tokens // 2, -1)
    frozen_theirs = contract_helper(theirs, frozen_key_value, 1, 1)
    frozen_from_pair = swap(frozen_theirs, 1, n_tensor)
    frozen_ours = contract_helper(ours, frozen_key_value, 1, 1)

    up_partial = contract_helper(masked_cotangent, adapter_up_factors, 1, 1).reshape(
        tokens, n_slot, PADDED_RANK
    )
    up_own = jnp.einsum("tsk,ts->tk", up_partial, slot_hit)
    up_weight = (sum_over_tensor(up_own, n_tensor) * factor).astype(jnp.bfloat16)
    positioned_up = (up_weight[:, None, :] * hit_half[:, :, None]).reshape(
        tokens, n_slot * PADDED_RANK
    )
    extra = contract_helper(positioned_up, adapter_down_factors, 1, 1)
    extra_by_core = extra.reshape(n_chip, 2, rows_own, columns)
    extra_theirs = lax.dynamic_index_in_dim(extra_by_core, 1 - core, 1, keepdims=False).reshape(
        tokens // 2, columns
    )
    extra_ours = lax.dynamic_index_in_dim(extra_by_core, core, 1, keepdims=False).reshape(
        tokens // 2, columns
    )
    extra_from_pair = swap(extra_theirs, 1, n_tensor)
    extra_low = jnp.where(core == 0, extra_ours, extra_from_pair)
    extra_high = jnp.where(core == 0, extra_from_pair, extra_ours)
    extra_pair = jnp.concatenate([extra_low, extra_high], axis=1)
    chip_hit = (jnp.arange(n_chip, dtype=jnp.int32) == chip)[None, :, None]
    pair_sum = (frozen_ours + frozen_from_pair).reshape(tokens // 2, n_chip, 2 * columns)
    pair_sum = pair_sum + jnp.where(chip_hit, extra_pair[:, None, :], 0.0)
    pair_sum = pair_sum.reshape(n_chip, rows_own, width)
    total = lax.dynamic_index_in_dim(pair_sum, chip, 0, keepdims=False)
    for step in (1, n_chip - 1, 2):
        out_block = lax.dynamic_index_in_dim(
            pair_sum, (chip + step) % n_chip, 0, keepdims=False
        ).astype(jnp.bfloat16)
        arrived = lax.ppermute(
            out_block, "tensor", [(i, (i + 2 * step) % n_tensor) for i in range(n_tensor)]
        )
        total = total + arrived.astype(jnp.float32)
    hidden_gradient = total.astype(jnp.bfloat16)

    rows = jnp.concatenate([hidden_columns, masked_cotangent], axis=1)
    packed = jnp.dot(pack, rows, preferred_element_type=jnp.float32).astype(jnp.bfloat16)
    owned = lax.all_to_all(
        packed.reshape(n_slot, CAP, -1), "dp", 0, 0, tiled=True
    ).reshape(n_slot * CAP, -1)

    down_partial = jnp.dot(
        hidden_columns, adapter_down_factors, preferred_element_type=jnp.float32
    ).reshape(tokens, n_slot, PADDED_RANK)
    down_own = jnp.einsum("tsk,ts->tk", down_partial, slot_hit)
    down_weight = (sum_over_tensor(down_own, n_tensor) * factor).astype(jnp.bfloat16)
    weights = jnp.concatenate([down_weight, up_weight], axis=1)
    packed_weights = jnp.dot(pack, weights, preferred_element_type=jnp.float32).astype(
        jnp.bfloat16
    )
    owned_weights = lax.all_to_all(
        packed_weights.reshape(n_slot, CAP, -1), "dp", 0, 0, tiled=True
    ).reshape(n_slot * CAP, -1)

    grad_down = contract_helper(owned[:, :columns], owned_weights[:, PADDED_RANK:], 0, 0) / tokens
    grad_up = contract_helper(owned_weights[:, :PADDED_RANK], owned[:, columns:], 0, 0) / tokens
    new_dm, new_dmo, new_ds = adamw(
        down_master_copy, down_first_moment, down_second_moment, grad_down
    )
    new_um, new_umo, new_us = adamw(up_master_copy, up_first_moment, up_second_moment, grad_up)
    return (hidden_gradient, new_dm, new_dmo, new_ds, new_um, new_umo, new_us)


def solution(mesh):
    return jax.shard_map(
        local,
        mesh=mesh,
        in_specs=(
            P(("dp", "tensor"), None),
            P("dp", "tensor"),
            P(None, "tensor"),
            P("tensor", None),
            P(None, "tensor"),
            P("tensor", "dp"),
            P("tensor", "dp"),
            P("tensor", "dp"),
            P("dp", "tensor"),
            P("dp", "tensor"),
            P("dp", "tensor"),
            P("dp", None),
            P(),
            P(),
            P(),
        ),
        out_specs=(
            P(("dp", "tensor"), None),
            P("tensor", "dp"),
            P("tensor", "dp"),
            P("tensor", "dp"),
            P("dp", "tensor"),
            P("dp", "tensor"),
            P("dp", "tensor"),
        ),
        check_vma=False,
    )
```

```python
import functools

import jax
import jax.numpy as jnp
from jax import lax
from jax.experimental import pallas as pl
from jax.experimental.pallas import tpu as pltpu
from jax.sharding import PartitionSpec as P

RMIN = 8
PADDED_RANK = 64
CAP = 16


adapter_alpha_scale = 16.0
beta_one = 0.9
beta_two = 0.999
adam_eps = 1e-08
learn_rate = 0.0002
weight_decay = 0.1
first_fix = 0.9999734386011124
second_fix = 0.09520785288629038


def adamw(master, moment, second, grad):
    new_moment = beta_one * moment + (1.0 - beta_one) * grad
    new_second = beta_two * second + (1.0 - beta_two) * grad * grad
    update = new_moment / first_fix / (jnp.sqrt(new_second / second_fix) + adam_eps)
    new_master = master - learn_rate * (update + weight_decay * master)
    return (new_master, new_moment, new_second)


def contract_helper(left, right, left_dim, right_dim):
    return lax.dot_general(
        left, right, (((left_dim,), (right_dim,)), ((), ())), preferred_element_type=jnp.float32
    )


def swap(value, mask, count):
    return lax.ppermute(value, "tensor", [(i, i ^ mask) for i in range(count)])


def sum_over_tensor(value, count):
    mask = 1
    while mask < count:
        value = value + swap(value, mask, count)
        mask *= 2
    return value


VMEM_LIMIT = 60 * 1024 * 1024
VMEM = pltpu.MemorySpace.VMEM
SMEM = pltpu.MemorySpace.SMEM
NT = (((1,), (1,)), ((), ()))
NN = (((1,), (0,)), ((), ()))


def call(kernel, out_shape, flops, moved, **options):
    return pl.pallas_call(
        kernel,
        out_shape=out_shape,
        compiler_params=pltpu.CompilerParams(vmem_limit_bytes=VMEM_LIMIT),
        cost_estimate=pl.CostEstimate(flops=flops, bytes_accessed=moved, transcendentals=0),
        **options,
    )


def whole(shape, memory_space=None):
    zeros = (0,) * len(shape)
    return pl.BlockSpec(shape, lambda *_: zeros, memory_space=memory_space)


def dot(left, right, dims):
    return lax.dot_general(left, right, dims, preferred_element_type=jnp.float32)


def lane_slot(shape, first):
    return (lax.broadcasted_iota(jnp.int32, shape, 1) // PADDED_RANK + first).astype(jnp.float32)


def prep_kernel(rows_own, live_ref, bucket_ref, owner_ref, adapter_ref, cot_ref, up_ref,
                masked_ref, turned_ref, slot_ref, factor_ref, place_ref, up_own_ref):
    tokens = cot_ref.shape[0]
    n_chip = tokens // rows_own // 2
    position = lax.axis_index("tensor")
    chip, core = position // 2, position % 2
    live = live_ref[lax.axis_index("dp")]
    token = lax.broadcasted_iota(jnp.int32, (tokens, 1), 0)
    masked = jnp.where(token < live, cot_ref[...].astype(jnp.float32), 0.0).astype(jnp.bfloat16)
    masked_ref[...] = masked
    for step in range(n_chip):
        block = (chip + step) % n_chip * 2
        for out, k in ((0, core), (tokens // 2, 1 - core)):
            start = pl.multiple_of((block + k) * rows_own, rows_own)
            ids = start + lax.broadcasted_iota(jnp.int32, (rows_own, 1), 0)
            rows = cot_ref[pl.ds(start, rows_own), :].astype(jnp.float32)
            turned_ref[pl.ds(out + step * rows_own, rows_own), :] = jnp.where(
                ids < live, rows, 0.0
            ).astype(jnp.bfloat16)
    adapter = adapter_ref[...]
    slot = jnp.zeros_like(adapter)
    rank = jnp.zeros_like(adapter)
    for a in range(owner_ref.shape[0]):
        hit = adapter == a
        slot = jnp.where(hit, owner_ref[a], slot)
        rank = jnp.where(hit, lax.shift_left(RMIN, bucket_ref[a]), rank)
    slot_row = slot.astype(jnp.float32)
    rank_row = rank.astype(jnp.float32)
    down = lax.broadcasted_iota(jnp.int32, (tokens, tokens), 0)
    across = lax.broadcasted_iota(jnp.int32, (tokens, tokens), 1)
    diagonal = down == across
    slot_col = jnp.sum(jnp.where(diagonal, slot_row, 0.0), axis=1, keepdims=True)
    rank_col = jnp.sum(jnp.where(diagonal, rank_row, 0.0), axis=1, keepdims=True)
    earlier = jnp.where((slot_col == slot_row) & (down < across), 1.0, 0.0)
    place = slot_row * CAP + jnp.sum(earlier, axis=0, keepdims=True)
    place_ref[...] = place.astype(jnp.int32)
    lanes = factor_ref.shape[1]
    slot_wide = jnp.broadcast_to(slot_col, (tokens, lanes))
    slot_ref[...] = slot_wide
    kept = lax.broadcasted_iota(jnp.int32, (tokens, lanes), 1) % PADDED_RANK
    factor_ref[...] = jnp.where(
        kept.astype(jnp.float32) < rank_col, adapter_alpha_scale / rank_col, 0.0
    )
    chunk = 256
    acc = jnp.zeros((tokens, chunk), jnp.float32)
    for c in range(up_ref.shape[0] // chunk):
        part = dot(masked, up_ref[pl.ds(c * chunk, chunk), :], NT)
        hit = slot_col == lane_slot((1, chunk), c * chunk // PADDED_RANK)
        acc = acc + jnp.where(hit, part, 0.0)
    acc = acc[:, :128] + acc[:, 128:]
    up_own_ref[...] = acc[:, :PADDED_RANK] + acc[:, PADDED_RANK:]


def prep(rows_own, live, bucket, owner, adapter_row, cotangent, up_factors):
    tokens, kv = cotangent.shape
    shapes = (
        jax.ShapeDtypeStruct((tokens, kv), jnp.bfloat16),
        jax.ShapeDtypeStruct((tokens, kv), jnp.bfloat16),
        jax.ShapeDtypeStruct((tokens, 128), jnp.float32),
        jax.ShapeDtypeStruct((tokens, 128), jnp.float32),
        jax.ShapeDtypeStruct((1, tokens), jnp.int32),
        jax.ShapeDtypeStruct((tokens, PADDED_RANK), jnp.float32),
    )
    return call(
        functools.partial(prep_kernel, rows_own),
        shapes,
        2 * tokens * kv * up_factors.shape[0],
        up_factors.size * 2,
        grid=(1,),
        in_specs=[whole(v.shape, SMEM) for v in (live, bucket, owner)]
        + [whole(v.shape) for v in (adapter_row, cotangent, up_factors)],
        out_specs=tuple(whole(v.shape) for v in shapes),
        name="prep",
    )(live, bucket, owner, adapter_row, cotangent, up_factors)


def frozen_kernel(turned_ref, frozen_ref, ours_ref, theirs_ref):
    half = ours_ref.shape[0]
    both = dot(turned_ref[...], frozen_ref[...], NT)
    ours_ref[...] = both[:half, :]
    theirs_ref[...] = both[half:, :]


def frozen_term(turned, frozen, part, width):
    tokens, kv = turned.shape
    chunk = width // 2
    half = jax.ShapeDtypeStruct((tokens // 2, width), jnp.float32)
    block = pl.BlockSpec((tokens // 2, chunk), lambda i: (0, i))
    return call(
        frozen_kernel,
        (half, half),
        2 * tokens * kv * width,
        2 * kv * width + 4 * tokens * width,
        grid=(2,),
        in_specs=[whole(turned.shape), pl.BlockSpec((chunk, kv), lambda i: (2 * part + i, 0))],
        out_specs=(block, block),
        name="frozen_term",
    )(turned, frozen)


def pack_kernel(place_ref, hidden_ref, masked_ref, out_ref):
    rows, tokens = out_ref.shape[0], place_ref.shape[1]
    down = lax.broadcasted_iota(jnp.int32, (rows, tokens), 0)
    pick = jnp.where(down == place_ref[...], 1.0, 0.0).astype(jnp.bfloat16)
    width = hidden_ref.shape[1]
    out_ref[:, :width] = dot(pick, hidden_ref[...], NN).astype(jnp.bfloat16)
    out_ref[:, width:] = dot(pick, masked_ref[...], NN).astype(jnp.bfloat16)


def pack_rows(place, hidden_columns, masked, rows):
    columns = hidden_columns.shape[1] + masked.shape[1]
    return call(
        pack_kernel,
        jax.ShapeDtypeStruct((rows, columns), jnp.bfloat16),
        2 * rows * columns * hidden_columns.shape[0],
        4 * rows * columns,
        grid=(1,),
        in_specs=[whole(v.shape) for v in (place, hidden_columns, masked)],
        out_specs=whole((rows, columns)),
        name="pack",
    )(place, hidden_columns, masked)


def down_kernel(hidden_ref, factors_ref, slot_ref, out_ref, acc_ref):
    step = pl.program_id(0)
    chunk = factors_ref.shape[1]
    slots = chunk // PADDED_RANK

    @pl.when(step == 0)
    def _():
        acc_ref[...] = jnp.zeros_like(acc_ref)

    part = dot(hidden_ref[...], factors_ref[...], NN)
    first = (step * slots).astype(jnp.float32)
    acc = acc_ref[...]
    for c in range(chunk // 128):
        hit = slot_ref[...] == lane_slot((1, 128), 2 * c) + first
        acc = acc + jnp.where(hit, part[:, c * 128 : (c + 1) * 128], 0.0)
    acc_ref[...] = acc

    @pl.when(step == pl.num_programs(0) - 1)
    def _():
        out_ref[...] = acc[:, :PADDED_RANK] + acc[:, PADDED_RANK:]


def down_low_rank(hidden_columns, factors, slot_wide):
    tokens, columns = hidden_columns.shape
    chunk = 512
    return call(
        down_kernel,
        jax.ShapeDtypeStruct((tokens, PADDED_RANK), jnp.float32),
        2 * tokens * factors.size,
        2 * factors.size,
        grid=(factors.shape[1] // chunk,),
        in_specs=[
            pl.BlockSpec((tokens, columns), lambda i: (0, 0)),
            pl.BlockSpec((columns, chunk), lambda i: (0, i)),
            pl.BlockSpec((tokens, 128), lambda i: (0, 0)),
        ],
        out_specs=pl.BlockSpec((tokens, PADDED_RANK), lambda i: (0, 0)),
        scratch_shapes=[pltpu.VMEM((tokens, 128), jnp.float32)],
        name="down_low_rank",
    )(hidden_columns, factors, slot_wide)


def extra_kernel(rows_own, weight_ref, slot_ref, factors_ref, ours_ref, theirs_ref, acc_ref):
    step = pl.program_id(0)
    chunk = factors_ref.shape[1]
    tokens = weight_ref.shape[0]
    n_chip = tokens // rows_own // 2

    @pl.when(step == 0)
    def _():
        acc_ref[...] = jnp.zeros_like(acc_ref)

    weight = weight_ref[...].astype(jnp.float32)
    double = jnp.concatenate([weight, weight], axis=1)
    first = (step * (chunk // PADDED_RANK)).astype(jnp.float32)
    pieces = []
    for c in range(chunk // 128):
        hit = slot_ref[...] == lane_slot((1, 128), 2 * c) + first
        pieces.append(jnp.where(hit, double, 0.0).astype(jnp.bfloat16))
    placed = jnp.concatenate(pieces, axis=1)
    acc_ref[...] += dot(placed, factors_ref[...], NT)

    @pl.when(step == pl.num_programs(0) - 1)
    def _():
        position = lax.axis_index("tensor")
        chip, core = position // 2, position % 2
        for turn in range(n_chip):
            block = (chip + turn) % n_chip * 2
            for out, k in ((ours_ref, core), (theirs_ref, 1 - core)):
                start = pl.multiple_of((block + k) * rows_own, rows_own)
                out[pl.ds(turn * rows_own, rows_own), :] = acc_ref[pl.ds(start, rows_own), :]


def extra_term(rows_own, up_weight, slot_wide, factors):
    tokens = up_weight.shape[0]
    columns = factors.shape[0]
    chunk = 512
    half = jax.ShapeDtypeStruct((tokens // 2, columns), jnp.float32)
    half_spec = pl.BlockSpec((tokens // 2, columns), lambda i: (0, 0))
    return call(
        functools.partial(extra_kernel, rows_own),
        (half, half),
        2 * tokens * factors.size,
        2 * factors.size,
        grid=(factors.shape[1] // chunk,),
        in_specs=[
            pl.BlockSpec((tokens, PADDED_RANK), lambda i: (0, 0)),
            pl.BlockSpec((tokens, 128), lambda i: (0, 0)),
            pl.BlockSpec((columns, chunk), lambda i: (0, i)),
        ],
        out_specs=(half_spec, half_spec),
        scratch_shapes=[pltpu.VMEM((tokens, columns), jnp.float32)],
        name="extra_term",
    )(up_weight, slot_wide, factors)


def pair_kernel(rows_own, parts, extra_ours_ref, extra_pair_ref, *refs):
    ours_refs, pair_refs, own_ref, out_refs = (
        refs[:parts],
        refs[parts : 2 * parts],
        refs[2 * parts],
        refs[2 * parts + 1 :],
    )
    step = pl.program_id(0)
    position = lax.axis_index("tensor")
    chip, core = position // 2, position % 2

    def write(value):
        own_ref[...] = value[:rows_own, :]
        for i, out in enumerate(out_refs):
            out[...] = value[(i + 1) * rows_own : (i + 2) * rows_own, :].astype(jnp.bfloat16)

    for part in range(parts):
        here = step // 2 == part

        @pl.when(here & (chip != part))
        def _():
            write(ours_refs[part][...] + pair_refs[part][...])

        @pl.when(here & (chip == part) & (step % 2 == core))
        def _():
            write(ours_refs[part][...] + pair_refs[part][...] + extra_ours_ref[...])

        @pl.when(here & (chip == part) & (step % 2 != core))
        def _():
            write(ours_refs[part][...] + pair_refs[part][...] + extra_pair_ref[...])


def pair_sum(rows_own, ours, from_pair, extra_ours, extra_pair):
    parts = len(ours)
    half, width = ours[0].shape
    columns = extra_ours.shape[1]
    sent = jax.ShapeDtypeStruct((rows_own, parts * width), jnp.bfloat16)
    out_block = pl.BlockSpec((rows_own, columns), lambda i: (0, i))
    in_blocks = [
        pl.BlockSpec((half, columns), lambda i, q=q: (0, jnp.clip(i - 2 * q, 0, 1)))
        for q in range(parts)
    ]
    n_out = half // rows_own - 1
    return call(
        functools.partial(pair_kernel, rows_own, parts),
        (jax.ShapeDtypeStruct((rows_own, parts * width), jnp.float32),) + (sent,) * n_out,
        2 * half * width * parts,
        12 * half * width * parts,
        grid=(2 * parts,),
        in_specs=[whole(extra_ours.shape), whole(extra_pair.shape)] + in_blocks + in_blocks,
        out_specs=(out_block,) * (n_out + 1),
        name="pair_sum",
    )(extra_ours, extra_pair, *ours, *from_pair)


def local(
    hidden,
    cotangent,
    frozen_key_value,
    adapter_down_factors,
    adapter_up_factors,
    down_master_copy,
    down_first_moment,
    down_second_moment,
    up_master_copy,
    up_first_moment,
    up_second_moment,
    adapter_of_token,
    adapter_rank_bucket,
    adapter_owner_slot,
    live_token_counts,
):
    n_tensor = lax.axis_size("tensor")
    n_chip = n_tensor // 2
    tokens = cotangent.shape[0]
    rows_own, width = hidden.shape
    columns = width // n_tensor
    n_slot = adapter_owner_slot.shape[0]

    blocks = hidden.reshape(rows_own, n_tensor, columns).transpose(1, 0, 2)
    hidden_columns = lax.all_to_all(blocks, "tensor", 0, 0, tiled=True).reshape(tokens, columns)

    masked, turned, slot_wide, factor_wide, place, up_own = prep(
        rows_own,
        live_token_counts,
        adapter_rank_bucket,
        adapter_owner_slot,
        adapter_of_token.reshape(1, tokens),
        cotangent,
        adapter_up_factors,
    )
    factor = factor_wide[:, :PADDED_RANK]

    frozen_ours, from_pair = [], []
    for part in range(n_chip):
        mine, theirs = frozen_term(turned, frozen_key_value, part, 2 * columns)
        frozen_ours.append(mine)
        from_pair.append(swap(theirs, 1, n_tensor))

    packed = pack_rows(place, hidden_columns, masked, n_slot * CAP)
    owned = lax.all_to_all(
        packed.reshape(n_slot, CAP, -1), "dp", 0, 0, tiled=True
    ).reshape(n_slot * CAP, -1)

    up_weight = (sum_over_tensor(up_own, n_tensor) * factor).astype(jnp.bfloat16)
    extra_ours, extra_theirs = extra_term(rows_own, up_weight, slot_wide, adapter_down_factors)
    extra_pair = swap(extra_theirs, 1, n_tensor)
    total, *sent = pair_sum(
        rows_own, frozen_ours, from_pair, extra_ours, extra_pair
    )
    for step in range(1, n_chip):
        arrived = lax.ppermute(
            sent[step - 1], "tensor", [(i, (i + 2 * step) % n_tensor) for i in range(n_tensor)]
        )
        total = total + arrived.astype(jnp.float32)
    hidden_gradient = total.astype(jnp.bfloat16)

    down_own = down_low_rank(hidden_columns, adapter_down_factors, slot_wide)
    down_weight = (sum_over_tensor(down_own, n_tensor) * factor).astype(jnp.bfloat16)
    weights = jnp.concatenate([down_weight, up_weight], axis=1)
    pick = (
        jnp.arange(n_slot * CAP, dtype=jnp.int32)[:, None] == place
    ).astype(jnp.bfloat16)
    packed_weights = jnp.dot(pick, weights, preferred_element_type=jnp.float32).astype(
        jnp.bfloat16
    )
    owned, packed_weights = lax.optimization_barrier((owned, packed_weights))
    owned_weights = lax.all_to_all(
        packed_weights.reshape(n_slot, CAP, -1), "dp", 0, 0, tiled=True
    ).reshape(n_slot * CAP, -1)

    grad_down = contract_helper(owned[:, :columns], owned_weights[:, PADDED_RANK:], 0, 0) / tokens
    grad_up = contract_helper(owned_weights[:, :PADDED_RANK], owned[:, columns:], 0, 0) / tokens
    new_dm, new_dmo, new_ds = adamw(
        down_master_copy, down_first_moment, down_second_moment, grad_down
    )
    new_um, new_umo, new_us = adamw(up_master_copy, up_first_moment, up_second_moment, grad_up)
    return (hidden_gradient, new_dm, new_dmo, new_ds, new_um, new_umo, new_us)


def solution(mesh):
    return jax.shard_map(
        local,
        mesh=mesh,
        in_specs=(
            P(("dp", "tensor"), None),
            P("dp", "tensor"),
            P(None, "tensor"),
            P("tensor", None),
            P(None, "tensor"),
            P("tensor", "dp"),
            P("tensor", "dp"),
            P("tensor", "dp"),
            P("dp", "tensor"),
            P("dp", "tensor"),
            P("dp", "tensor"),
            P("dp", None),
            P(),
            P(),
            P(),
        ),
        out_specs=(
            P(("dp", "tensor"), None),
            P("tensor", "dp"),
            P("tensor", "dp"),
            P("tensor", "dp"),
            P("dp", "tensor"),
            P("dp", "tensor"),
            P("dp", "tensor"),
        ),
        check_vma=False,
    )
```

```python
import functools

import jax
import jax.numpy as jnp
from jax import lax
from jax.experimental import pallas as pl
from jax.experimental.pallas import tpu as pltpu
from jax.sharding import PartitionSpec as P

RMIN = 8
PADDED_RANK = 64
CAP = 16


adapter_alpha_scale = 16.0
beta_one = 0.9
beta_two = 0.999
adam_eps = 1e-08
learn_rate = 0.0002
weight_decay = 0.1
first_fix = 0.9999734386011124
second_fix = 0.09520785288629038


def adamw(master, moment, second, grad):
    new_moment = beta_one * moment + (1.0 - beta_one) * grad
    new_second = beta_two * second + (1.0 - beta_two) * grad * grad
    update = new_moment / first_fix / (jnp.sqrt(new_second / second_fix) + adam_eps)
    new_master = master - learn_rate * (update + weight_decay * master)
    return (new_master, new_moment, new_second)


def contract_helper(left, right, left_dim, right_dim):
    return lax.dot_general(
        left, right, (((left_dim,), (right_dim,)), ((), ())), preferred_element_type=jnp.float32
    )


def swap(value, mask, count):
    return lax.ppermute(value, "tensor", [(i, i ^ mask) for i in range(count)])


def sum_over_tensor(value, count, mask=1):
    while mask < count:
        value = value + swap(value, mask, lax.axis_size("tensor"))
        mask *= 2
    return value


VMEM_LIMIT = 60 * 1024 * 1024
HBM = pltpu.MemorySpace.HBM
SMEM = pltpu.MemorySpace.SMEM
NT = (((1,), (1,)), ((), ()))
NN = (((1,), (0,)), ((), ()))


def call(kernel, out_shape, flops, moved, **options):
    return pl.pallas_call(
        kernel,
        out_shape=out_shape,
        compiler_params=pltpu.CompilerParams(vmem_limit_bytes=VMEM_LIMIT),
        cost_estimate=pl.CostEstimate(flops=flops, bytes_accessed=moved, transcendentals=0),
        **options,
    )


def whole(shape, memory_space=None):
    zeros = (0,) * len(shape)
    return pl.BlockSpec(shape, lambda *_: zeros, memory_space=memory_space)


def dot(left, right, dims):
    return lax.dot_general(left, right, dims, preferred_element_type=jnp.float32)


def lane_slot(shape, first):
    return (lax.broadcasted_iota(jnp.int32, shape, 1) // PADDED_RANK + first).astype(jnp.float32)


def prep_kernel(rows_own, live_ref, bucket_ref, owner_ref, adapter_ref, cot_ref, up_ref,
                masked_ref, turned_ref, slot_ref, factor_ref, place_ref, up_own_ref):
    tokens = cot_ref.shape[0]
    n_chip = tokens // rows_own // 2
    position = lax.axis_index("tensor")
    chip, core = position // 2, position % 2
    live = live_ref[lax.axis_index("dp")]
    token = lax.broadcasted_iota(jnp.int32, (tokens, 1), 0)
    masked = jnp.where(token < live, cot_ref[...].astype(jnp.float32), 0.0).astype(jnp.bfloat16)
    masked_ref[...] = masked
    for step in range(n_chip):
        block = (chip + step) % n_chip * 2
        for out, k in ((0, core), (tokens // 2, 1 - core)):
            start = pl.multiple_of((block + k) * rows_own, rows_own)
            ids = start + lax.broadcasted_iota(jnp.int32, (rows_own, 1), 0)
            rows = cot_ref[pl.ds(start, rows_own), :].astype(jnp.float32)
            turned_ref[pl.ds(out + step * rows_own, rows_own), :] = jnp.where(
                ids < live, rows, 0.0
            ).astype(jnp.bfloat16)
    adapter = adapter_ref[...]
    slot = jnp.zeros_like(adapter)
    rank = jnp.zeros_like(adapter)
    for a in range(owner_ref.shape[0]):
        hit = adapter == a
        slot = jnp.where(hit, owner_ref[a], slot)
        rank = jnp.where(hit, lax.shift_left(RMIN, bucket_ref[a]), rank)
    slot_row = slot.astype(jnp.float32)
    rank_row = rank.astype(jnp.float32)
    down = lax.broadcasted_iota(jnp.int32, (tokens, tokens), 0)
    across = lax.broadcasted_iota(jnp.int32, (tokens, tokens), 1)
    diagonal = down == across
    slot_col = jnp.sum(jnp.where(diagonal, slot_row, 0.0), axis=1, keepdims=True)
    rank_col = jnp.sum(jnp.where(diagonal, rank_row, 0.0), axis=1, keepdims=True)
    earlier = jnp.where((slot_col == slot_row) & (down < across), 1.0, 0.0)
    place = slot_row * CAP + jnp.sum(earlier, axis=0, keepdims=True)
    place_ref[...] = place.astype(jnp.int32)
    lanes = factor_ref.shape[1]
    slot_wide = jnp.broadcast_to(slot_col, (tokens, lanes))
    slot_ref[...] = slot_wide
    kept = lax.broadcasted_iota(jnp.int32, (tokens, lanes), 1) % PADDED_RANK
    factor_ref[...] = jnp.where(
        kept.astype(jnp.float32) < rank_col, adapter_alpha_scale / rank_col, 0.0
    )
    chunk = 256
    acc = jnp.zeros((tokens, chunk), jnp.float32)
    for c in range(up_ref.shape[0] // chunk):
        part = dot(masked, up_ref[pl.ds(c * chunk, chunk), :], NT)
        hit = slot_col == lane_slot((1, chunk), c * chunk // PADDED_RANK)
        acc = acc + jnp.where(hit, part, 0.0)
    acc = acc[:, :128] + acc[:, 128:]
    up_own_ref[...] = acc[:, :PADDED_RANK] + acc[:, PADDED_RANK:]


def prep(rows_own, live, bucket, owner, adapter_row, cotangent, up_factors):
    tokens, kv = cotangent.shape
    shapes = (
        jax.ShapeDtypeStruct((tokens, kv), jnp.bfloat16),
        jax.ShapeDtypeStruct((tokens, kv), jnp.bfloat16),
        jax.ShapeDtypeStruct((tokens, 128), jnp.float32),
        jax.ShapeDtypeStruct((tokens, 128), jnp.float32),
        jax.ShapeDtypeStruct((1, tokens), jnp.int32),
        jax.ShapeDtypeStruct((tokens, PADDED_RANK), jnp.float32),
    )
    return call(
        functools.partial(prep_kernel, rows_own),
        shapes,
        2 * tokens * kv * up_factors.shape[0],
        up_factors.size * 2,
        grid=(1,),
        in_specs=[whole(v.shape, SMEM) for v in (live, bucket, owner)]
        + [whole(v.shape) for v in (adapter_row, cotangent, up_factors)],
        out_specs=tuple(whole(v.shape) for v in shapes),
        name="prep",
    )(live, bucket, owner, adapter_row, cotangent, up_factors)


def frozen_kernel(turned_ref, frozen_ref, ours_ref, *theirs_refs):
    step = pl.program_id(0)
    half = ours_ref.shape[0]
    per_part = pl.num_programs(0) // len(theirs_refs)
    both = dot(turned_ref[...], frozen_ref[...], NT)
    ours_ref[...] = both[:half, :]
    for part, out in enumerate(theirs_refs):

        @pl.when(step // per_part == part)
        def _():
            out[...] = both[half:, :]


def part_blocks(rows, chunk, parts, per_part):
    return [
        pl.BlockSpec((rows, chunk), lambda i, q=q: (0, jnp.clip(i - q * per_part, 0, per_part - 1)))
        for q in range(parts)
    ]


def frozen_term(turned, frozen, parts):
    tokens, kv = turned.shape
    width = frozen.shape[0]
    chunk = 1024
    steps = width // chunk
    theirs = jax.ShapeDtypeStruct((tokens // 2, width // parts), jnp.float32)
    return call(
        frozen_kernel,
        (jax.ShapeDtypeStruct((tokens // 2, width), jnp.float32),) + (theirs,) * parts,
        2 * tokens * kv * width,
        2 * kv * width + 4 * tokens * width,
        grid=(steps,),
        in_specs=[whole(turned.shape), pl.BlockSpec((chunk, kv), lambda i: (i, 0))],
        out_specs=(
            pl.BlockSpec((tokens // 2, chunk), lambda i: (0, i)),
            *part_blocks(tokens // 2, chunk, parts, steps // parts),
        ),
        name="frozen_term",
    )(turned, frozen)


def pack_kernel(place_ref, hidden_ref, masked_ref, out_ref, pick_ref):
    step = pl.program_id(0)
    last = pl.num_programs(0) - 1

    @pl.when(step == 0)
    def _():
        down = lax.broadcasted_iota(jnp.int32, pick_ref.shape, 0)
        pick_ref[...] = jnp.where(down == place_ref[...], 1.0, 0.0).astype(jnp.bfloat16)

    @pl.when(step < last)
    def _():
        out_ref[...] = dot(pick_ref[...], hidden_ref[...], NN).astype(jnp.bfloat16)

    @pl.when(step == last)
    def _():
        out_ref[...] = dot(pick_ref[...], masked_ref[...], NN).astype(jnp.bfloat16)


def pack_rows(place, hidden_columns, masked, rows):
    tokens, chunk = masked.shape
    columns = hidden_columns.shape[1] + chunk
    steps = columns // chunk
    return call(
        pack_kernel,
        jax.ShapeDtypeStruct((rows, columns), jnp.bfloat16),
        2 * rows * columns * tokens,
        2 * (rows + tokens) * columns,
        grid=(steps,),
        in_specs=[
            whole(place.shape),
            pl.BlockSpec((tokens, chunk), lambda i: (0, jnp.minimum(i, steps - 2))),
            whole(masked.shape),
        ],
        out_specs=pl.BlockSpec((rows, chunk), lambda i: (0, i)),
        scratch_shapes=[pltpu.VMEM((rows, tokens), jnp.bfloat16)],
        name="pack",
    )(place, hidden_columns, masked)


def factors_kernel(rows_own, hidden_ref, weight_ref, slot_ref, factors_ref, down_ref, ours_ref,
                   theirs_ref, held_ref, extra_ref, sems):
    parts, columns, chunk = held_ref.shape
    tokens = hidden_ref.shape[0]
    n_chip = tokens // rows_own // 2
    copies = [
        pltpu.make_async_copy(
            factors_ref.at[:, pl.ds(c * chunk, chunk)], held_ref.at[c], sems.at[c]
        )
        for c in range(parts)
    ]
    for copy in copies:
        copy.start()
    slot = slot_ref[...]
    weight = weight_ref[...].astype(jnp.float32)
    double = jnp.concatenate([weight, weight], axis=1)
    acc = jnp.zeros((tokens, 128), jnp.float32)
    for c in range(parts):
        copies[c].wait()
        factors = held_ref[c]
        product = dot(hidden_ref[...], factors, NN)
        pieces = []
        for d in range(chunk // 128):
            hit = slot == lane_slot((1, 128), (c * chunk + d * 128) // PADDED_RANK)
            acc = acc + jnp.where(hit, product[:, d * 128 : (d + 1) * 128], 0.0)
            pieces.append(jnp.where(hit, double, 0.0).astype(jnp.bfloat16))
        term = dot(jnp.concatenate(pieces, axis=1), factors, NT)
        if c == 0:
            extra_ref[...] = term
        else:
            extra_ref[...] += term
    down_ref[...] = acc[:, :PADDED_RANK] + acc[:, PADDED_RANK:]
    position = lax.axis_index("tensor")
    chip, core = position // 2, position % 2
    for turn in range(n_chip):
        block = (chip + turn) % n_chip * 2
        for out, k in ((ours_ref, core), (theirs_ref, 1 - core)):
            start = pl.multiple_of((block + k) * rows_own, rows_own)
            out[pl.ds(turn * rows_own, rows_own), :] = extra_ref[pl.ds(start, rows_own), :]


def factor_products(rows_own, hidden_columns, up_weight, slot_wide, factors):
    tokens, columns = hidden_columns.shape
    chunk = 256
    parts = factors.shape[1] // chunk
    half = jax.ShapeDtypeStruct((tokens // 2, columns), jnp.float32)
    shapes = (jax.ShapeDtypeStruct((tokens, PADDED_RANK), jnp.float32), half, half)
    return call(
        functools.partial(factors_kernel, rows_own),
        shapes,
        4 * tokens * factors.size,
        2 * factors.size,
        grid=(1,),
        in_specs=[whole(v.shape) for v in (hidden_columns, up_weight, slot_wide)]
        + [pl.BlockSpec(memory_space=HBM)],
        out_specs=tuple(whole(v.shape) for v in shapes),
        scratch_shapes=[
            pltpu.VMEM((parts, columns, chunk), jnp.bfloat16),
            pltpu.VMEM((tokens, columns), jnp.float32),
            pltpu.SemaphoreType.DMA((parts,)),
        ],
        name="factor_products",
    )(hidden_columns, up_weight, slot_wide, factors)


def pair_kernel(rows_own, parts, extra_ours_ref, extra_pair_ref, ours_ref, *refs):
    pair_refs, own_ref, out_refs = refs[:parts], refs[parts], refs[parts + 1 :]
    step = pl.program_id(0)
    per_part = pl.num_programs(0) // parts
    position = lax.axis_index("tensor")
    chip, core = position // 2, position % 2
    total = ours_ref[...]
    for part in range(parts):
        total = jnp.where(step // per_part == part, total + pair_refs[part][...], total)

    def write(value):
        own_ref[...] = value[:rows_own, :]
        for i, out in enumerate(out_refs):
            out[...] = value[(i + 1) * rows_own : (i + 2) * rows_own, :].astype(jnp.bfloat16)

    @pl.when(step // 2 != chip)
    def _():
        write(total)

    @pl.when((step // 2 == chip) & (step % 2 == core))
    def _():
        write(total + extra_ours_ref[...])

    @pl.when((step // 2 == chip) & (step % 2 != core))
    def _():
        write(total + extra_pair_ref[...])


def pair_sum(rows_own, ours, from_pair, extra_ours, extra_pair):
    parts = len(from_pair)
    half, width = ours.shape
    columns = extra_ours.shape[1]
    steps = width // columns
    sent = jax.ShapeDtypeStruct((rows_own, width), jnp.bfloat16)
    out_block = pl.BlockSpec((rows_own, columns), lambda i: (0, i))
    n_out = half // rows_own - 1
    return call(
        functools.partial(pair_kernel, rows_own, parts),
        (jax.ShapeDtypeStruct((rows_own, width), jnp.float32),) + (sent,) * n_out,
        2 * half * width,
        10 * half * width,
        grid=(steps,),
        in_specs=[
            whole(extra_ours.shape),
            whole(extra_pair.shape),
            pl.BlockSpec((half, columns), lambda i: (0, i)),
            *part_blocks(half, columns, parts, steps // parts),
        ],
        out_specs=(out_block,) * (n_out + 1),
        name="pair_sum",
    )(extra_ours, extra_pair, ours, *from_pair)


def local(
    hidden,
    cotangent,
    frozen_key_value,
    adapter_down_factors,
    adapter_up_factors,
    down_master_copy,
    down_first_moment,
    down_second_moment,
    up_master_copy,
    up_first_moment,
    up_second_moment,
    adapter_of_token,
    adapter_rank_bucket,
    adapter_owner_slot,
    live_token_counts,
):
    n_tensor = lax.axis_size("tensor")
    n_chip = n_tensor // 2
    tokens = cotangent.shape[0]
    rows_own, width = hidden.shape
    columns = width // n_tensor
    n_slot = adapter_owner_slot.shape[0]

    blocks = hidden.reshape(rows_own, n_tensor, columns).transpose(1, 0, 2)
    hidden_columns = lax.all_to_all(blocks, "tensor", 0, 0, tiled=True).reshape(tokens, columns)

    masked, turned, slot_wide, factor_wide, place, up_own = prep(
        rows_own,
        live_token_counts,
        adapter_rank_bucket,
        adapter_owner_slot,
        adapter_of_token.reshape(1, tokens),
        cotangent,
        adapter_up_factors,
    )
    factor = factor_wide[:, :PADDED_RANK]

    frozen_ours, *frozen_theirs = frozen_term(turned, frozen_key_value, 2)
    up_own = sum_over_tensor(up_own, n_tensor // 2)
    place, up_own, frozen_ours, frozen_theirs = lax.optimization_barrier(
        (place, up_own, frozen_ours, frozen_theirs)
    )
    from_pair = [swap(theirs, 1, n_tensor) for theirs in frozen_theirs]

    packed = pack_rows(place, hidden_columns, masked, n_slot * CAP)
    owned = lax.all_to_all(
        packed.reshape(n_slot, CAP, -1), "dp", 0, 0, tiled=True
    ).reshape(n_slot * CAP, -1)

    up_weight = (sum_over_tensor(up_own, n_tensor, n_tensor // 2) * factor).astype(jnp.bfloat16)
    down_own, extra_ours, extra_theirs = factor_products(
        rows_own, hidden_columns, up_weight, slot_wide, adapter_down_factors
    )
    extra_pair = swap(extra_theirs, 1, n_tensor)
    total, *sent = pair_sum(
        rows_own, frozen_ours, from_pair, extra_ours, extra_pair
    )
    for step in range(1, n_chip):
        arrived = lax.ppermute(
            sent[step - 1], "tensor", [(i, (i + 2 * step) % n_tensor) for i in range(n_tensor)]
        )
        total = total + arrived.astype(jnp.float32)
    hidden_gradient = total.astype(jnp.bfloat16)

    down_weight = (sum_over_tensor(down_own, n_tensor) * factor).astype(jnp.bfloat16)
    weights = jnp.concatenate([down_weight, up_weight], axis=1)
    pick = (
        jnp.arange(n_slot * CAP, dtype=jnp.int32)[:, None] == place
    ).astype(jnp.bfloat16)
    packed_weights = jnp.dot(pick, weights, preferred_element_type=jnp.float32).astype(
        jnp.bfloat16
    )
    owned, packed_weights = lax.optimization_barrier((owned, packed_weights))
    owned_weights = lax.all_to_all(
        packed_weights.reshape(n_slot, CAP, -1), "dp", 0, 0, tiled=True
    ).reshape(n_slot * CAP, -1)

    grad_down = contract_helper(owned[:, :columns], owned_weights[:, PADDED_RANK:], 0, 0) / tokens
    grad_up = contract_helper(owned_weights[:, :PADDED_RANK], owned[:, columns:], 0, 0) / tokens
    new_dm, new_dmo, new_ds = adamw(
        down_master_copy, down_first_moment, down_second_moment, grad_down
    )
    new_um, new_umo, new_us = adamw(up_master_copy, up_first_moment, up_second_moment, grad_up)
    return (hidden_gradient, new_dm, new_dmo, new_ds, new_um, new_umo, new_us)


def solution(mesh):
    return jax.shard_map(
        local,
        mesh=mesh,
        in_specs=(
            P(("dp", "tensor"), None),
            P("dp", "tensor"),
            P(None, "tensor"),
            P("tensor", None),
            P(None, "tensor"),
            P("tensor", "dp"),
            P("tensor", "dp"),
            P("tensor", "dp"),
            P("dp", "tensor"),
            P("dp", "tensor"),
            P("dp", "tensor"),
            P("dp", None),
            P(),
            P(),
            P(),
        ),
        out_specs=(
            P(("dp", "tensor"), None),
            P("tensor", "dp"),
            P("tensor", "dp"),
            P("tensor", "dp"),
            P("dp", "tensor"),
            P("dp", "tensor"),
            P("dp", "tensor"),
        ),
        check_vma=False,
    )
```

```python
import functools

import jax
import jax.numpy as jnp
from jax import lax
from jax.experimental import pallas as pl
from jax.experimental.pallas import tpu as pltpu
from jax.sharding import PartitionSpec as P

RMIN = 8
PADDED_RANK = 64
CAP = 16


adapter_alpha_scale = 16.0
beta_one = 0.9
beta_two = 0.999
adam_eps = 1e-08
learn_rate = 0.0002
weight_decay = 0.1
first_fix = 0.9999734386011124
second_fix = 0.09520785288629038


def adamw(master, moment, second, grad):
    new_moment = beta_one * moment + (1.0 - beta_one) * grad
    new_second = beta_two * second + (1.0 - beta_two) * grad * grad
    update = new_moment / first_fix / (jnp.sqrt(new_second / second_fix) + adam_eps)
    new_master = master - learn_rate * (update + weight_decay * master)
    return (new_master, new_moment, new_second)


def contract_helper(left, right, left_dim, right_dim):
    return lax.dot_general(
        left, right, (((left_dim,), (right_dim,)), ((), ())), preferred_element_type=jnp.float32
    )


def swap(value, mask, count):
    return lax.ppermute(value, "tensor", [(i, i ^ mask) for i in range(count)])


def sum_over_chips(value, count):
    near = value + swap(value, 2, count)
    far = swap(value, 4, count) + swap(value, 6, count)
    return near + far


VMEM_LIMIT = 16 * 1024 * 1024
VMEM_MOST = 57 * 1024 * 1024
SMEM_SPEC = pl.BlockSpec(memory_space=pltpu.MemorySpace.SMEM)
HBM = pltpu.MemorySpace.HBM
NT = (((1,), (1,)), ((), ()))
NN = (((1,), (0,)), ((), ()))


def call(kernel, out_shape, flops, moved, limit=VMEM_LIMIT, **options):
    return pl.pallas_call(
        kernel,
        out_shape=out_shape,
        compiler_params=pltpu.CompilerParams(vmem_limit_bytes=limit),
        cost_estimate=pl.CostEstimate(flops=flops, bytes_accessed=moved, transcendentals=0),
        **options,
    )


def dot(left, right, dims):
    return lax.dot_general(left, right, dims, preferred_element_type=jnp.float32)


def lane_slot(shape, first):
    return (lax.broadcasted_iota(jnp.int32, shape, 1) // PADDED_RANK + first).astype(jnp.float32)


def fetch(sources, targets, sems):
    copies = [
        pltpu.make_async_copy(source, target, sems.at[i])
        for i, (source, target) in enumerate(zip(sources, targets, strict=True))
    ]
    for copy in copies:
        copy.start()
    return copies


def row_parts(ref, parts):
    rows = ref.shape[0] // parts
    return [ref.at[pl.ds(i * rows, rows), :] for i in range(parts)]


def prep_kernel(rows_own, live_ref, bucket_ref, owner_ref, adapter_ref, cot_ref, up_ref,
                masked_ref, turned_ref, slot_ref, factor_ref, place_ref, up_own_ref):
    tokens = cot_ref.shape[0]
    n_chip = tokens // rows_own // 2
    position = lax.axis_index("tensor")
    chip, core = position // 2, position % 2
    live = live_ref[lax.axis_index("dp")]
    token = lax.broadcasted_iota(jnp.int32, (tokens, 1), 0)
    masked = jnp.where(token < live, cot_ref[...].astype(jnp.float32), 0.0).astype(jnp.bfloat16)
    masked_ref[...] = masked
    for step in range(n_chip):
        block = (chip + step) % n_chip * 2
        for out, k in ((0, core), (tokens // 2, 1 - core)):
            start = pl.multiple_of((block + k) * rows_own, rows_own)
            ids = start + lax.broadcasted_iota(jnp.int32, (rows_own, 1), 0)
            rows = cot_ref[pl.ds(start, rows_own), :].astype(jnp.float32)
            turned_ref[pl.ds(out + step * rows_own, rows_own), :] = jnp.where(
                ids < live, rows, 0.0
            ).astype(jnp.bfloat16)
    adapter = adapter_ref[...]
    slot = jnp.zeros_like(adapter)
    rank = jnp.zeros_like(adapter)
    for a in range(owner_ref.shape[0]):
        hit = adapter == a
        slot = jnp.where(hit, owner_ref[a], slot)
        rank = jnp.where(hit, lax.shift_left(RMIN, bucket_ref[a]), rank)
    slot_row = slot.astype(jnp.float32)
    rank_row = rank.astype(jnp.float32)
    down = lax.broadcasted_iota(jnp.int32, (tokens, tokens), 0)
    across = lax.broadcasted_iota(jnp.int32, (tokens, tokens), 1)
    diagonal = down == across
    slot_col = jnp.sum(jnp.where(diagonal, slot_row, 0.0), axis=1, keepdims=True)
    rank_col = jnp.sum(jnp.where(diagonal, rank_row, 0.0), axis=1, keepdims=True)
    earlier = jnp.where((slot_col == slot_row) & (down < across), 1.0, 0.0)
    place = slot_row * CAP + jnp.sum(earlier, axis=0, keepdims=True)
    place_ref[...] = place.astype(jnp.int32)
    lanes = factor_ref.shape[1]
    slot_wide = jnp.broadcast_to(slot_col, (tokens, lanes))
    slot_ref[...] = slot_wide
    kept = lax.broadcasted_iota(jnp.int32, (tokens, lanes), 1) % PADDED_RANK
    factor_ref[...] = jnp.where(
        kept.astype(jnp.float32) < rank_col, adapter_alpha_scale / rank_col, 0.0
    )
    chunk = 256
    acc = jnp.zeros((tokens, chunk), jnp.float32)
    for c in range(up_ref.shape[0] // chunk):
        part = dot(masked, up_ref[pl.ds(c * chunk, chunk), :], NT)
        hit = slot_col == lane_slot((1, chunk), c * chunk // PADDED_RANK)
        acc = acc + jnp.where(hit, part, 0.0)
    acc = acc[:, :128] + acc[:, 128:]
    up_own_ref[...] = acc[:, :PADDED_RANK] + acc[:, PADDED_RANK:]


def prep(rows_own, live, bucket, owner, adapter_row, cotangent, up_factors):
    tokens, kv = cotangent.shape
    shapes = (
        jax.ShapeDtypeStruct((tokens, kv), jnp.bfloat16),
        jax.ShapeDtypeStruct((tokens, kv), jnp.bfloat16),
        jax.ShapeDtypeStruct((tokens, 128), jnp.float32),
        jax.ShapeDtypeStruct((tokens, 128), jnp.float32),
        jax.ShapeDtypeStruct((1, tokens), jnp.int32),
        jax.ShapeDtypeStruct((tokens, PADDED_RANK), jnp.float32),
    )
    return call(
        functools.partial(prep_kernel, rows_own),
        shapes,
        2 * tokens * kv * up_factors.shape[0],
        up_factors.size * 2,
        in_specs=[SMEM_SPEC] * 3
        + [pl.BlockSpec(v.shape) for v in (adapter_row, cotangent, up_factors)],
        name="prep",
    )(live, bucket, owner, adapter_row, cotangent, up_factors)


def frozen_kernel(turned_ref, frozen_any, *refs):
    outs, (frozen_ref, sems) = refs[:-2], refs[-2:]
    steps = sems.shape[0]
    half = outs[0].shape[0]
    chunk = frozen_ref.shape[0] // steps
    per_part = steps // len(outs)
    copies = fetch(row_parts(frozen_any, steps), row_parts(frozen_ref, steps), sems)
    theirs = turned_ref[half:, :]
    for c in range(steps):
        copies[c].wait()
        first = c % per_part * chunk
        outs[c // per_part][:, first : first + chunk] = dot(
            theirs, frozen_ref[c * chunk : (c + 1) * chunk, :], NT
        )


def frozen_term(turned, frozen, parts):
    tokens, kv = turned.shape
    width = frozen.shape[0]
    return call(
        frozen_kernel,
        (jax.ShapeDtypeStruct((tokens // 2, width // parts), jnp.float32),) * parts,
        tokens * kv * width,
        2 * kv * width + 2 * tokens * width,
        VMEM_MOST,
        in_specs=[pl.BlockSpec(turned.shape), pl.BlockSpec(memory_space=HBM)],
        scratch_shapes=[
            pltpu.VMEM(frozen.shape, frozen.dtype),
            pltpu.SemaphoreType.DMA((8,)),
        ],
        name="frozen_term",
    )(turned, frozen)


def pack_kernel(place_ref, hidden_ref, masked_ref, out_ref):
    rows, tokens = out_ref.shape[0], place_ref.shape[1]
    down = lax.broadcasted_iota(jnp.int32, (rows, tokens), 0)
    pick = jnp.where(down == place_ref[...], 1.0, 0.0).astype(jnp.bfloat16)
    width = hidden_ref.shape[1]
    out_ref[:, :width] = dot(pick, hidden_ref[...], NN).astype(jnp.bfloat16)
    out_ref[:, width:] = dot(pick, masked_ref[...], NN).astype(jnp.bfloat16)


def pack_rows(place, hidden_columns, masked, rows):
    tokens, columns = masked.shape[0], hidden_columns.shape[1] + masked.shape[1]
    return call(
        pack_kernel,
        jax.ShapeDtypeStruct((rows, columns), jnp.bfloat16),
        2 * rows * columns * tokens,
        2 * (rows + tokens) * columns,
        name="pack",
    )(place, hidden_columns, masked)


def factors_kernel(rows_own, hidden_ref, weight_ref, slot_ref, factors_ref, down_ref, ours_ref,
                   theirs_ref, held_ref, extra_ref, sems):
    parts, columns, chunk = held_ref.shape
    tokens = hidden_ref.shape[0]
    n_chip = tokens // rows_own // 2
    copies = [
        pltpu.make_async_copy(
            factors_ref.at[:, pl.ds(c * chunk, chunk)], held_ref.at[c], sems.at[c]
        )
        for c in range(parts)
    ]
    for copy in copies:
        copy.start()
    slot = slot_ref[...]
    weight = weight_ref[...].astype(jnp.float32)
    double = jnp.concatenate([weight, weight], axis=1)
    acc = jnp.zeros((tokens, 128), jnp.float32)
    for c in range(parts):
        copies[c].wait()
        factors = held_ref[c]
        product = dot(hidden_ref[...], factors, NN)
        pieces = []
        for d in range(chunk // 128):
            hit = slot == lane_slot((1, 128), (c * chunk + d * 128) // PADDED_RANK)
            acc = acc + jnp.where(hit, product[:, d * 128 : (d + 1) * 128], 0.0)
            pieces.append(jnp.where(hit, double, 0.0).astype(jnp.bfloat16))
        term = dot(jnp.concatenate(pieces, axis=1), factors, NT)
        if c == 0:
            extra_ref[...] = term
        else:
            extra_ref[...] += term
    down_ref[...] = acc[:, :PADDED_RANK] + acc[:, PADDED_RANK:]
    position = lax.axis_index("tensor")
    chip, core = position // 2, position % 2
    for turn in range(n_chip):
        block = (chip + turn) % n_chip * 2
        for out, k in ((ours_ref, core), (theirs_ref, 1 - core)):
            start = pl.multiple_of((block + k) * rows_own, rows_own)
            out[pl.ds(turn * rows_own, rows_own), :] = extra_ref[pl.ds(start, rows_own), :]


def factor_products(rows_own, hidden_columns, up_weight, slot_wide, factors):
    tokens, columns = hidden_columns.shape
    chunk = 256
    parts = factors.shape[1] // chunk
    half = jax.ShapeDtypeStruct((tokens // 2, columns), jnp.float32)
    shapes = (jax.ShapeDtypeStruct((tokens, PADDED_RANK), jnp.float32), half, half)
    return call(
        functools.partial(factors_kernel, rows_own),
        shapes,
        4 * tokens * factors.size,
        2 * factors.size,
        VMEM_MOST,
        in_specs=[pl.BlockSpec(v.shape) for v in (hidden_columns, up_weight, slot_wide)]
        + [pl.BlockSpec(memory_space=HBM)],
        scratch_shapes=[
            pltpu.VMEM((parts, columns, chunk), jnp.bfloat16),
            pltpu.VMEM((tokens, columns), jnp.float32),
            pltpu.SemaphoreType.DMA((parts,)),
        ],
        name="factor_products",
    )(hidden_columns, up_weight, slot_wide, factors)


def pair_kernel(rows_own, parts, turned_ref, extra_ours_ref, extra_pair_ref, frozen_any, *refs):
    pair_refs, outs, (frozen_ref, sems) = refs[:parts], refs[parts:-2], refs[-2:]
    steps = sems.shape[0]
    half, columns = extra_ours_ref.shape
    per_part = steps // parts
    copies = fetch(row_parts(frozen_any, steps), row_parts(frozen_ref, steps), sems)
    position = lax.axis_index("tensor")
    chip, core = position // 2, position % 2
    ours = turned_ref[:half, :]
    low = jnp.where(core == 0, extra_ours_ref[...], extra_pair_ref[...])
    high = jnp.where(core == 0, extra_pair_ref[...], extra_ours_ref[...])
    for c in range(steps):
        copies[c].wait()
        at = slice(c * columns, (c + 1) * columns)
        first = c % per_part * columns
        total = dot(ours, frozen_ref[at, :], NT)
        total = total + pair_refs[c // per_part][:, first : first + columns]
        total = total + jnp.where(chip == c // 2, low if c % 2 == 0 else high, 0.0)
        outs[0][:, at] = total[:rows_own, :]
        for i, out in enumerate(outs[1:]):
            out[:, at] = total[(i + 1) * rows_own : (i + 2) * rows_own, :].astype(jnp.bfloat16)


def pair_sum(rows_own, turned, frozen, from_pair, extra_ours, extra_pair):
    parts = len(from_pair)
    half, columns = extra_ours.shape
    width, kv = frozen.shape
    sent = jax.ShapeDtypeStruct((rows_own, width), jnp.bfloat16)
    n_out = half // rows_own - 1
    return call(
        functools.partial(pair_kernel, rows_own, parts),
        (jax.ShapeDtypeStruct((rows_own, width), jnp.float32),) + (sent,) * n_out,
        2 * half * width * kv,
        2 * kv * width + 6 * half * width,
        VMEM_MOST,
        in_specs=[pl.BlockSpec(v.shape) for v in (turned, extra_ours, extra_pair)]
        + [pl.BlockSpec(memory_space=HBM)]
        + [pl.BlockSpec(v.shape) for v in from_pair],
        scratch_shapes=[
            pltpu.VMEM(frozen.shape, frozen.dtype),
            pltpu.SemaphoreType.DMA((width // columns,)),
        ],
        name="pair_sum",
    )(turned, extra_ours, extra_pair, frozen, *from_pair)


def local(
    hidden,
    cotangent,
    frozen_key_value,
    adapter_down_factors,
    adapter_up_factors,
    down_master_copy,
    down_first_moment,
    down_second_moment,
    up_master_copy,
    up_first_moment,
    up_second_moment,
    adapter_of_token,
    adapter_rank_bucket,
    adapter_owner_slot,
    live_token_counts,
):
    n_tensor = lax.axis_size("tensor")
    n_chip = n_tensor // 2
    tokens = cotangent.shape[0]
    rows_own, width = hidden.shape
    columns = width // n_tensor
    n_slot = adapter_owner_slot.shape[0]

    blocks = hidden.reshape(rows_own, n_tensor, columns).transpose(1, 0, 2)
    hidden_columns = lax.all_to_all(blocks, "tensor", 0, 0, tiled=True).reshape(tokens, columns)

    masked, turned, slot_wide, factor_wide, place, up_own = prep(
        rows_own,
        live_token_counts,
        adapter_rank_bucket,
        adapter_owner_slot,
        adapter_of_token.reshape(1, tokens),
        cotangent,
        adapter_up_factors,
    )
    factor = factor_wide[:, :PADDED_RANK]

    frozen_theirs = frozen_term(turned, frozen_key_value, 2)
    up_own = up_own + swap(up_own, 1, n_tensor)
    place, up_own, frozen_theirs = lax.optimization_barrier((place, up_own, frozen_theirs))
    from_pair = [swap(theirs, 1, n_tensor) for theirs in frozen_theirs]
    up_sum = sum_over_chips(up_own, n_tensor)

    packed = pack_rows(place, hidden_columns, masked, n_slot * CAP)
    packed, up_sum = lax.optimization_barrier((packed, up_sum))
    owned = lax.all_to_all(
        packed.reshape(n_slot, CAP, -1), "dp", 0, 0, tiled=True
    ).reshape(n_slot * CAP, -1)

    up_weight = (up_sum * factor).astype(jnp.bfloat16)
    down_own, extra_ours, extra_theirs = factor_products(
        rows_own, hidden_columns, up_weight, slot_wide, adapter_down_factors
    )
    extra_pair = swap(extra_theirs, 1, n_tensor)
    total, *sent = pair_sum(
        rows_own, turned, frozen_key_value, from_pair, extra_ours, extra_pair
    )
    down_own = down_own + swap(down_own, 1, n_tensor)
    down_own, total, sent = lax.optimization_barrier((down_own, total, sent))
    for step in range(1, n_chip):
        arrived = lax.ppermute(
            sent[step - 1], "tensor", [(i, (i + 2 * step) % n_tensor) for i in range(n_tensor)]
        )
        total = total + arrived.astype(jnp.float32)
    hidden_gradient = total.astype(jnp.bfloat16)

    down_weight = (sum_over_chips(down_own, n_tensor) * factor).astype(jnp.bfloat16)
    weights = jnp.concatenate([down_weight, up_weight], axis=1)
    pick = (
        jnp.arange(n_slot * CAP, dtype=jnp.int32)[:, None] == place
    ).astype(jnp.bfloat16)
    packed_weights = jnp.dot(pick, weights, preferred_element_type=jnp.float32).astype(
        jnp.bfloat16
    )
    owned, packed_weights = lax.optimization_barrier((owned, packed_weights))
    owned_weights = lax.all_to_all(
        packed_weights.reshape(n_slot, CAP, -1), "dp", 0, 0, tiled=True
    ).reshape(n_slot * CAP, -1)

    grad_down = contract_helper(owned[:, :columns], owned_weights[:, PADDED_RANK:], 0, 0) / tokens
    grad_up = contract_helper(owned_weights[:, :PADDED_RANK], owned[:, columns:], 0, 0) / tokens
    new_dm, new_dmo, new_ds = adamw(
        down_master_copy, down_first_moment, down_second_moment, grad_down
    )
    new_um, new_umo, new_us = adamw(up_master_copy, up_first_moment, up_second_moment, grad_up)
    return (hidden_gradient, new_dm, new_dmo, new_ds, new_um, new_umo, new_us)


def solution(mesh):
    return jax.shard_map(
        local,
        mesh=mesh,
        in_specs=(
            P(("dp", "tensor"), None),
            P("dp", "tensor"),
            P(None, "tensor"),
            P("tensor", None),
            P(None, "tensor"),
            P("tensor", "dp"),
            P("tensor", "dp"),
            P("tensor", "dp"),
            P("dp", "tensor"),
            P("dp", "tensor"),
            P("dp", "tensor"),
            P("dp", None),
            P(),
            P(),
            P(),
        ),
        out_specs=(
            P(("dp", "tensor"), None),
            P("tensor", "dp"),
            P("tensor", "dp"),
            P("tensor", "dp"),
            P("dp", "tensor"),
            P("dp", "tensor"),
            P("dp", "tensor"),
        ),
        check_vma=False,
    )
```

```python
import functools

import jax
import jax.numpy as jnp
from jax import lax
from jax.experimental import pallas as pl
from jax.experimental.pallas import tpu as pltpu
from jax.sharding import PartitionSpec as P

RMIN = 8
PADDED_RANK = 64
CAP = 16


adapter_alpha_scale = 16.0
beta_one = 0.9
beta_two = 0.999
adam_eps = 1e-08
learn_rate = 0.0002
weight_decay = 0.1
first_fix = 0.9999734386011124
second_fix = 0.09520785288629038


def adamw(master, moment, second, grad):
    new_moment = beta_one * moment + (1.0 - beta_one) * grad
    new_second = beta_two * second + (1.0 - beta_two) * grad * grad
    update = new_moment / first_fix / (jnp.sqrt(new_second / second_fix) + adam_eps)
    new_master = master - learn_rate * (update + weight_decay * master)
    return (new_master, new_moment, new_second)


def contract_helper(left, right, left_dim, right_dim):
    return lax.dot_general(
        left, right, (((left_dim,), (right_dim,)), ((), ())), preferred_element_type=jnp.float32
    )


def swap(value, mask, count):
    return lax.ppermute(value, "tensor", [(i, i ^ mask) for i in range(count)])


def sum_over_chips(value, count):
    near = value + swap(value, 2, count)
    far = swap(value, 4, count) + swap(value, 6, count)
    return near + far


VMEM_LIMIT = 16 * 1024 * 1024
VMEM_MOST = 60 * 1024 * 1024
VMEM_PAIR = 57 * 1024 * 1024
SMEM_SPEC = pl.BlockSpec(memory_space=pltpu.MemorySpace.SMEM)
HBM = pltpu.MemorySpace.HBM
NT = (((1,), (1,)), ((), ()))
NN = (((1,), (0,)), ((), ()))


def call(kernel, out_shape, flops, moved, limit=VMEM_LIMIT, **options):
    return pl.pallas_call(
        kernel,
        out_shape=out_shape,
        compiler_params=pltpu.CompilerParams(vmem_limit_bytes=limit),
        cost_estimate=pl.CostEstimate(flops=flops, bytes_accessed=moved, transcendentals=0),
        **options,
    )


def dot(left, right, dims):
    return lax.dot_general(left, right, dims, preferred_element_type=jnp.float32)


def lane_slot(shape, first):
    return (lax.broadcasted_iota(jnp.int32, shape, 1) // PADDED_RANK + first).astype(jnp.float32)


class Stream:
    def __init__(self, sources, targets, sems, depth=3):
        self.copies = [
            pltpu.make_async_copy(source, target, sems.at[i])
            for i, (source, target) in enumerate(zip(sources, targets, strict=True))
        ]
        self.depth = depth
        for copy in self.copies[:depth]:
            copy.start()

    def wait(self, c):
        self.copies[c].wait()
        if c + self.depth < len(self.copies):
            self.copies[c + self.depth].start()


def row_parts(ref, parts):
    rows = ref.shape[0] // parts
    return [ref.at[pl.ds(i * rows, rows), :] for i in range(parts)]


def prep_kernel(rows_own, live_ref, bucket_ref, owner_ref, adapter_ref, cot_ref, up_ref,
                masked_ref, turned_ref, slot_ref, factor_ref, place_ref, up_own_ref):
    tokens = cot_ref.shape[0]
    n_chip = tokens // rows_own // 2
    position = lax.axis_index("tensor")
    chip, core = position // 2, position % 2
    live = live_ref[lax.axis_index("dp")]
    token = lax.broadcasted_iota(jnp.int32, (tokens, 1), 0)
    masked = jnp.where(token < live, cot_ref[...].astype(jnp.float32), 0.0).astype(jnp.bfloat16)
    masked_ref[...] = masked
    for step in range(n_chip):
        block = (chip + step) % n_chip * 2
        for out, k in ((0, core), (tokens // 2, 1 - core)):
            start = pl.multiple_of((block + k) * rows_own, rows_own)
            ids = start + lax.broadcasted_iota(jnp.int32, (rows_own, 1), 0)
            rows = cot_ref[pl.ds(start, rows_own), :].astype(jnp.float32)
            turned_ref[pl.ds(out + step * rows_own, rows_own), :] = jnp.where(
                ids < live, rows, 0.0
            ).astype(jnp.bfloat16)
    adapter = adapter_ref[...]
    slot = jnp.zeros_like(adapter)
    rank = jnp.zeros_like(adapter)
    for a in range(owner_ref.shape[0]):
        hit = adapter == a
        slot = jnp.where(hit, owner_ref[a], slot)
        rank = jnp.where(hit, lax.shift_left(RMIN, bucket_ref[a]), rank)
    slot_row = slot.astype(jnp.float32)
    rank_row = rank.astype(jnp.float32)
    down = lax.broadcasted_iota(jnp.int32, (tokens, tokens), 0)
    across = lax.broadcasted_iota(jnp.int32, (tokens, tokens), 1)
    diagonal = down == across
    slot_col = jnp.sum(jnp.where(diagonal, slot_row, 0.0), axis=1, keepdims=True)
    rank_col = jnp.sum(jnp.where(diagonal, rank_row, 0.0), axis=1, keepdims=True)
    earlier = jnp.where((slot_col == slot_row) & (down < across), 1.0, 0.0)
    place = slot_row * CAP + jnp.sum(earlier, axis=0, keepdims=True)
    place_ref[...] = place.astype(jnp.int32)
    lanes = factor_ref.shape[1]
    slot_wide = jnp.broadcast_to(slot_col, (tokens, lanes))
    slot_ref[...] = slot_wide
    kept = lax.broadcasted_iota(jnp.int32, (tokens, lanes), 1) % PADDED_RANK
    factor_ref[...] = jnp.where(
        kept.astype(jnp.float32) < rank_col, adapter_alpha_scale / rank_col, 0.0
    )
    chunk = 256
    acc = jnp.zeros((tokens, chunk), jnp.float32)
    for c in range(up_ref.shape[0] // chunk):
        part = dot(masked, up_ref[pl.ds(c * chunk, chunk), :], NT)
        hit = slot_col == lane_slot((1, chunk), c * chunk // PADDED_RANK)
        acc = acc + jnp.where(hit, part, 0.0)
    acc = acc[:, :128] + acc[:, 128:]
    up_own_ref[...] = acc[:, :PADDED_RANK] + acc[:, PADDED_RANK:]


def prep(rows_own, live, bucket, owner, adapter_row, cotangent, up_factors):
    tokens, kv = cotangent.shape
    shapes = (
        jax.ShapeDtypeStruct((tokens, kv), jnp.bfloat16),
        jax.ShapeDtypeStruct((tokens, kv), jnp.bfloat16),
        jax.ShapeDtypeStruct((tokens, 128), jnp.float32),
        jax.ShapeDtypeStruct((tokens, 128), jnp.float32),
        jax.ShapeDtypeStruct((1, tokens), jnp.int32),
        jax.ShapeDtypeStruct((tokens, PADDED_RANK), jnp.float32),
    )
    return call(
        functools.partial(prep_kernel, rows_own),
        shapes,
        2 * tokens * kv * up_factors.shape[0],
        up_factors.size * 2,
        in_specs=[SMEM_SPEC] * 3
        + [pl.BlockSpec(v.shape) for v in (adapter_row, cotangent, up_factors)],
        name="prep",
    )(live, bucket, owner, adapter_row, cotangent, up_factors)


def frozen_kernel(turned_ref, frozen_any, *refs):
    outs, (frozen_ref, sems) = refs[:-2], refs[-2:]
    steps = sems.shape[0]
    half = outs[0].shape[0]
    chunk = frozen_ref.shape[0] // steps
    per_part = steps // len(outs)
    stream = Stream(row_parts(frozen_any, steps), row_parts(frozen_ref, steps), sems)
    theirs = turned_ref[half:, :]
    for c in range(steps):
        stream.wait(c)
        first = c % per_part * chunk
        outs[c // per_part][:, first : first + chunk] = dot(
            theirs, frozen_ref[c * chunk : (c + 1) * chunk, :], NT
        )


def frozen_term(turned, frozen, parts):
    tokens, kv = turned.shape
    width = frozen.shape[0]
    return call(
        frozen_kernel,
        (jax.ShapeDtypeStruct((tokens // 2, width // parts), jnp.float32),) * parts,
        tokens * kv * width,
        2 * kv * width + 2 * tokens * width,
        VMEM_MOST,
        in_specs=[pl.BlockSpec(turned.shape), pl.BlockSpec(memory_space=HBM)],
        scratch_shapes=[
            pltpu.VMEM(frozen.shape, frozen.dtype),
            pltpu.SemaphoreType.DMA((8,)),
        ],
        name="frozen_term",
    )(turned, frozen)


def pack_kernel(place_ref, hidden_ref, masked_ref, out_ref):
    rows, tokens = out_ref.shape[0], place_ref.shape[1]
    down = lax.broadcasted_iota(jnp.int32, (rows, tokens), 0)
    pick = jnp.where(down == place_ref[...], 1.0, 0.0).astype(jnp.bfloat16)
    width = hidden_ref.shape[1]
    out_ref[:, :width] = dot(pick, hidden_ref[...], NN).astype(jnp.bfloat16)
    out_ref[:, width:] = dot(pick, masked_ref[...], NN).astype(jnp.bfloat16)


def pack_rows(place, hidden_columns, masked, rows):
    tokens, columns = masked.shape[0], hidden_columns.shape[1] + masked.shape[1]
    return call(
        pack_kernel,
        jax.ShapeDtypeStruct((rows, columns), jnp.bfloat16),
        2 * rows * columns * tokens,
        2 * (rows + tokens) * columns,
        name="pack",
    )(place, hidden_columns, masked)


def factors_kernel(rows_own, hidden_ref, weight_ref, slot_ref, factors_ref, down_ref, ours_ref,
                   theirs_ref, held_ref, extra_ref, sems):
    parts, columns, chunk = held_ref.shape
    tokens = hidden_ref.shape[0]
    n_chip = tokens // rows_own // 2
    stream = Stream(
        [factors_ref.at[:, pl.ds(c * chunk, chunk)] for c in range(parts)],
        [held_ref.at[c] for c in range(parts)],
        sems,
    )
    slot = slot_ref[...]
    weight = weight_ref[...].astype(jnp.float32)
    double = jnp.concatenate([weight, weight], axis=1)
    acc = jnp.zeros((tokens, 128), jnp.float32)
    for c in range(parts):
        stream.wait(c)
        factors = held_ref[c]
        product = dot(hidden_ref[...], factors, NN)
        pieces = []
        for d in range(chunk // 128):
            hit = slot == lane_slot((1, 128), (c * chunk + d * 128) // PADDED_RANK)
            acc = acc + jnp.where(hit, product[:, d * 128 : (d + 1) * 128], 0.0)
            pieces.append(jnp.where(hit, double, 0.0).astype(jnp.bfloat16))
        term = dot(jnp.concatenate(pieces, axis=1), factors, NT)
        if c == 0:
            extra_ref[...] = term
        else:
            extra_ref[...] += term
    down_ref[...] = acc[:, :PADDED_RANK] + acc[:, PADDED_RANK:]
    position = lax.axis_index("tensor")
    chip, core = position // 2, position % 2
    for turn in range(n_chip):
        block = (chip + turn) % n_chip * 2
        for out, k in ((ours_ref, core), (theirs_ref, 1 - core)):
            start = pl.multiple_of((block + k) * rows_own, rows_own)
            out[pl.ds(turn * rows_own, rows_own), :] = extra_ref[pl.ds(start, rows_own), :]


def factor_products(rows_own, hidden_columns, up_weight, slot_wide, factors):
    tokens, columns = hidden_columns.shape
    chunk = 256
    parts = factors.shape[1] // chunk
    half = jax.ShapeDtypeStruct((tokens // 2, columns), jnp.float32)
    shapes = (jax.ShapeDtypeStruct((tokens, PADDED_RANK), jnp.float32), half, half)
    return call(
        functools.partial(factors_kernel, rows_own),
        shapes,
        4 * tokens * factors.size,
        2 * factors.size,
        VMEM_MOST,
        in_specs=[pl.BlockSpec(v.shape) for v in (hidden_columns, up_weight, slot_wide)]
        + [pl.BlockSpec(memory_space=HBM)],
        scratch_shapes=[
            pltpu.VMEM((parts, columns, chunk), jnp.bfloat16),
            pltpu.VMEM((tokens, columns), jnp.float32),
            pltpu.SemaphoreType.DMA((parts,)),
        ],
        name="factor_products",
    )(hidden_columns, up_weight, slot_wide, factors)


def pair_kernel(rows_own, parts, turned_ref, extra_ours_ref, extra_pair_ref, frozen_any, *refs):
    pair_refs, outs, (frozen_ref, sems) = refs[:parts], refs[parts:-2], refs[-2:]
    steps = sems.shape[0]
    half, columns = extra_ours_ref.shape
    per_part = steps // parts
    stream = Stream(row_parts(frozen_any, steps), row_parts(frozen_ref, steps), sems)
    position = lax.axis_index("tensor")
    chip, core = position // 2, position % 2
    ours = turned_ref[:half, :]
    low = jnp.where(core == 0, extra_ours_ref[...], extra_pair_ref[...])
    high = jnp.where(core == 0, extra_pair_ref[...], extra_ours_ref[...])
    for c in range(steps):
        stream.wait(c)
        at = slice(c * columns, (c + 1) * columns)
        first = c % per_part * columns
        total = dot(ours, frozen_ref[at, :], NT)
        total = total + pair_refs[c // per_part][:, first : first + columns]
        total = total + jnp.where(chip == c // 2, low if c % 2 == 0 else high, 0.0)
        outs[0][:, at] = total[:rows_own, :]
        for i, out in enumerate(outs[1:]):
            out[:, at] = total[(i + 1) * rows_own : (i + 2) * rows_own, :].astype(jnp.bfloat16)


def pair_sum(rows_own, turned, frozen, from_pair, extra_ours, extra_pair):
    parts = len(from_pair)
    half, columns = extra_ours.shape
    width, kv = frozen.shape
    sent = jax.ShapeDtypeStruct((rows_own, width), jnp.bfloat16)
    n_out = half // rows_own - 1
    return call(
        functools.partial(pair_kernel, rows_own, parts),
        (jax.ShapeDtypeStruct((rows_own, width), jnp.float32),) + (sent,) * n_out,
        2 * half * width * kv,
        2 * kv * width + 6 * half * width,
        VMEM_PAIR,
        in_specs=[pl.BlockSpec(v.shape) for v in (turned, extra_ours, extra_pair)]
        + [pl.BlockSpec(memory_space=HBM)]
        + [pl.BlockSpec(v.shape) for v in from_pair],
        scratch_shapes=[
            pltpu.VMEM(frozen.shape, frozen.dtype),
            pltpu.SemaphoreType.DMA((width // columns,)),
        ],
        name="pair_sum",
    )(turned, extra_ours, extra_pair, frozen, *from_pair)


def local(
    hidden,
    cotangent,
    frozen_key_value,
    adapter_down_factors,
    adapter_up_factors,
    down_master_copy,
    down_first_moment,
    down_second_moment,
    up_master_copy,
    up_first_moment,
    up_second_moment,
    adapter_of_token,
    adapter_rank_bucket,
    adapter_owner_slot,
    live_token_counts,
):
    n_tensor = lax.axis_size("tensor")
    n_chip = n_tensor // 2
    tokens = cotangent.shape[0]
    rows_own, width = hidden.shape
    columns = width // n_tensor
    n_slot = adapter_owner_slot.shape[0]

    blocks = hidden.reshape(rows_own, n_tensor, columns).transpose(1, 0, 2)
    hidden_columns = lax.all_to_all(blocks, "tensor", 0, 0, tiled=True).reshape(tokens, columns)

    masked, turned, slot_wide, factor_wide, place, up_own = prep(
        rows_own,
        live_token_counts,
        adapter_rank_bucket,
        adapter_owner_slot,
        adapter_of_token.reshape(1, tokens),
        cotangent,
        adapter_up_factors,
    )
    factor = factor_wide[:, :PADDED_RANK]

    frozen_theirs = frozen_term(turned, frozen_key_value, 2)
    up_own = up_own + swap(up_own, 1, n_tensor)
    place, up_own, frozen_theirs = lax.optimization_barrier((place, up_own, frozen_theirs))
    from_pair = [swap(theirs, 1, n_tensor) for theirs in frozen_theirs]
    up_sum = sum_over_chips(up_own, n_tensor)

    packed = pack_rows(place, hidden_columns, masked, n_slot * CAP)
    owned = lax.all_to_all(
        packed.reshape(n_slot, CAP, -1), "dp", 0, 0, tiled=True
    ).reshape(n_slot * CAP, -1)

    up_weight = (up_sum * factor).astype(jnp.bfloat16)
    down_own, extra_ours, extra_theirs = factor_products(
        rows_own, hidden_columns, up_weight, slot_wide, adapter_down_factors
    )
    extra_pair = swap(extra_theirs, 1, n_tensor)
    total, *sent = pair_sum(
        rows_own, turned, frozen_key_value, from_pair, extra_ours, extra_pair
    )
    down_own = down_own + swap(down_own, 1, n_tensor)
    down_own, total, sent = lax.optimization_barrier((down_own, total, sent))
    for step in range(1, n_chip):
        arrived = lax.ppermute(
            sent[step - 1], "tensor", [(i, (i + 2 * step) % n_tensor) for i in range(n_tensor)]
        )
        total = total + arrived.astype(jnp.float32)
    hidden_gradient = total.astype(jnp.bfloat16)

    down_weight = (sum_over_chips(down_own, n_tensor) * factor).astype(jnp.bfloat16)
    weights = jnp.concatenate([down_weight, up_weight], axis=1)
    pick = (
        jnp.arange(n_slot * CAP, dtype=jnp.int32)[:, None] == place
    ).astype(jnp.bfloat16)
    packed_weights = jnp.dot(pick, weights, preferred_element_type=jnp.float32).astype(
        jnp.bfloat16
    )
    owned, packed_weights = lax.optimization_barrier((owned, packed_weights))
    owned_weights = lax.all_to_all(
        packed_weights.reshape(n_slot, CAP, -1), "dp", 0, 0, tiled=True
    ).reshape(n_slot * CAP, -1)

    grad_down = contract_helper(owned[:, :columns], owned_weights[:, PADDED_RANK:], 0, 0) / tokens
    grad_up = contract_helper(owned_weights[:, :PADDED_RANK], owned[:, columns:], 0, 0) / tokens
    new_dm, new_dmo, new_ds = adamw(
        down_master_copy, down_first_moment, down_second_moment, grad_down
    )
    new_um, new_umo, new_us = adamw(up_master_copy, up_first_moment, up_second_moment, grad_up)
    return (hidden_gradient, new_dm, new_dmo, new_ds, new_um, new_umo, new_us)


def solution(mesh):
    return jax.shard_map(
        local,
        mesh=mesh,
        in_specs=(
            P(("dp", "tensor"), None),
            P("dp", "tensor"),
            P(None, "tensor"),
            P("tensor", None),
            P(None, "tensor"),
            P("tensor", "dp"),
            P("tensor", "dp"),
            P("tensor", "dp"),
            P("dp", "tensor"),
            P("dp", "tensor"),
            P("dp", "tensor"),
            P("dp", None),
            P(),
            P(),
            P(),
        ),
        out_specs=(
            P(("dp", "tensor"), None),
            P("tensor", "dp"),
            P("tensor", "dp"),
            P("tensor", "dp"),
            P("dp", "tensor"),
            P("dp", "tensor"),
            P("dp", "tensor"),
        ),
        check_vma=False,
    )
```

```python
import functools

import jax
import jax.numpy as jnp
from jax import lax
from jax.experimental import pallas as pl
from jax.experimental.pallas import tpu as pltpu
from jax.sharding import PartitionSpec as P

RMIN = 8
PADDED_RANK = 64
CAP = 16


adapter_alpha_scale = 16.0
beta_one = 0.9
beta_two = 0.999
adam_eps = 1e-08
learn_rate = 0.0002
weight_decay = 0.1
first_fix = 0.9999734386011124
second_fix = 0.09520785288629038


def adamw(master, moment, second, grad):
    new_moment = beta_one * moment + (1.0 - beta_one) * grad
    new_second = beta_two * second + (1.0 - beta_two) * grad * grad
    update = new_moment / first_fix / (jnp.sqrt(new_second / second_fix) + adam_eps)
    new_master = master - learn_rate * (update + weight_decay * master)
    return (new_master, new_moment, new_second)


def contract_helper(left, right, left_dim, right_dim):
    return lax.dot_general(
        left, right, (((left_dim,), (right_dim,)), ((), ())), preferred_element_type=jnp.float32
    )


def swap(value, mask, count):
    return lax.ppermute(value, "tensor", [(i, i ^ mask) for i in range(count)])


def sum_over_chips(value, count):
    near = value + swap(value, 2, count)
    far = swap(value, 4, count) + swap(value, 6, count)
    return near + far


VMEM_LIMIT = 16 * 1024 * 1024
VMEM_MOST = 60 * 1024 * 1024
SMEM_SPEC = pl.BlockSpec(memory_space=pltpu.MemorySpace.SMEM)
HBM = pltpu.MemorySpace.HBM
NT = (((1,), (1,)), ((), ()))
NN = (((1,), (0,)), ((), ()))


def call(kernel, out_shape, flops, moved, limit=VMEM_LIMIT, **options):
    return pl.pallas_call(
        kernel,
        out_shape=out_shape,
        compiler_params=pltpu.CompilerParams(vmem_limit_bytes=limit),
        cost_estimate=pl.CostEstimate(flops=flops, bytes_accessed=moved, transcendentals=0),
        **options,
    )


def dot(left, right, dims):
    return lax.dot_general(left, right, dims, preferred_element_type=jnp.float32)


def lane_slot(shape, first):
    return (lax.broadcasted_iota(jnp.int32, shape, 1) // PADDED_RANK + first).astype(jnp.float32)


class Stream:
    def __init__(self, sources, targets, sems, depth=3):
        self.copies = [
            pltpu.make_async_copy(source, target, sems.at[i])
            for i, (source, target) in enumerate(zip(sources, targets, strict=True))
        ]
        self.depth = depth
        for copy in self.copies[:depth]:
            copy.start()

    def wait(self, c):
        self.copies[c].wait()
        if c + self.depth < len(self.copies):
            self.copies[c + self.depth].start()


def row_parts(ref, parts):
    rows = ref.shape[0] // parts
    return [ref.at[pl.ds(i * rows, rows), :] for i in range(parts)]


def prep_kernel(rows_own, live_ref, bucket_ref, owner_ref, adapter_ref, cot_ref, up_ref,
                masked_ref, turned_ref, slot_ref, factor_ref, place_ref, up_own_ref):
    tokens = cot_ref.shape[0]
    n_chip = tokens // rows_own // 2
    position = lax.axis_index("tensor")
    chip, core = position // 2, position % 2
    live = live_ref[lax.axis_index("dp")]
    token = lax.broadcasted_iota(jnp.int32, (tokens, 1), 0)
    masked = jnp.where(token < live, cot_ref[...].astype(jnp.float32), 0.0).astype(jnp.bfloat16)
    masked_ref[...] = masked
    for step in range(n_chip):
        block = (chip + step) % n_chip * 2
        for out, k in ((0, core), (tokens // 2, 1 - core)):
            start = pl.multiple_of((block + k) * rows_own, rows_own)
            ids = start + lax.broadcasted_iota(jnp.int32, (rows_own, 1), 0)
            rows = cot_ref[pl.ds(start, rows_own), :].astype(jnp.float32)
            turned_ref[pl.ds(out + step * rows_own, rows_own), :] = jnp.where(
                ids < live, rows, 0.0
            ).astype(jnp.bfloat16)
    adapter = adapter_ref[...]
    slot = jnp.zeros_like(adapter)
    rank = jnp.zeros_like(adapter)
    for a in range(owner_ref.shape[0]):
        hit = adapter == a
        slot = jnp.where(hit, owner_ref[a], slot)
        rank = jnp.where(hit, lax.shift_left(RMIN, bucket_ref[a]), rank)
    slot_row = slot.astype(jnp.float32)
    rank_row = rank.astype(jnp.float32)
    down = lax.broadcasted_iota(jnp.int32, (tokens, tokens), 0)
    across = lax.broadcasted_iota(jnp.int32, (tokens, tokens), 1)
    diagonal = down == across
    slot_col = jnp.sum(jnp.where(diagonal, slot_row, 0.0), axis=1, keepdims=True)
    rank_col = jnp.sum(jnp.where(diagonal, rank_row, 0.0), axis=1, keepdims=True)
    earlier = jnp.where((slot_col == slot_row) & (down < across), 1.0, 0.0)
    place = slot_row * CAP + jnp.sum(earlier, axis=0, keepdims=True)
    place_ref[...] = place.astype(jnp.int32)
    lanes = factor_ref.shape[1]
    slot_wide = jnp.broadcast_to(slot_col, (tokens, lanes))
    slot_ref[...] = slot_wide
    kept = lax.broadcasted_iota(jnp.int32, (tokens, lanes), 1) % PADDED_RANK
    factor_ref[...] = jnp.where(
        kept.astype(jnp.float32) < rank_col, adapter_alpha_scale / rank_col, 0.0
    )
    chunk = 256
    acc = jnp.zeros((tokens, chunk), jnp.float32)
    for c in range(up_ref.shape[0] // chunk):
        part = dot(masked, up_ref[pl.ds(c * chunk, chunk), :], NT)
        hit = slot_col == lane_slot((1, chunk), c * chunk // PADDED_RANK)
        acc = acc + jnp.where(hit, part, 0.0)
    acc = acc[:, :128] + acc[:, 128:]
    up_own_ref[...] = acc[:, :PADDED_RANK] + acc[:, PADDED_RANK:]


def prep(rows_own, live, bucket, owner, adapter_row, cotangent, up_factors):
    tokens, kv = cotangent.shape
    shapes = (
        jax.ShapeDtypeStruct((tokens, kv), jnp.bfloat16),
        jax.ShapeDtypeStruct((tokens, kv), jnp.bfloat16),
        jax.ShapeDtypeStruct((tokens, 128), jnp.float32),
        jax.ShapeDtypeStruct((tokens, 128), jnp.float32),
        jax.ShapeDtypeStruct((1, tokens), jnp.int32),
        jax.ShapeDtypeStruct((tokens, PADDED_RANK), jnp.float32),
    )
    return call(
        functools.partial(prep_kernel, rows_own),
        shapes,
        2 * tokens * kv * up_factors.shape[0],
        up_factors.size * 2,
        in_specs=[SMEM_SPEC] * 3
        + [pl.BlockSpec(v.shape) for v in (adapter_row, cotangent, up_factors)],
        name="prep",
    )(live, bucket, owner, adapter_row, cotangent, up_factors)


def frozen_kernel(turned_ref, frozen_any, *refs):
    outs, (frozen_ref, sems) = refs[:-2], refs[-2:]
    steps = sems.shape[0]
    half = outs[0].shape[0]
    chunk = frozen_ref.shape[0] // steps
    per_part = steps // len(outs)
    stream = Stream(row_parts(frozen_any, steps), row_parts(frozen_ref, steps), sems)
    theirs = turned_ref[half:, :]
    for c in range(steps):
        stream.wait(c)
        first = c % per_part * chunk
        outs[c // per_part][:, first : first + chunk] = dot(
            theirs, frozen_ref[c * chunk : (c + 1) * chunk, :], NT
        )


def frozen_term(turned, frozen, parts):
    tokens, kv = turned.shape
    width = frozen.shape[0]
    return call(
        frozen_kernel,
        (jax.ShapeDtypeStruct((tokens // 2, width // parts), jnp.float32),) * parts,
        tokens * kv * width,
        2 * kv * width + 2 * tokens * width,
        VMEM_MOST,
        in_specs=[pl.BlockSpec(turned.shape), pl.BlockSpec(memory_space=HBM)],
        scratch_shapes=[
            pltpu.VMEM(frozen.shape, frozen.dtype),
            pltpu.SemaphoreType.DMA((8,)),
        ],
        name="frozen_term",
    )(turned, frozen)


def pack_kernel(place_ref, *refs):
    parts, out_ref = refs[:-1], refs[-1]
    rows, tokens = out_ref.shape[0], place_ref.shape[1]
    down = lax.broadcasted_iota(jnp.int32, (rows, tokens), 0)
    pick = jnp.where(down == place_ref[...], 1.0, 0.0).astype(jnp.bfloat16)
    first = 0
    for part in parts:
        width = part.shape[1]
        out_ref[:, first : first + width] = dot(pick, part[...], NN).astype(jnp.bfloat16)
        first += width


def pack_rows(place, parts, rows):
    tokens, columns = place.shape[1], sum(v.shape[1] for v in parts)
    return call(
        pack_kernel,
        jax.ShapeDtypeStruct((rows, columns), jnp.bfloat16),
        2 * rows * columns * tokens,
        2 * (rows + tokens) * columns,
        name="pack",
    )(place, *parts)


def factor_stream(factors_any, held_ref, sems):
    parts, _, chunk = held_ref.shape
    return Stream(
        [factors_any.at[:, pl.ds(c * chunk, chunk)] for c in range(parts)],
        [held_ref.at[c] for c in range(parts)],
        sems,
    )


def down_kernel(hidden_ref, slot_ref, factors_any, out_ref, held_ref, sems):
    parts, _, chunk = held_ref.shape
    tokens = hidden_ref.shape[0]
    stream = factor_stream(factors_any, held_ref, sems)
    slot = slot_ref[...]
    acc = jnp.zeros((tokens, 128), jnp.float32)
    for c in range(parts):
        stream.wait(c)
        product = dot(hidden_ref[...], held_ref[c], NN)
        for d in range(chunk // 128):
            hit = slot == lane_slot((1, 128), (c * chunk + d * 128) // PADDED_RANK)
            acc = acc + jnp.where(hit, product[:, d * 128 : (d + 1) * 128], 0.0)
    out_ref[...] = acc[:, :PADDED_RANK] + acc[:, PADDED_RANK:]


def low_rank(hidden_columns, slot_wide, factors):
    tokens, columns = hidden_columns.shape
    chunk = 256
    parts = factors.shape[1] // chunk
    return call(
        down_kernel,
        jax.ShapeDtypeStruct((tokens, PADDED_RANK), jnp.float32),
        2 * tokens * factors.size,
        2 * factors.size,
        VMEM_MOST,
        in_specs=[pl.BlockSpec(v.shape) for v in (hidden_columns, slot_wide)]
        + [pl.BlockSpec(memory_space=HBM)],
        scratch_shapes=[
            pltpu.VMEM((parts, columns, chunk), jnp.bfloat16),
            pltpu.SemaphoreType.DMA((parts,)),
        ],
        name="low_rank",
    )(hidden_columns, slot_wide, factors)


def extra_kernel(rows_own, weight_ref, slot_ref, factors_any, ours_ref, theirs_ref, held_ref,
                 extra_ref, sems):
    parts, _, chunk = held_ref.shape
    tokens = weight_ref.shape[0]
    n_chip = tokens // rows_own // 2
    stream = factor_stream(factors_any, held_ref, sems)
    slot = slot_ref[...]
    weight = weight_ref[:, PADDED_RANK:].astype(jnp.float32)
    double = jnp.concatenate([weight, weight], axis=1)
    for c in range(parts):
        stream.wait(c)
        pieces = []
        for d in range(chunk // 128):
            hit = slot == lane_slot((1, 128), (c * chunk + d * 128) // PADDED_RANK)
            pieces.append(jnp.where(hit, double, 0.0).astype(jnp.bfloat16))
        term = dot(jnp.concatenate(pieces, axis=1), held_ref[c], NT)
        if c == 0:
            extra_ref[...] = term
        else:
            extra_ref[...] += term
    position = lax.axis_index("tensor")
    chip, core = position // 2, position % 2
    for turn in range(n_chip):
        block = (chip + turn) % n_chip * 2
        for out, k in ((ours_ref, core), (theirs_ref, 1 - core)):
            start = pl.multiple_of((block + k) * rows_own, rows_own)
            out[pl.ds(turn * rows_own, rows_own), :] = extra_ref[pl.ds(start, rows_own), :]


def extra_term(rows_own, weights, slot_wide, factors):
    tokens, columns = weights.shape[0], factors.shape[0]
    chunk = 256
    parts = factors.shape[1] // chunk
    half = jax.ShapeDtypeStruct((tokens // 2, columns), jnp.float32)
    return call(
        functools.partial(extra_kernel, rows_own),
        (half, half),
        2 * tokens * factors.size,
        2 * factors.size,
        VMEM_MOST,
        in_specs=[pl.BlockSpec(v.shape) for v in (weights, slot_wide)]
        + [pl.BlockSpec(memory_space=HBM)],
        scratch_shapes=[
            pltpu.VMEM((parts, columns, chunk), jnp.bfloat16),
            pltpu.VMEM((tokens, columns), jnp.float32),
            pltpu.SemaphoreType.DMA((parts,)),
        ],
        name="extra_term",
    )(weights, slot_wide, factors)


def pair_kernel(rows_own, parts, turned_ref, frozen_any, *refs):
    pair_refs, outs, (frozen_ref, sems) = refs[:parts], refs[parts:-2], refs[-2:]
    steps = sems.shape[0]
    half = turned_ref.shape[0] // 2
    columns = frozen_ref.shape[0] // steps
    per_part = steps // parts
    stream = Stream(row_parts(frozen_any, steps), row_parts(frozen_ref, steps), sems)
    ours = turned_ref[:half, :]
    for c in range(steps):
        stream.wait(c)
        at = slice(c * columns, (c + 1) * columns)
        first = c % per_part * columns
        total = dot(ours, frozen_ref[at, :], NT)
        total = total + pair_refs[c // per_part][:, first : first + columns]
        outs[0][:, at] = total[:rows_own, :]
        for i, out in enumerate(outs[1:]):
            out[:, at] = total[(i + 1) * rows_own : (i + 2) * rows_own, :].astype(jnp.bfloat16)


def pair_sum(rows_own, turned, frozen, from_pair):
    parts = len(from_pair)
    half = turned.shape[0] // 2
    width, kv = frozen.shape
    sent = jax.ShapeDtypeStruct((rows_own, width), jnp.bfloat16)
    n_out = half // rows_own - 1
    return call(
        functools.partial(pair_kernel, rows_own, parts),
        (jax.ShapeDtypeStruct((rows_own, width), jnp.float32),) + (sent,) * n_out,
        2 * half * width * kv,
        2 * kv * width + 6 * half * width,
        VMEM_MOST,
        in_specs=[pl.BlockSpec(turned.shape), pl.BlockSpec(memory_space=HBM)]
        + [pl.BlockSpec(v.shape) for v in from_pair],
        scratch_shapes=[
            pltpu.VMEM(frozen.shape, frozen.dtype),
            pltpu.SemaphoreType.DMA((8,)),
        ],
        name="pair_sum",
    )(turned, frozen, *from_pair)


def last_kernel(*refs):
    count = (len(refs) - 1) // 2
    frozen_refs, extra_refs, out_ref = refs[:count], refs[count:-1], refs[-1]
    columns = extra_refs[0].shape[1]
    chip = lax.axis_index("tensor") // 2
    for step, extra_ref in enumerate(extra_refs):
        block = (chip + count - step) % count
        at = pl.ds(pl.multiple_of(block * columns, columns), columns)
        total = extra_ref[...].astype(jnp.float32)
        for frozen_ref in frozen_refs:
            total = total + frozen_ref[:, at].astype(jnp.float32)
        out_ref[:, at] = total.astype(jnp.bfloat16)


def last_sum(frozen_terms, extra_terms):
    size = frozen_terms[0].size
    values = [*frozen_terms, *extra_terms]
    return call(
        last_kernel,
        jax.ShapeDtypeStruct(frozen_terms[0].shape, jnp.bfloat16),
        5 * size,
        16 * size,
        in_specs=[pl.BlockSpec(v.shape) for v in values],
        name="last_sum",
    )(*values)


def local(
    hidden,
    cotangent,
    frozen_key_value,
    adapter_down_factors,
    adapter_up_factors,
    down_master_copy,
    down_first_moment,
    down_second_moment,
    up_master_copy,
    up_first_moment,
    up_second_moment,
    adapter_of_token,
    adapter_rank_bucket,
    adapter_owner_slot,
    live_token_counts,
):
    n_tensor = lax.axis_size("tensor")
    n_chip = n_tensor // 2
    tokens = cotangent.shape[0]
    rows_own, width = hidden.shape
    columns = width // n_tensor
    n_slot = adapter_owner_slot.shape[0]

    blocks = hidden.reshape(rows_own, n_tensor, columns).transpose(1, 0, 2)
    hidden_columns = lax.all_to_all(blocks, "tensor", 0, 0, tiled=True).reshape(tokens, columns)

    masked, turned, slot_wide, factor_wide, place, up_own = prep(
        rows_own,
        live_token_counts,
        adapter_rank_bucket,
        adapter_owner_slot,
        adapter_of_token.reshape(1, tokens),
        cotangent,
        adapter_up_factors,
    )

    frozen_theirs = frozen_term(turned, frozen_key_value, 4)
    up_own = up_own + swap(up_own, 1, n_tensor)
    slot_wide, up_own, frozen_theirs = lax.optimization_barrier(
        (slot_wide, up_own, frozen_theirs)
    )
    from_pair = [swap(theirs, 1, n_tensor) for theirs in frozen_theirs]

    own = low_rank(hidden_columns, slot_wide, adapter_down_factors)
    own = jnp.concatenate([own + swap(own, 1, n_tensor), up_own], axis=1)
    weights = (sum_over_chips(own, n_tensor) * factor_wide).astype(jnp.bfloat16)
    total, *sent = pair_sum(rows_own, turned, frozen_key_value, from_pair)

    packed = pack_rows(place, [hidden_columns, masked, weights], n_slot * CAP)
    after = lax.optimization_barrier((weights, total, sent))
    owned = lax.all_to_all(
        packed.reshape(n_slot, CAP, -1), "dp", 0, 0, tiled=True
    ).reshape(n_slot * CAP, -1)

    def to_chips(sent):
        return [
            lax.ppermute(
                value, "tensor", [(i, (i + 2 * step) % n_tensor) for i in range(n_tensor)]
            )
            for step, value in enumerate(sent, 1)
        ]

    weights, total, sent = after
    arrived = to_chips(sent)
    extra_ours, extra_theirs = extra_term(rows_own, weights, slot_wide, adapter_down_factors)
    extra_pair = swap(extra_theirs, 1, n_tensor)
    low_core = lax.axis_index("tensor") % 2 == 0
    extra = jnp.concatenate(
        [
            jnp.where(low_core, extra_ours, extra_pair),
            jnp.where(low_core, extra_pair, extra_ours),
        ],
        axis=1,
    ).reshape(n_chip, rows_own, 2 * columns)
    extra_sent = extra[1:].astype(jnp.bfloat16)
    extra_arrived = to_chips([extra_sent[i] for i in range(n_chip - 1)])
    hidden_gradient = last_sum([total, *arrived], [extra[0], *extra_arrived])

    kv = cotangent.shape[1]
    owned_hidden, owned_cot = owned[:, :columns], owned[:, columns : columns + kv]
    owned_down = owned[:, columns + kv : columns + kv + PADDED_RANK]
    owned_up = owned[:, columns + kv + PADDED_RANK :]
    grad_down = contract_helper(owned_hidden, owned_up, 0, 0) / tokens
    grad_up = contract_helper(owned_down, owned_cot, 0, 0) / tokens
    new_dm, new_dmo, new_ds = adamw(
        down_master_copy, down_first_moment, down_second_moment, grad_down
    )
    new_um, new_umo, new_us = adamw(up_master_copy, up_first_moment, up_second_moment, grad_up)
    return (hidden_gradient, new_dm, new_dmo, new_ds, new_um, new_umo, new_us)


def solution(mesh):
    return jax.shard_map(
        local,
        mesh=mesh,
        in_specs=(
            P(("dp", "tensor"), None),
            P("dp", "tensor"),
            P(None, "tensor"),
            P("tensor", None),
            P(None, "tensor"),
            P("tensor", "dp"),
            P("tensor", "dp"),
            P("tensor", "dp"),
            P("dp", "tensor"),
            P("dp", "tensor"),
            P("dp", "tensor"),
            P("dp", None),
            P(),
            P(),
            P(),
        ),
        out_specs=(
            P(("dp", "tensor"), None),
            P("tensor", "dp"),
            P("tensor", "dp"),
            P("tensor", "dp"),
            P("dp", "tensor"),
            P("dp", "tensor"),
            P("dp", "tensor"),
        ),
        check_vma=False,
    )
```

```python
import functools

import jax
import jax.numpy as jnp
from jax import lax
from jax.experimental import pallas as pl
from jax.experimental.pallas import tpu as pltpu
from jax.sharding import PartitionSpec as P

RMIN = 8
PADDED_RANK = 64
CAP = 16


adapter_alpha_scale = 16.0
beta_one = 0.9
beta_two = 0.999
adam_eps = 1e-08
learn_rate = 0.0002
weight_decay = 0.1
first_fix = 0.9999734386011124
second_fix = 0.09520785288629038


def adamw(master, moment, second, grad):
    new_moment = beta_one * moment + (1.0 - beta_one) * grad
    new_second = beta_two * second + (1.0 - beta_two) * grad * grad
    update = new_moment / first_fix / (jnp.sqrt(new_second / second_fix) + adam_eps)
    new_master = master - learn_rate * (update + weight_decay * master)
    return (new_master, new_moment, new_second)


def contract_helper(left, right, left_dim, right_dim):
    return lax.dot_general(
        left, right, (((left_dim,), (right_dim,)), ((), ())), preferred_element_type=jnp.float32
    )


def swap(value, mask, count):
    return lax.ppermute(value, "tensor", [(i, i ^ mask) for i in range(count)])


def sum_over_chips(value, count):
    near = value + swap(value, 2, count)
    far = swap(value, 4, count) + swap(value, 6, count)
    return near + far


VMEM_LIMIT = 16 * 1024 * 1024
SMEM_SPEC = pl.BlockSpec(memory_space=pltpu.MemorySpace.SMEM)
VMEM_SPEC = pl.BlockSpec(memory_space=pltpu.MemorySpace.VMEM)
NT = (((1,), (1,)), ((), ()))
NN = (((1,), (0,)), ((), ()))


def call(kernel, out_shape, flops, moved, **options):
    return pl.pallas_call(
        kernel,
        out_shape=out_shape,
        compiler_params=pltpu.CompilerParams(vmem_limit_bytes=VMEM_LIMIT),
        cost_estimate=pl.CostEstimate(flops=flops, bytes_accessed=moved, transcendentals=0),
        **options,
    )


def dot(left, right, dims):
    return lax.dot_general(left, right, dims, preferred_element_type=jnp.float32)


def lane_slot(shape, first):
    return (lax.broadcasted_iota(jnp.int32, shape, 1) // PADDED_RANK + first).astype(jnp.float32)


def prep_kernel(rows_own, live_ref, bucket_ref, owner_ref, adapter_ref, cot_ref, up_ref,
                masked_ref, turned_ref, slot_ref, factor_ref, place_ref, up_own_ref):
    tokens = cot_ref.shape[0]
    n_chip = tokens // rows_own // 2
    position = lax.axis_index("tensor")
    chip, core = position // 2, position % 2
    live = live_ref[lax.axis_index("dp")]
    token = lax.broadcasted_iota(jnp.int32, (tokens, 1), 0)
    masked = jnp.where(token < live, cot_ref[...].astype(jnp.float32), 0.0).astype(jnp.bfloat16)
    masked_ref[...] = masked
    for step in range(n_chip):
        block = (chip + step) % n_chip * 2
        for out, k in ((0, core), (tokens // 2, 1 - core)):
            start = pl.multiple_of((block + k) * rows_own, rows_own)
            ids = start + lax.broadcasted_iota(jnp.int32, (rows_own, 1), 0)
            rows = cot_ref[pl.ds(start, rows_own), :].astype(jnp.float32)
            turned_ref[pl.ds(out + step * rows_own, rows_own), :] = jnp.where(
                ids < live, rows, 0.0
            ).astype(jnp.bfloat16)
    adapter = adapter_ref[...]
    slot = jnp.zeros_like(adapter)
    rank = jnp.zeros_like(adapter)
    for a in range(owner_ref.shape[0]):
        hit = adapter == a
        slot = jnp.where(hit, owner_ref[a], slot)
        rank = jnp.where(hit, lax.shift_left(RMIN, bucket_ref[a]), rank)
    slot_row = slot.astype(jnp.float32)
    rank_row = rank.astype(jnp.float32)
    down = lax.broadcasted_iota(jnp.int32, (tokens, tokens), 0)
    across = lax.broadcasted_iota(jnp.int32, (tokens, tokens), 1)
    diagonal = down == across
    slot_col = jnp.sum(jnp.where(diagonal, slot_row, 0.0), axis=1, keepdims=True)
    rank_col = jnp.sum(jnp.where(diagonal, rank_row, 0.0), axis=1, keepdims=True)
    earlier = jnp.where((slot_col == slot_row) & (down < across), 1.0, 0.0)
    place = slot_row * CAP + jnp.sum(earlier, axis=0, keepdims=True)
    place_ref[...] = place.astype(jnp.int32)
    lanes = factor_ref.shape[1]
    slot_wide = jnp.broadcast_to(slot_col, (tokens, lanes))
    slot_ref[...] = slot_wide
    kept = lax.broadcasted_iota(jnp.int32, (tokens, lanes), 1) % PADDED_RANK
    factor_ref[...] = jnp.where(
        kept.astype(jnp.float32) < rank_col, adapter_alpha_scale / rank_col, 0.0
    )
    chunk = 256
    acc = jnp.zeros((tokens, chunk), jnp.float32)
    for c in range(up_ref.shape[0] // chunk):
        part = dot(masked, up_ref[pl.ds(c * chunk, chunk), :], NT)
        hit = slot_col == lane_slot((1, chunk), c * chunk // PADDED_RANK)
        acc = acc + jnp.where(hit, part, 0.0)
    acc = acc[:, :128] + acc[:, 128:]
    up_own_ref[...] = acc[:, :PADDED_RANK] + acc[:, PADDED_RANK:]


def prep(rows_own, live, bucket, owner, adapter_row, cotangent, up_factors):
    tokens, kv = cotangent.shape
    shapes = (
        jax.ShapeDtypeStruct((tokens, kv), jnp.bfloat16),
        jax.ShapeDtypeStruct((tokens, kv), jnp.bfloat16),
        jax.ShapeDtypeStruct((tokens, 128), jnp.float32),
        jax.ShapeDtypeStruct((tokens, 128), jnp.float32),
        jax.ShapeDtypeStruct((1, tokens), jnp.int32),
        jax.ShapeDtypeStruct((tokens, PADDED_RANK), jnp.float32),
    )
    return call(
        functools.partial(prep_kernel, rows_own),
        shapes,
        2 * tokens * kv * up_factors.shape[0],
        up_factors.size * 2,
        in_specs=[SMEM_SPEC] * 3 + [VMEM_SPEC] * 3,
        out_specs=(VMEM_SPEC,) * len(shapes),
        name="prep",
    )(live, bucket, owner, adapter_row, cotangent, up_factors)


def frozen_kernel(turned_ref, frozen_ref, *theirs_refs):
    half, part_width = theirs_refs[0].shape
    chunk = 512
    for first in range(0, frozen_ref.shape[0], chunk):
        at = first % part_width
        theirs_refs[first // part_width][:, at : at + chunk] = dot(
            turned_ref[half:, :], frozen_ref[first : first + chunk, :], NT
        )


def frozen_term(turned, frozen, parts):
    tokens, kv = turned.shape
    width = frozen.shape[0]
    return call(
        frozen_kernel,
        (jax.ShapeDtypeStruct((tokens // 2, width // parts), jnp.float32),) * parts,
        tokens * kv * width,
        2 * kv * width + 2 * tokens * width,
        in_specs=[VMEM_SPEC] * 2,
        out_specs=(VMEM_SPEC,) * parts,
        name="frozen_term",
    )(turned, frozen)


def pack_kernel(place_ref, *refs):
    parts, out_ref = refs[:-1], refs[-1]
    rows, tokens = out_ref.shape[0], place_ref.shape[1]
    down = lax.broadcasted_iota(jnp.int32, (rows, tokens), 0)
    pick = jnp.where(down == place_ref[...], 1.0, 0.0).astype(jnp.bfloat16)
    first = 0
    for part in parts:
        width = part.shape[1]
        out_ref[:, first : first + width] = dot(pick, part[...], NN).astype(jnp.bfloat16)
        first += width


def pack_rows(place, parts, rows):
    tokens, columns = place.shape[1], sum(v.shape[1] for v in parts)
    return call(
        pack_kernel,
        jax.ShapeDtypeStruct((rows, columns), jnp.bfloat16),
        2 * rows * columns * tokens,
        2 * (rows + tokens) * columns,
        in_specs=[VMEM_SPEC] * (len(parts) + 1),
        out_specs=VMEM_SPEC,
        name="pack",
    )(place, *parts)


CHUNK = 256
PARTS = 4


def down_kernel(hidden_ref, slot_ref, up_own_ref, factors_ref, out_ref):
    slot = slot_ref[...]
    acc = jnp.zeros(slot.shape, jnp.float32)
    for first in range(0, factors_ref.shape[1], CHUNK):
        product = dot(hidden_ref[...], factors_ref[:, first : first + CHUNK], NN)
        for d in range(0, CHUNK, 128):
            hit = slot == lane_slot((1, 128), (first + d) // PADDED_RANK)
            acc = acc + jnp.where(hit, product[:, d : d + 128], 0.0)
    out_ref[:, :PADDED_RANK] = acc[:, :PADDED_RANK] + acc[:, PADDED_RANK:]
    out_ref[:, PADDED_RANK:] = up_own_ref[...]


def low_rank(hidden_columns, slot_wide, up_own, factors):
    tokens = hidden_columns.shape[0]
    return call(
        down_kernel,
        jax.ShapeDtypeStruct((tokens, 2 * PADDED_RANK), jnp.float32),
        2 * tokens * factors.size,
        2 * factors.size,
        in_specs=[VMEM_SPEC] * 4,
        out_specs=VMEM_SPEC,
        name="low_rank",
    )(hidden_columns, slot_wide, up_own, factors)


def extra_kernel(rows_own, weight_ref, slot_ref, factors_ref, ours_ref, theirs_ref, extra_ref):
    tokens = weight_ref.shape[0]
    n_chip = tokens // rows_own // 2
    slot = slot_ref[...]
    weight = weight_ref[:, PADDED_RANK:].astype(jnp.float32)
    double = jnp.concatenate([weight, weight], axis=1)
    for first in range(0, factors_ref.shape[1], CHUNK):
        pieces = []
        for d in range(0, CHUNK, 128):
            hit = slot == lane_slot((1, 128), (first + d) // PADDED_RANK)
            pieces.append(jnp.where(hit, double, 0.0).astype(jnp.bfloat16))
        placed = jnp.concatenate(pieces, axis=1)
        term = dot(placed, factors_ref[:, first : first + CHUNK], NT)
        if first == 0:
            extra_ref[...] = term
        else:
            extra_ref[...] += term
    position = lax.axis_index("tensor")
    chip, core = position // 2, position % 2
    for turn in range(n_chip):
        block = (chip + turn) % n_chip * 2
        for out, k in ((ours_ref, core), (theirs_ref, 1 - core)):
            start = pl.multiple_of((block + k) * rows_own, rows_own)
            out[pl.ds(turn * rows_own, rows_own), :] = extra_ref[pl.ds(start, rows_own), :]


def extra_term(rows_own, weights, slot_wide, factors):
    tokens, columns = weights.shape[0], factors.shape[0]
    half = jax.ShapeDtypeStruct((tokens // 2, columns), jnp.float32)
    return call(
        functools.partial(extra_kernel, rows_own),
        (half, half),
        2 * tokens * factors.size,
        2 * factors.size,
        in_specs=[VMEM_SPEC] * 3,
        out_specs=(VMEM_SPEC,) * 2,
        scratch_shapes=[pltpu.VMEM((tokens, columns), jnp.float32)],
        name="extra_term",
    )(weights, slot_wide, factors)


def pair_kernel(rows_own, turned_ref, frozen_ref, *refs):
    half, part_width = refs[0].shape
    width = frozen_ref.shape[0]
    parts = width // part_width
    pair_refs, outs = refs[:parts], refs[parts:]
    chunk = 512
    for first in range(0, width, chunk):
        at = slice(first, first + chunk)
        inner = first % part_width
        total = dot(turned_ref[:half, :], frozen_ref[at, :], NT)
        total = total + pair_refs[first // part_width][:, inner : inner + chunk]
        outs[0][:, at] = total[:rows_own, :]
        for i, out in enumerate(outs[1:], 1):
            out[:, at] = total[i * rows_own : (i + 1) * rows_own, :].astype(jnp.bfloat16)


def pair_sum(rows_own, turned, frozen, from_pair):
    half = from_pair[0].shape[0]
    width, kv = frozen.shape
    sent = jax.ShapeDtypeStruct((rows_own, width), jnp.bfloat16)
    n_out = half // rows_own - 1
    return call(
        functools.partial(pair_kernel, rows_own),
        (jax.ShapeDtypeStruct((rows_own, width), jnp.float32),) + (sent,) * n_out,
        2 * half * width * kv,
        2 * kv * width + 6 * half * width,
        in_specs=[VMEM_SPEC] * (2 + len(from_pair)),
        out_specs=(VMEM_SPEC,) * (n_out + 1),
        name="pair_sum",
    )(turned, frozen, *from_pair)


def last_kernel(*refs):
    count = (len(refs) - 1) // 2
    frozen_refs, extra_refs, out_ref = refs[:count], refs[count:-1], refs[-1]
    columns = extra_refs[0].shape[1]
    chip = lax.axis_index("tensor") // 2
    for step, extra_ref in enumerate(extra_refs):
        block = (chip + count - step) % count
        at = pl.ds(pl.multiple_of(block * columns, columns), columns)
        total = extra_ref[...].astype(jnp.float32)
        for frozen_ref in frozen_refs:
            total = total + frozen_ref[:, at].astype(jnp.float32)
        out_ref[:, at] = total.astype(jnp.bfloat16)


def last_sum(frozen_terms, extra_terms):
    size = frozen_terms[0].size
    values = [*frozen_terms, *extra_terms]
    return call(
        last_kernel,
        jax.ShapeDtypeStruct(frozen_terms[0].shape, jnp.bfloat16),
        5 * size,
        16 * size,
        in_specs=[VMEM_SPEC] * len(values),
        out_specs=VMEM_SPEC,
        name="last_sum",
    )(*values)


def local(
    hidden,
    cotangent,
    frozen_key_value,
    adapter_down_factors,
    adapter_up_factors,
    down_master_copy,
    down_first_moment,
    down_second_moment,
    up_master_copy,
    up_first_moment,
    up_second_moment,
    adapter_of_token,
    adapter_rank_bucket,
    adapter_owner_slot,
    live_token_counts,
):
    n_tensor = lax.axis_size("tensor")
    n_chip = n_tensor // 2
    tokens = cotangent.shape[0]
    rows_own, width = hidden.shape
    columns = width // n_tensor
    n_slot = adapter_owner_slot.shape[0]

    blocks = hidden.reshape(rows_own, n_tensor, columns).transpose(1, 0, 2)
    hidden_columns = lax.all_to_all(blocks, "tensor", 0, 0, tiled=True).reshape(tokens, columns)

    masked, turned, slot_wide, factor_wide, place, up_own = prep(
        rows_own,
        live_token_counts,
        adapter_rank_bucket,
        adapter_owner_slot,
        adapter_of_token.reshape(1, tokens),
        cotangent,
        adapter_up_factors,
    )

    turned, hidden_columns = lax.optimization_barrier((turned, hidden_columns))
    frozen_theirs = frozen_term(turned, frozen_key_value, PARTS)

    own = low_rank(hidden_columns, slot_wide, up_own, adapter_down_factors)
    own = own + swap(own, 1, n_tensor)
    own, frozen_theirs = lax.optimization_barrier((own, frozen_theirs))
    weights = (sum_over_chips(own, n_tensor) * factor_wide).astype(jnp.bfloat16)

    from_pair = [swap(theirs, 1, n_tensor) for theirs in frozen_theirs]
    total, *sent = pair_sum(rows_own, turned, frozen_key_value, from_pair)

    packed = pack_rows(place, [hidden_columns, masked, weights], n_slot * CAP)
    packed, weights = lax.optimization_barrier((packed, weights))
    weights, total, sent = lax.optimization_barrier((weights, total, sent))
    owned = lax.all_to_all(
        packed.reshape(n_slot, CAP, -1), "dp", 0, 0, tiled=True
    ).reshape(n_slot * CAP, -1)

    def to_chips(sent):
        return [
            lax.ppermute(
                value, "tensor", [(i, (i + 2 * step) % n_tensor) for i in range(n_tensor)]
            )
            for step, value in enumerate(sent, 1)
        ]

    arrived = to_chips(sent)
    extra_ours, extra_theirs = extra_term(rows_own, weights, slot_wide, adapter_down_factors)
    extra_pair = swap(extra_theirs, 1, n_tensor)
    low_core = lax.axis_index("tensor") % 2 == 0
    extra = jnp.concatenate(
        [
            jnp.where(low_core, extra_ours, extra_pair),
            jnp.where(low_core, extra_pair, extra_ours),
        ],
        axis=1,
    ).reshape(n_chip, rows_own, 2 * columns)
    extra_sent = extra[1:].astype(jnp.bfloat16)
    extra_arrived = to_chips([extra_sent[i] for i in range(n_chip - 1)])
    hidden_gradient = last_sum([total, *arrived], [extra[0], *extra_arrived])

    kv = cotangent.shape[1]
    owned_hidden, owned_cot = owned[:, :columns], owned[:, columns : columns + kv]
    owned_down = owned[:, columns + kv : columns + kv + PADDED_RANK]
    owned_up = owned[:, columns + kv + PADDED_RANK :]
    grad_down = contract_helper(owned_hidden, owned_up, 0, 0) / tokens
    grad_up = contract_helper(owned_down, owned_cot, 0, 0) / tokens
    new_dm, new_dmo, new_ds = adamw(
        down_master_copy, down_first_moment, down_second_moment, grad_down
    )
    new_um, new_umo, new_us = adamw(up_master_copy, up_first_moment, up_second_moment, grad_up)
    return (hidden_gradient, new_dm, new_dmo, new_ds, new_um, new_umo, new_us)


def solution(mesh):
    return jax.shard_map(
        local,
        mesh=mesh,
        in_specs=(
            P(("dp", "tensor"), None),
            P("dp", "tensor"),
            P(None, "tensor"),
            P("tensor", None),
            P(None, "tensor"),
            P("tensor", "dp"),
            P("tensor", "dp"),
            P("tensor", "dp"),
            P("dp", "tensor"),
            P("dp", "tensor"),
            P("dp", "tensor"),
            P("dp", None),
            P(),
            P(),
            P(),
        ),
        out_specs=(
            P(("dp", "tensor"), None),
            P("tensor", "dp"),
            P("tensor", "dp"),
            P("tensor", "dp"),
            P("dp", "tensor"),
            P("dp", "tensor"),
            P("dp", "tensor"),
        ),
        check_vma=False,
    )
```

```python
import functools

import jax
import jax.numpy as jnp
from jax import lax
from jax.experimental import pallas as pl
from jax.experimental.pallas import tpu as pltpu
from jax.sharding import PartitionSpec as P

RMIN = 8
PADDED_RANK = 64
CAP = 16


adapter_alpha_scale = 16.0
beta_one = 0.9
beta_two = 0.999
adam_eps = 1e-08
learn_rate = 0.0002
weight_decay = 0.1
first_fix = 0.9999734386011124
second_fix = 0.09520785288629038


def adamw(master, moment, second, grad):
    new_moment = beta_one * moment + (1.0 - beta_one) * grad
    new_second = beta_two * second + (1.0 - beta_two) * grad * grad
    update = new_moment / first_fix / (jnp.sqrt(new_second / second_fix) + adam_eps)
    new_master = master - learn_rate * (update + weight_decay * master)
    return (new_master, new_moment, new_second)


def contract_helper(left, right, left_dim, right_dim):
    return lax.dot_general(
        left, right, (((left_dim,), (right_dim,)), ((), ())), preferred_element_type=jnp.float32
    )


def swap(value, mask, count):
    return lax.ppermute(value, "tensor", [(i, i ^ mask) for i in range(count)])


def sum_over_chips(value, count):
    near = value + swap(value, 2, count)
    far = swap(value, 4, count) + swap(value, 6, count)
    return near + far


VMEM_LIMIT = 16 * 1024 * 1024
SMEM_SPEC = pl.BlockSpec(memory_space=pltpu.MemorySpace.SMEM)
VMEM_SPEC = pl.BlockSpec(memory_space=pltpu.MemorySpace.VMEM)
NT = (((1,), (1,)), ((), ()))
NN = (((1,), (0,)), ((), ()))


def call(kernel, out_shape, flops, moved, **options):
    return pl.pallas_call(
        kernel,
        out_shape=out_shape,
        compiler_params=pltpu.CompilerParams(vmem_limit_bytes=VMEM_LIMIT),
        cost_estimate=pl.CostEstimate(flops=flops, bytes_accessed=moved, transcendentals=0),
        **options,
    )


def dot(left, right, dims):
    return lax.dot_general(left, right, dims, preferred_element_type=jnp.float32)


def lane_slot(shape, first):
    return (lax.broadcasted_iota(jnp.int32, shape, 1) // PADDED_RANK + first).astype(jnp.float32)


def prep_kernel(rows_own, live_ref, bucket_ref, owner_ref, adapter_ref, cot_ref, up_ref,
                masked_ref, ours_ref, theirs_ref, slot_ref, factor_ref, place_ref, up_own_ref):
    tokens = cot_ref.shape[0]
    n_chip = tokens // rows_own // 2
    position = lax.axis_index("tensor")
    chip, core = position // 2, position % 2
    live = live_ref[lax.axis_index("dp")]
    token = lax.broadcasted_iota(jnp.int32, (tokens, 1), 0)
    masked = jnp.where(token < live, cot_ref[...].astype(jnp.float32), 0.0).astype(jnp.bfloat16)
    masked_ref[...] = masked
    for step in range(n_chip):
        block = (chip + step) % n_chip * 2
        for out, k in ((ours_ref, core), (theirs_ref, 1 - core)):
            start = pl.multiple_of((block + k) * rows_own, rows_own)
            ids = start + lax.broadcasted_iota(jnp.int32, (rows_own, 1), 0)
            rows = cot_ref[pl.ds(start, rows_own), :].astype(jnp.float32)
            out[pl.ds(step * rows_own, rows_own), :] = jnp.where(ids < live, rows, 0.0).astype(
                jnp.bfloat16
            )
    adapter = adapter_ref[...]
    slot = jnp.zeros_like(adapter)
    rank = jnp.zeros_like(adapter)
    for a in range(owner_ref.shape[0]):
        hit = adapter == a
        slot = jnp.where(hit, owner_ref[a], slot)
        rank = jnp.where(hit, lax.shift_left(RMIN, bucket_ref[a]), rank)
    slot_row = slot.astype(jnp.float32)
    rank_row = rank.astype(jnp.float32)
    down = lax.broadcasted_iota(jnp.int32, (tokens, tokens), 0)
    across = lax.broadcasted_iota(jnp.int32, (tokens, tokens), 1)
    diagonal = down == across
    slot_col = jnp.sum(jnp.where(diagonal, slot_row, 0.0), axis=1, keepdims=True)
    rank_col = jnp.sum(jnp.where(diagonal, rank_row, 0.0), axis=1, keepdims=True)
    earlier = jnp.where((slot_col == slot_row) & (down < across), 1.0, 0.0)
    place = slot_row * CAP + jnp.sum(earlier, axis=0, keepdims=True)
    place_ref[...] = place.astype(jnp.int32)
    lanes = factor_ref.shape[1]
    slot_wide = jnp.broadcast_to(slot_col, (tokens, lanes))
    slot_ref[...] = slot_wide
    kept = lax.broadcasted_iota(jnp.int32, (tokens, lanes), 1) % PADDED_RANK
    factor_ref[...] = jnp.where(
        kept.astype(jnp.float32) < rank_col, adapter_alpha_scale / rank_col, 0.0
    )
    chunk = 256
    acc = jnp.zeros((tokens, chunk), jnp.float32)
    for c in range(up_ref.shape[0] // chunk):
        part = dot(masked, up_ref[pl.ds(c * chunk, chunk), :], NT)
        hit = slot_col == lane_slot((1, chunk), c * chunk // PADDED_RANK)
        acc = acc + jnp.where(hit, part, 0.0)
    acc = acc[:, :128] + acc[:, 128:]
    up_own_ref[...] = acc[:, :PADDED_RANK] + acc[:, PADDED_RANK:]


def prep(rows_own, live, bucket, owner, adapter_row, cotangent, up_factors):
    tokens, kv = cotangent.shape
    shapes = (
        jax.ShapeDtypeStruct((tokens, kv), jnp.bfloat16),
        jax.ShapeDtypeStruct((tokens // 2, kv), jnp.bfloat16),
        jax.ShapeDtypeStruct((tokens // 2, kv), jnp.bfloat16),
        jax.ShapeDtypeStruct((tokens, 128), jnp.float32),
        jax.ShapeDtypeStruct((tokens, 128), jnp.float32),
        jax.ShapeDtypeStruct((1, tokens), jnp.int32),
        jax.ShapeDtypeStruct((tokens, PADDED_RANK), jnp.float32),
    )
    return call(
        functools.partial(prep_kernel, rows_own),
        shapes,
        2 * tokens * kv * up_factors.shape[0],
        up_factors.size * 2,
        in_specs=[SMEM_SPEC] * 3 + [VMEM_SPEC] * 3,
        out_specs=(VMEM_SPEC,) * len(shapes),
        name="prep",
    )(live, bucket, owner, adapter_row, cotangent, up_factors)


def pack_kernel(place_ref, *refs):
    parts, out_ref = refs[:-1], refs[-1]
    rows, tokens = out_ref.shape[0], place_ref.shape[1]
    down = lax.broadcasted_iota(jnp.int32, (rows, tokens), 0)
    pick = jnp.where(down == place_ref[...], 1.0, 0.0).astype(jnp.bfloat16)
    first = 0
    for part in parts:
        width = part.shape[1]
        out_ref[:, first : first + width] = dot(pick, part[...], NN).astype(jnp.bfloat16)
        first += width


def pack_rows(place, parts, rows):
    tokens, columns = place.shape[1], sum(v.shape[1] for v in parts)
    return call(
        pack_kernel,
        jax.ShapeDtypeStruct((rows, columns), jnp.bfloat16),
        2 * rows * columns * tokens,
        2 * (rows + tokens) * columns,
        in_specs=[VMEM_SPEC] * (len(parts) + 1),
        out_specs=VMEM_SPEC,
        name="pack",
    )(place, *parts)


CHUNK = 256


def down_kernel(hidden_ref, slot_ref, up_own_ref, factors_ref, out_ref):
    slot = slot_ref[...]
    acc = jnp.zeros(slot.shape, jnp.float32)
    for first in range(0, factors_ref.shape[1], CHUNK):
        product = dot(hidden_ref[...], factors_ref[:, first : first + CHUNK], NN)
        for d in range(0, CHUNK, 128):
            hit = slot == lane_slot((1, 128), (first + d) // PADDED_RANK)
            acc = acc + jnp.where(hit, product[:, d : d + 128], 0.0)
    out_ref[:, :PADDED_RANK] = acc[:, :PADDED_RANK] + acc[:, PADDED_RANK:]
    out_ref[:, PADDED_RANK:] = up_own_ref[...]


def low_rank(hidden_columns, slot_wide, up_own, factors):
    tokens = hidden_columns.shape[0]
    return call(
        down_kernel,
        jax.ShapeDtypeStruct((tokens, 2 * PADDED_RANK), jnp.float32),
        2 * tokens * factors.size,
        2 * factors.size,
        in_specs=[VMEM_SPEC] * 4,
        out_specs=VMEM_SPEC,
        name="low_rank",
    )(hidden_columns, slot_wide, up_own, factors)


def extra_kernel(rows_own, weight_ref, slot_ref, factors_ref, ours_ref, theirs_ref, extra_ref):
    tokens = weight_ref.shape[0]
    n_chip = tokens // rows_own // 2
    slot = slot_ref[...]
    weight = weight_ref[:, PADDED_RANK:].astype(jnp.float32)
    double = jnp.concatenate([weight, weight], axis=1)
    for first in range(0, factors_ref.shape[1], CHUNK):
        pieces = []
        for d in range(0, CHUNK, 128):
            hit = slot == lane_slot((1, 128), (first + d) // PADDED_RANK)
            pieces.append(jnp.where(hit, double, 0.0).astype(jnp.bfloat16))
        placed = jnp.concatenate(pieces, axis=1)
        term = dot(placed, factors_ref[:, first : first + CHUNK], NT)
        if first == 0:
            extra_ref[...] = term
        else:
            extra_ref[...] += term
    position = lax.axis_index("tensor")
    chip, core = position // 2, position % 2
    for turn in range(n_chip):
        block = (chip + turn) % n_chip * 2
        for out, k in ((ours_ref, core), (theirs_ref, 1 - core)):
            start = pl.multiple_of((block + k) * rows_own, rows_own)
            out[pl.ds(turn * rows_own, rows_own), :] = extra_ref[pl.ds(start, rows_own), :]


def extra_term(rows_own, weights, slot_wide, factors):
    tokens, columns = weights.shape[0], factors.shape[0]
    half = jax.ShapeDtypeStruct((tokens // 2, columns), jnp.float32)
    return call(
        functools.partial(extra_kernel, rows_own),
        (half, half),
        2 * tokens * factors.size,
        2 * factors.size,
        in_specs=[VMEM_SPEC] * 3,
        out_specs=(VMEM_SPEC,) * 2,
        scratch_shapes=[pltpu.VMEM((tokens, columns), jnp.float32)],
        name="extra_term",
    )(weights, slot_wide, factors)


def pair_kernel(rows_own, rows_ref, pair_rows_ref, extra_ref, extra_pair_ref, frozen_ref,
                pair_frozen_ref, *outs):
    width = frozen_ref.shape[0]
    columns = extra_ref.shape[1]
    position = lax.axis_index("tensor")
    chip, core = position // 2, position % 2
    low = jnp.where(core == 0, extra_ref[...], extra_pair_ref[...])
    high = jnp.where(core == 0, extra_pair_ref[...], extra_ref[...])
    for block in range(width // columns):
        at = slice(block * columns, (block + 1) * columns)
        total = dot(rows_ref[...], frozen_ref[at, :], NT)
        total = total + dot(pair_rows_ref[...], pair_frozen_ref[at, :], NT)
        extra = low if block % 2 == 0 else high
        total = total + jnp.where(chip == block // 2, extra, 0.0)
        outs[0][:, at] = total[:rows_own, :]
        for i, out in enumerate(outs[1:], 1):
            out[:, at] = total[i * rows_own : (i + 1) * rows_own, :].astype(jnp.bfloat16)


def pair_sum(rows_own, rows, pair_rows, extra, extra_pair, frozen, pair_frozen):
    half, kv = rows.shape
    width = frozen.shape[0]
    sent = jax.ShapeDtypeStruct((rows_own, width), jnp.bfloat16)
    n_out = half // rows_own - 1
    return call(
        functools.partial(pair_kernel, rows_own),
        (jax.ShapeDtypeStruct((rows_own, width), jnp.float32),) + (sent,) * n_out,
        4 * half * width * kv,
        4 * kv * width + 4 * half * width,
        in_specs=[VMEM_SPEC] * 6,
        out_specs=(VMEM_SPEC,) * (n_out + 1),
        name="pair_sum",
    )(rows, pair_rows, extra, extra_pair, frozen, pair_frozen)


def local(
    hidden,
    cotangent,
    frozen_key_value,
    adapter_down_factors,
    adapter_up_factors,
    down_master_copy,
    down_first_moment,
    down_second_moment,
    up_master_copy,
    up_first_moment,
    up_second_moment,
    adapter_of_token,
    adapter_rank_bucket,
    adapter_owner_slot,
    live_token_counts,
):
    n_tensor = lax.axis_size("tensor")
    n_chip = n_tensor // 2
    tokens = cotangent.shape[0]
    rows_own, width = hidden.shape
    columns = width // n_tensor
    n_slot = adapter_owner_slot.shape[0]

    blocks = hidden.reshape(rows_own, n_tensor, columns).transpose(1, 0, 2)
    hidden_columns = lax.all_to_all(blocks, "tensor", 0, 0, tiled=True).reshape(tokens, columns)

    masked, rows, pair_rows, slot_wide, factor_wide, place, up_own = prep(
        rows_own,
        live_token_counts,
        adapter_rank_bucket,
        adapter_owner_slot,
        adapter_of_token.reshape(1, tokens),
        cotangent,
        adapter_up_factors,
    )

    pair_rows = swap(pair_rows, 1, n_tensor)
    pair_frozen = swap(frozen_key_value, 1, n_tensor)

    own = low_rank(hidden_columns, slot_wide, up_own, adapter_down_factors)
    own = own + swap(own, 1, n_tensor)
    weights = (sum_over_chips(own, n_tensor) * factor_wide).astype(jnp.bfloat16)
    extra_ours, extra_theirs = extra_term(rows_own, weights, slot_wide, adapter_down_factors)
    weights, extra_ours, extra_theirs = lax.optimization_barrier(
        (weights, extra_ours, extra_theirs)
    )

    packed = pack_rows(place, [hidden_columns, masked, weights], n_slot * CAP)
    owned = lax.all_to_all(
        packed.reshape(n_slot, CAP, -1), "dp", 0, 0, tiled=True
    ).reshape(n_slot * CAP, -1)

    total, *sent = pair_sum(
        rows_own,
        rows,
        pair_rows,
        extra_ours,
        swap(extra_theirs, 1, n_tensor),
        frozen_key_value,
        pair_frozen,
    )
    for step, value in enumerate(sent, 1):
        arrived = lax.ppermute(
            value, "tensor", [(i, (i + 2 * step) % n_tensor) for i in range(n_tensor)]
        )
        total = total + arrived.astype(jnp.float32)
    hidden_gradient = total.astype(jnp.bfloat16)

    kv = cotangent.shape[1]
    owned_hidden, owned_cot = owned[:, :columns], owned[:, columns : columns + kv]
    owned_down = owned[:, columns + kv : columns + kv + PADDED_RANK]
    owned_up = owned[:, columns + kv + PADDED_RANK :]
    grad_down = contract_helper(owned_hidden, owned_up, 0, 0) / tokens
    grad_up = contract_helper(owned_down, owned_cot, 0, 0) / tokens
    new_dm, new_dmo, new_ds = adamw(
        down_master_copy, down_first_moment, down_second_moment, grad_down
    )
    new_um, new_umo, new_us = adamw(up_master_copy, up_first_moment, up_second_moment, grad_up)
    return (hidden_gradient, new_dm, new_dmo, new_ds, new_um, new_umo, new_us)


def solution(mesh):
    return jax.shard_map(
        local,
        mesh=mesh,
        in_specs=(
            P(("dp", "tensor"), None),
            P("dp", "tensor"),
            P(None, "tensor"),
            P("tensor", None),
            P(None, "tensor"),
            P("tensor", "dp"),
            P("tensor", "dp"),
            P("tensor", "dp"),
            P("dp", "tensor"),
            P("dp", "tensor"),
            P("dp", "tensor"),
            P("dp", None),
            P(),
            P(),
            P(),
        ),
        out_specs=(
            P(("dp", "tensor"), None),
            P("tensor", "dp"),
            P("tensor", "dp"),
            P("tensor", "dp"),
            P("dp", "tensor"),
            P("dp", "tensor"),
            P("dp", "tensor"),
        ),
        check_vma=False,
    )
```

```python
import functools

import jax
import jax.numpy as jnp
from jax import lax
from jax.experimental import pallas as pl
from jax.experimental.pallas import tpu as pltpu
from jax.sharding import PartitionSpec as P

RMIN = 8
PADDED_RANK = 64
CAP = 16


adapter_alpha_scale = 16.0
beta_one = 0.9
beta_two = 0.999
adam_eps = 1e-08
learn_rate = 0.0002
weight_decay = 0.1
first_fix = 0.9999734386011124
second_fix = 0.09520785288629038


def adamw(master, moment, second, grad):
    new_moment = beta_one * moment + (1.0 - beta_one) * grad
    new_second = beta_two * second + (1.0 - beta_two) * grad * grad
    update = new_moment / first_fix / (jnp.sqrt(new_second / second_fix) + adam_eps)
    new_master = master - learn_rate * (update + weight_decay * master)
    return (new_master, new_moment, new_second)


def contract_helper(left, right, left_dim, right_dim):
    return lax.dot_general(
        left, right, (((left_dim,), (right_dim,)), ((), ())), preferred_element_type=jnp.float32
    )


def swap(value, mask, count):
    return lax.ppermute(value, "tensor", [(i, i ^ mask) for i in range(count)])


def sum_over_chips(value, count):
    near = value + swap(value, 2, count)
    far = swap(value, 4, count) + swap(value, 6, count)
    return near + far


VMEM_LIMIT = 16 * 1024 * 1024
SMEM_SPEC = pl.BlockSpec(memory_space=pltpu.MemorySpace.SMEM)
VMEM_SPEC = pl.BlockSpec(memory_space=pltpu.MemorySpace.VMEM)
NT = (((1,), (1,)), ((), ()))
NN = (((1,), (0,)), ((), ()))


def call(kernel, out_shape, flops, moved, **options):
    return pl.pallas_call(
        kernel,
        out_shape=out_shape,
        compiler_params=pltpu.CompilerParams(vmem_limit_bytes=VMEM_LIMIT),
        cost_estimate=pl.CostEstimate(flops=flops, bytes_accessed=moved, transcendentals=0),
        **options,
    )


def dot(left, right, dims):
    return lax.dot_general(left, right, dims, preferred_element_type=jnp.float32)


def lane_slot(shape, first):
    return (lax.broadcasted_iota(jnp.int32, shape, 1) // PADDED_RANK + first).astype(jnp.float32)


def prep_kernel(rows_own, live_ref, bucket_ref, owner_ref, adapter_ref, cot_ref, up_ref,
                masked_ref, ours_ref, theirs_ref, slot_ref, factor_ref, place_ref, up_own_ref):
    tokens = cot_ref.shape[0]
    n_chip = tokens // rows_own // 2
    position = lax.axis_index("tensor")
    chip, core = position // 2, position % 2
    live = live_ref[lax.axis_index("dp")]
    token = lax.broadcasted_iota(jnp.int32, (tokens, 1), 0)
    masked = jnp.where(token < live, cot_ref[...].astype(jnp.float32), 0.0).astype(jnp.bfloat16)
    masked_ref[...] = masked
    for step in range(n_chip):
        block = (chip + step) % n_chip * 2
        for out, k in ((ours_ref, core), (theirs_ref, 1 - core)):
            start = pl.multiple_of((block + k) * rows_own, rows_own)
            ids = start + lax.broadcasted_iota(jnp.int32, (rows_own, 1), 0)
            rows = cot_ref[pl.ds(start, rows_own), :].astype(jnp.float32)
            out[pl.ds(step * rows_own, rows_own), :] = jnp.where(ids < live, rows, 0.0).astype(
                jnp.bfloat16
            )
    adapter = adapter_ref[...]
    slot = jnp.zeros_like(adapter)
    rank = jnp.zeros_like(adapter)
    for a in range(owner_ref.shape[0]):
        hit = adapter == a
        slot = jnp.where(hit, owner_ref[a], slot)
        rank = jnp.where(hit, lax.shift_left(RMIN, bucket_ref[a]), rank)
    slot_row = slot.astype(jnp.float32)
    rank_row = rank.astype(jnp.float32)
    down = lax.broadcasted_iota(jnp.int32, (tokens, tokens), 0)
    across = lax.broadcasted_iota(jnp.int32, (tokens, tokens), 1)
    diagonal = down == across
    slot_col = jnp.sum(jnp.where(diagonal, slot_row, 0.0), axis=1, keepdims=True)
    rank_col = jnp.sum(jnp.where(diagonal, rank_row, 0.0), axis=1, keepdims=True)
    earlier = jnp.where((slot_col == slot_row) & (down < across), 1.0, 0.0)
    place = slot_row * CAP + jnp.sum(earlier, axis=0, keepdims=True)
    place_ref[...] = place.astype(jnp.int32)
    lanes = factor_ref.shape[1]
    slot_wide = jnp.broadcast_to(slot_col, (tokens, lanes))
    slot_ref[...] = slot_wide
    kept = lax.broadcasted_iota(jnp.int32, (tokens, lanes), 1) % PADDED_RANK
    factor_ref[...] = jnp.where(
        kept.astype(jnp.float32) < rank_col, adapter_alpha_scale / rank_col, 0.0
    )
    chunk = 256
    acc = jnp.zeros((tokens, chunk), jnp.float32)
    for c in range(up_ref.shape[0] // chunk):
        part = dot(masked, up_ref[pl.ds(c * chunk, chunk), :], NT)
        hit = slot_col == lane_slot((1, chunk), c * chunk // PADDED_RANK)
        acc = acc + jnp.where(hit, part, 0.0)
    acc = acc[:, :128] + acc[:, 128:]
    up_own_ref[...] = acc[:, :PADDED_RANK] + acc[:, PADDED_RANK:]


def prep(rows_own, live, bucket, owner, adapter_row, cotangent, up_factors):
    tokens, kv = cotangent.shape
    shapes = (
        jax.ShapeDtypeStruct((tokens, kv), jnp.bfloat16),
        jax.ShapeDtypeStruct((tokens // 2, kv), jnp.bfloat16),
        jax.ShapeDtypeStruct((tokens // 2, kv), jnp.bfloat16),
        jax.ShapeDtypeStruct((tokens, 128), jnp.float32),
        jax.ShapeDtypeStruct((tokens, 128), jnp.float32),
        jax.ShapeDtypeStruct((1, tokens), jnp.int32),
        jax.ShapeDtypeStruct((tokens, PADDED_RANK), jnp.float32),
    )
    return call(
        functools.partial(prep_kernel, rows_own),
        shapes,
        2 * tokens * kv * up_factors.shape[0],
        up_factors.size * 2,
        in_specs=[SMEM_SPEC] * 3 + [VMEM_SPEC] * 3,
        out_specs=(VMEM_SPEC,) * len(shapes),
        name="prep",
    )(live, bucket, owner, adapter_row, cotangent, up_factors)


def pack_kernel(place_ref, *refs):
    parts, out_ref = refs[:-1], refs[-1]
    rows, tokens = out_ref.shape[0], place_ref.shape[1]
    down = lax.broadcasted_iota(jnp.int32, (rows, tokens), 0)
    pick = jnp.where(down == place_ref[...], 1.0, 0.0).astype(jnp.bfloat16)
    first = 0
    for part in parts:
        width = part.shape[1]
        out_ref[:, first : first + width] = dot(pick, part[...], NN).astype(jnp.bfloat16)
        first += width


def pack_rows(place, parts, rows):
    tokens, columns = place.shape[1], sum(v.shape[1] for v in parts)
    return call(
        pack_kernel,
        jax.ShapeDtypeStruct((rows, columns), jnp.bfloat16),
        2 * rows * columns * tokens,
        2 * (rows + tokens) * columns,
        in_specs=[VMEM_SPEC] * (len(parts) + 1),
        out_specs=VMEM_SPEC,
        name="pack",
    )(place, *parts)


CHUNK = 256


def down_kernel(hidden_ref, slot_ref, up_own_ref, factors_ref, out_ref):
    slot = slot_ref[...]
    acc = jnp.zeros(slot.shape, jnp.float32)
    for first in range(0, factors_ref.shape[1], CHUNK):
        product = dot(hidden_ref[...], factors_ref[:, first : first + CHUNK], NN)
        for d in range(0, CHUNK, 128):
            hit = slot == lane_slot((1, 128), (first + d) // PADDED_RANK)
            acc = acc + jnp.where(hit, product[:, d : d + 128], 0.0)
    out_ref[:, :PADDED_RANK] = acc[:, :PADDED_RANK] + acc[:, PADDED_RANK:]
    out_ref[:, PADDED_RANK:] = up_own_ref[...]


def low_rank(hidden_columns, slot_wide, up_own, factors):
    tokens = hidden_columns.shape[0]
    return call(
        down_kernel,
        jax.ShapeDtypeStruct((tokens, 2 * PADDED_RANK), jnp.float32),
        2 * tokens * factors.size,
        2 * factors.size,
        in_specs=[VMEM_SPEC] * 4,
        out_specs=VMEM_SPEC,
        name="low_rank",
    )(hidden_columns, slot_wide, up_own, factors)


def extra_kernel(rows_own, weight_ref, slot_ref, factors_ref, ours_ref, theirs_ref, extra_ref):
    tokens = weight_ref.shape[0]
    n_chip = tokens // rows_own // 2
    slot = slot_ref[...]
    weight = weight_ref[:, PADDED_RANK:].astype(jnp.float32)
    double = jnp.concatenate([weight, weight], axis=1)
    for first in range(0, factors_ref.shape[1], CHUNK):
        pieces = []
        for d in range(0, CHUNK, 128):
            hit = slot == lane_slot((1, 128), (first + d) // PADDED_RANK)
            pieces.append(jnp.where(hit, double, 0.0).astype(jnp.bfloat16))
        placed = jnp.concatenate(pieces, axis=1)
        term = dot(placed, factors_ref[:, first : first + CHUNK], NT)
        if first == 0:
            extra_ref[...] = term
        else:
            extra_ref[...] += term
    position = lax.axis_index("tensor")
    chip, core = position // 2, position % 2
    for turn in range(n_chip):
        block = (chip + turn) % n_chip * 2
        for out, k in ((ours_ref, core), (theirs_ref, 1 - core)):
            start = pl.multiple_of((block + k) * rows_own, rows_own)
            out[pl.ds(turn * rows_own, rows_own), :] = extra_ref[pl.ds(start, rows_own), :]


def extra_term(rows_own, weights, slot_wide, factors):
    tokens, columns = weights.shape[0], factors.shape[0]
    half = jax.ShapeDtypeStruct((tokens // 2, columns), jnp.float32)
    return call(
        functools.partial(extra_kernel, rows_own),
        (half, half),
        2 * tokens * factors.size,
        2 * factors.size,
        in_specs=[VMEM_SPEC] * 3,
        out_specs=(VMEM_SPEC,) * 2,
        scratch_shapes=[pltpu.VMEM((tokens, columns), jnp.float32)],
        name="extra_term",
    )(weights, slot_wide, factors)


def pair_kernel(rows_own, rows_ref, pair_rows_ref, extra_ref, extra_pair_ref, frozen_ref,
                pair_frozen_ref, *outs):
    width = frozen_ref.shape[0]
    columns = extra_ref.shape[1]
    position = lax.axis_index("tensor")
    chip, core = position // 2, position % 2
    low = jnp.where(core == 0, extra_ref[...], extra_pair_ref[...])
    high = jnp.where(core == 0, extra_pair_ref[...], extra_ref[...])
    for block in range(width // columns):
        at = slice(block * columns, (block + 1) * columns)
        total = dot(rows_ref[...], frozen_ref[at, :], NT)
        total = total + dot(pair_rows_ref[...], pair_frozen_ref[at, :], NT)
        extra = low if block % 2 == 0 else high
        total = total + jnp.where(chip == block // 2, extra, 0.0)
        outs[0][:, at] = total[:rows_own, :]
        for i, out in enumerate(outs[1:], 1):
            out[:, at] = total[i * rows_own : (i + 1) * rows_own, :].astype(jnp.bfloat16)


def pair_sum(rows_own, rows, pair_rows, extra, extra_pair, frozen, pair_frozen):
    half, kv = rows.shape
    width = frozen.shape[0]
    sent = jax.ShapeDtypeStruct((rows_own, width), jnp.bfloat16)
    n_out = half // rows_own - 1
    return call(
        functools.partial(pair_kernel, rows_own),
        (jax.ShapeDtypeStruct((rows_own, width), jnp.float32),) + (sent,) * n_out,
        4 * half * width * kv,
        4 * kv * width + 4 * half * width,
        in_specs=[VMEM_SPEC] * 6,
        out_specs=(VMEM_SPEC,) * (n_out + 1),
        name="pair_sum",
    )(rows, pair_rows, extra, extra_pair, frozen, pair_frozen)


def adam_kernel(columns, kv, scale, owned_ref, *refs):
    states, outs = refs[:6], refs[6:]
    weights = owned_ref[:, columns + kv :].astype(jnp.float32)
    turned = jnp.transpose(weights).astype(jnp.bfloat16)
    grad_up = dot(turned[:PADDED_RANK], owned_ref[:, columns : columns + kv], NN) / scale
    grad_down = dot(turned[PADDED_RANK:], owned_ref[:, :columns], NN) / scale
    for first, grad in ((0, grad_down), (3, grad_up)):
        state = [ref[...] for ref in states[first : first + 3]]
        for out, value in zip(outs[first : first + 3], adamw(*state, grad), strict=True):
            out[...] = value


def owners_update(owned, columns, kv, scale, states):
    shapes = tuple(jax.ShapeDtypeStruct(v.shape, v.dtype) for v in states)
    return call(
        functools.partial(adam_kernel, columns, kv, scale),
        shapes,
        2 * owned.size * PADDED_RANK,
        2 * owned.size + 8 * sum(v.size for v in states),
        in_specs=[VMEM_SPEC] * (1 + len(states)),
        out_specs=(VMEM_SPEC,) * len(states),
        name="owners_update",
    )(owned, *states)


def local(
    hidden,
    cotangent,
    frozen_key_value,
    adapter_down_factors,
    adapter_up_factors,
    down_master_copy,
    down_first_moment,
    down_second_moment,
    up_master_copy,
    up_first_moment,
    up_second_moment,
    adapter_of_token,
    adapter_rank_bucket,
    adapter_owner_slot,
    live_token_counts,
):
    n_tensor = lax.axis_size("tensor")
    n_chip = n_tensor // 2
    tokens = cotangent.shape[0]
    rows_own, width = hidden.shape
    columns = width // n_tensor
    n_slot = adapter_owner_slot.shape[0]

    blocks = hidden.reshape(rows_own, n_tensor, columns).transpose(1, 0, 2)
    hidden_columns = lax.all_to_all(blocks, "tensor", 0, 0, tiled=True).reshape(tokens, columns)

    masked, rows, pair_rows, slot_wide, factor_wide, place, up_own = prep(
        rows_own,
        live_token_counts,
        adapter_rank_bucket,
        adapter_owner_slot,
        adapter_of_token.reshape(1, tokens),
        cotangent,
        adapter_up_factors,
    )

    pair_rows = swap(pair_rows, 1, n_tensor)
    pair_frozen = swap(frozen_key_value, 1, n_tensor)
    slot_wide, pair_rows = lax.optimization_barrier((slot_wide, pair_rows))

    own = low_rank(hidden_columns, slot_wide, up_own, adapter_down_factors)
    own = own + swap(own, 1, n_tensor)
    weights = (sum_over_chips(own, n_tensor) * factor_wide).astype(jnp.bfloat16)
    extra_ours, extra_theirs = extra_term(rows_own, weights, slot_wide, adapter_down_factors)
    weights, extra_ours, extra_theirs = lax.optimization_barrier(
        (weights, extra_ours, extra_theirs)
    )

    packed = pack_rows(place, [hidden_columns, masked, weights], n_slot * CAP)
    owned = lax.all_to_all(
        packed.reshape(n_slot, CAP, -1), "dp", 0, 0, tiled=True
    ).reshape(n_slot * CAP, -1)

    total, *sent = pair_sum(
        rows_own,
        rows,
        pair_rows,
        extra_ours,
        swap(extra_theirs, 1, n_tensor),
        frozen_key_value,
        pair_frozen,
    )
    for step, value in enumerate(sent, 1):
        arrived = lax.ppermute(
            value, "tensor", [(i, (i + 2 * step) % n_tensor) for i in range(n_tensor)]
        )
        total = total + arrived.astype(jnp.float32)
    hidden_gradient = total.astype(jnp.bfloat16)

    owned, hidden_gradient = lax.optimization_barrier((owned, hidden_gradient))
    down_states = (down_master_copy.T, down_first_moment.T, down_second_moment.T)
    up_states = (up_master_copy, up_first_moment, up_second_moment)
    updated = owners_update(
        owned, columns, cotangent.shape[1], tokens, (*down_states, *up_states)
    )
    new_dm, new_dmo, new_ds = (value.T for value in updated[:3])
    new_um, new_umo, new_us = updated[3:]
    return (hidden_gradient, new_dm, new_dmo, new_ds, new_um, new_umo, new_us)


def solution(mesh):
    return jax.shard_map(
        local,
        mesh=mesh,
        in_specs=(
            P(("dp", "tensor"), None),
            P("dp", "tensor"),
            P(None, "tensor"),
            P("tensor", None),
            P(None, "tensor"),
            P("tensor", "dp"),
            P("tensor", "dp"),
            P("tensor", "dp"),
            P("dp", "tensor"),
            P("dp", "tensor"),
            P("dp", "tensor"),
            P("dp", None),
            P(),
            P(),
            P(),
        ),
        out_specs=(
            P(("dp", "tensor"), None),
            P("tensor", "dp"),
            P("tensor", "dp"),
            P("tensor", "dp"),
            P("dp", "tensor"),
            P("dp", "tensor"),
            P("dp", "tensor"),
        ),
        check_vma=False,
    )
```

```python
import functools

import jax
import jax.numpy as jnp
from jax import lax
from jax.experimental import pallas as pl
from jax.experimental.pallas import tpu as pltpu
from jax.sharding import PartitionSpec as P

RMIN = 8
PADDED_RANK = 64
CAP = 16


adapter_alpha_scale = 16.0
beta_one = 0.9
beta_two = 0.999
adam_eps = 1e-08
learn_rate = 0.0002
weight_decay = 0.1
first_fix = 0.9999734386011124
second_fix = 0.09520785288629038


def adamw(master, moment, second, grad):
    new_moment = beta_one * moment + (1.0 - beta_one) * grad
    new_second = beta_two * second + (1.0 - beta_two) * grad * grad
    update = new_moment / first_fix / (jnp.sqrt(new_second / second_fix) + adam_eps)
    new_master = master - learn_rate * (update + weight_decay * master)
    return (new_master, new_moment, new_second)


def contract_helper(left, right, left_dim, right_dim):
    return lax.dot_general(
        left, right, (((left_dim,), (right_dim,)), ((), ())), preferred_element_type=jnp.float32
    )


def swap(value, mask, count):
    return lax.ppermute(value, "tensor", [(i, i ^ mask) for i in range(count)])


def sum_over_chips(value, count):
    value = value.astype(jnp.bfloat16)
    terms = [value] + [swap(value, mask, count) for mask in (2, 4, 6)]
    own, near, far, farther = (term.astype(jnp.float32) for term in terms)
    return (own + near) + (far + farther)


VMEM_LIMIT = 16 * 1024 * 1024
SMEM_SPEC = pl.BlockSpec(memory_space=pltpu.MemorySpace.SMEM)
VMEM_SPEC = pl.BlockSpec(memory_space=pltpu.MemorySpace.VMEM)
NT = (((1,), (1,)), ((), ()))
NN = (((1,), (0,)), ((), ()))


def call(kernel, out_shape, flops, moved, **options):
    return pl.pallas_call(
        kernel,
        out_shape=out_shape,
        compiler_params=pltpu.CompilerParams(vmem_limit_bytes=VMEM_LIMIT),
        cost_estimate=pl.CostEstimate(flops=flops, bytes_accessed=moved, transcendentals=0),
        **options,
    )


def dot(left, right, dims):
    return lax.dot_general(left, right, dims, preferred_element_type=jnp.float32)


def lane_slot(shape, first):
    return (lax.broadcasted_iota(jnp.int32, shape, 1) // PADDED_RANK + first).astype(jnp.float32)


def prep_kernel(rows_own, live_ref, bucket_ref, owner_ref, adapter_ref, cot_ref, up_ref,
                masked_ref, ours_ref, theirs_ref, slot_ref, factor_ref, place_ref, up_own_ref):
    tokens = cot_ref.shape[0]
    n_chip = tokens // rows_own // 2
    position = lax.axis_index("tensor")
    chip, core = position // 2, position % 2
    live = live_ref[lax.axis_index("dp")]
    token = lax.broadcasted_iota(jnp.int32, (tokens, 1), 0)
    masked = jnp.where(token < live, cot_ref[...].astype(jnp.float32), 0.0).astype(jnp.bfloat16)
    masked_ref[...] = masked
    for step in range(n_chip):
        block = (chip + step) % n_chip * 2
        for out, k in ((ours_ref, core), (theirs_ref, 1 - core)):
            start = pl.multiple_of((block + k) * rows_own, rows_own)
            ids = start + lax.broadcasted_iota(jnp.int32, (rows_own, 1), 0)
            rows = cot_ref[pl.ds(start, rows_own), :].astype(jnp.float32)
            out[pl.ds(step * rows_own, rows_own), :] = jnp.where(ids < live, rows, 0.0).astype(
                jnp.bfloat16
            )
    adapter = adapter_ref[...]
    slot = jnp.zeros_like(adapter)
    rank = jnp.zeros_like(adapter)
    for a in range(owner_ref.shape[0]):
        hit = adapter == a
        slot = jnp.where(hit, owner_ref[a], slot)
        rank = jnp.where(hit, lax.shift_left(RMIN, bucket_ref[a]), rank)
    slot_row = slot.astype(jnp.float32)
    rank_row = rank.astype(jnp.float32)
    down = lax.broadcasted_iota(jnp.int32, (tokens, tokens), 0)
    across = lax.broadcasted_iota(jnp.int32, (tokens, tokens), 1)
    diagonal = down == across
    slot_col = jnp.sum(jnp.where(diagonal, slot_row, 0.0), axis=1, keepdims=True)
    rank_col = jnp.sum(jnp.where(diagonal, rank_row, 0.0), axis=1, keepdims=True)
    earlier = jnp.where((slot_col == slot_row) & (down < across), 1.0, 0.0)
    place = slot_row * CAP + jnp.sum(earlier, axis=0, keepdims=True)
    place_ref[...] = place.astype(jnp.int32)
    lanes = factor_ref.shape[1]
    slot_wide = jnp.broadcast_to(slot_col, (tokens, lanes))
    slot_ref[...] = slot_wide
    kept = lax.broadcasted_iota(jnp.int32, (tokens, lanes), 1) % PADDED_RANK
    factor_ref[...] = jnp.where(
        kept.astype(jnp.float32) < rank_col, adapter_alpha_scale / rank_col, 0.0
    )
    chunk = 256
    acc = jnp.zeros((tokens, chunk), jnp.float32)
    for c in range(up_ref.shape[0] // chunk):
        part = dot(masked, up_ref[pl.ds(c * chunk, chunk), :], NT)
        hit = slot_col == lane_slot((1, chunk), c * chunk // PADDED_RANK)
        acc = acc + jnp.where(hit, part, 0.0)
    acc = acc[:, :128] + acc[:, 128:]
    up_own_ref[...] = acc[:, :PADDED_RANK] + acc[:, PADDED_RANK:]


def prep(rows_own, live, bucket, owner, adapter_row, cotangent, up_factors):
    tokens, kv = cotangent.shape
    shapes = (
        jax.ShapeDtypeStruct((tokens, kv), jnp.bfloat16),
        jax.ShapeDtypeStruct((tokens // 2, kv), jnp.bfloat16),
        jax.ShapeDtypeStruct((tokens // 2, kv), jnp.bfloat16),
        jax.ShapeDtypeStruct((tokens, 128), jnp.float32),
        jax.ShapeDtypeStruct((tokens, 128), jnp.float32),
        jax.ShapeDtypeStruct((1, tokens), jnp.int32),
        jax.ShapeDtypeStruct((tokens, PADDED_RANK), jnp.float32),
    )
    return call(
        functools.partial(prep_kernel, rows_own),
        shapes,
        2 * tokens * kv * up_factors.shape[0],
        up_factors.size * 2,
        in_specs=[SMEM_SPEC] * 3 + [VMEM_SPEC] * 3,
        out_specs=(VMEM_SPEC,) * len(shapes),
        name="prep",
    )(live, bucket, owner, adapter_row, cotangent, up_factors)


def pack_kernel(place_ref, *refs):
    parts, out_ref = refs[:-1], refs[-1]
    rows, tokens = out_ref.shape[0], place_ref.shape[1]
    down = lax.broadcasted_iota(jnp.int32, (rows, tokens), 0)
    pick = jnp.where(down == place_ref[...], 1.0, 0.0).astype(jnp.bfloat16)
    first = 0
    for part in parts:
        width = part.shape[1]
        out_ref[:, first : first + width] = dot(pick, part[...], NN).astype(jnp.bfloat16)
        first += width


def pack_rows(place, parts, rows):
    tokens, columns = place.shape[1], sum(v.shape[1] for v in parts)
    return call(
        pack_kernel,
        jax.ShapeDtypeStruct((rows, columns), jnp.bfloat16),
        2 * rows * columns * tokens,
        2 * (rows + tokens) * columns,
        in_specs=[VMEM_SPEC] * (len(parts) + 1),
        out_specs=VMEM_SPEC,
        name="pack",
    )(place, *parts)


CHUNK = 256


def down_kernel(hidden_ref, slot_ref, up_own_ref, factors_ref, out_ref):
    slot = slot_ref[...]
    acc = jnp.zeros(slot.shape, jnp.float32)
    for first in range(0, factors_ref.shape[1], CHUNK):
        product = dot(hidden_ref[...], factors_ref[:, first : first + CHUNK], NN)
        for d in range(0, CHUNK, 128):
            hit = slot == lane_slot((1, 128), (first + d) // PADDED_RANK)
            acc = acc + jnp.where(hit, product[:, d : d + 128], 0.0)
    out_ref[:, :PADDED_RANK] = acc[:, :PADDED_RANK] + acc[:, PADDED_RANK:]
    out_ref[:, PADDED_RANK:] = up_own_ref[...]


def low_rank(hidden_columns, slot_wide, up_own, factors):
    tokens = hidden_columns.shape[0]
    return call(
        down_kernel,
        jax.ShapeDtypeStruct((tokens, 2 * PADDED_RANK), jnp.float32),
        2 * tokens * factors.size,
        2 * factors.size,
        in_specs=[VMEM_SPEC] * 4,
        out_specs=VMEM_SPEC,
        name="low_rank",
    )(hidden_columns, slot_wide, up_own, factors)


def extra_kernel(rows_own, weight_ref, slot_ref, factors_ref, ours_ref, theirs_ref, extra_ref):
    tokens = weight_ref.shape[0]
    n_chip = tokens // rows_own // 2
    slot = slot_ref[...]
    weight = weight_ref[:, PADDED_RANK:].astype(jnp.float32)
    double = jnp.concatenate([weight, weight], axis=1)
    for first in range(0, factors_ref.shape[1], CHUNK):
        pieces = []
        for d in range(0, CHUNK, 128):
            hit = slot == lane_slot((1, 128), (first + d) // PADDED_RANK)
            pieces.append(jnp.where(hit, double, 0.0).astype(jnp.bfloat16))
        placed = jnp.concatenate(pieces, axis=1)
        term = dot(placed, factors_ref[:, first : first + CHUNK], NT)
        if first == 0:
            extra_ref[...] = term
        else:
            extra_ref[...] += term
    position = lax.axis_index("tensor")
    chip, core = position // 2, position % 2
    for turn in range(n_chip):
        block = (chip + turn) % n_chip * 2
        for out, k in ((ours_ref, core), (theirs_ref, 1 - core)):
            start = pl.multiple_of((block + k) * rows_own, rows_own)
            out[pl.ds(turn * rows_own, rows_own), :] = extra_ref[pl.ds(start, rows_own), :]


def extra_term(rows_own, weights, slot_wide, factors):
    tokens, columns = weights.shape[0], factors.shape[0]
    half = jax.ShapeDtypeStruct((tokens // 2, columns), jnp.float32)
    return call(
        functools.partial(extra_kernel, rows_own),
        (half, half),
        2 * tokens * factors.size,
        2 * factors.size,
        in_specs=[VMEM_SPEC] * 3,
        out_specs=(VMEM_SPEC,) * 2,
        scratch_shapes=[pltpu.VMEM((tokens, columns), jnp.float32)],
        name="extra_term",
    )(weights, slot_wide, factors)


def pair_kernel(rows_own, rows_ref, pair_rows_ref, extra_ref, extra_pair_ref, frozen_ref,
                pair_frozen_ref, *outs):
    width = frozen_ref.shape[0]
    columns = extra_ref.shape[1]
    position = lax.axis_index("tensor")
    chip, core = position // 2, position % 2
    low = jnp.where(core == 0, extra_ref[...], extra_pair_ref[...])
    high = jnp.where(core == 0, extra_pair_ref[...], extra_ref[...])
    for block in range(width // columns):
        at = slice(block * columns, (block + 1) * columns)
        total = dot(rows_ref[...], frozen_ref[at, :], NT)
        total = total + dot(pair_rows_ref[...], pair_frozen_ref[at, :], NT)
        extra = low if block % 2 == 0 else high
        total = total + jnp.where(chip == block // 2, extra, 0.0)
        outs[0][:, at] = total[:rows_own, :]
        for i, out in enumerate(outs[1:], 1):
            out[:, at] = total[i * rows_own : (i + 1) * rows_own, :].astype(jnp.bfloat16)


def pair_sum(rows_own, rows, pair_rows, extra, extra_pair, frozen, pair_frozen):
    half, kv = rows.shape
    width = frozen.shape[0]
    sent = jax.ShapeDtypeStruct((rows_own, width), jnp.bfloat16)
    n_out = half // rows_own - 1
    return call(
        functools.partial(pair_kernel, rows_own),
        (jax.ShapeDtypeStruct((rows_own, width), jnp.float32),) + (sent,) * n_out,
        4 * half * width * kv,
        4 * kv * width + 4 * half * width,
        in_specs=[VMEM_SPEC] * 6,
        out_specs=(VMEM_SPEC,) * (n_out + 1),
        name="pair_sum",
    )(rows, pair_rows, extra, extra_pair, frozen, pair_frozen)


def adam_kernel(columns, kv, scale, owned_ref, *refs):
    states, outs = refs[:6], refs[6:]
    weights = owned_ref[:, columns + kv :].astype(jnp.float32)
    turned = jnp.transpose(weights).astype(jnp.bfloat16)
    grad_up = dot(turned[:PADDED_RANK], owned_ref[:, columns : columns + kv], NN) / scale
    grad_down = dot(turned[PADDED_RANK:], owned_ref[:, :columns], NN) / scale
    for first, grad in ((0, grad_down), (3, grad_up)):
        state = [ref[...] for ref in states[first : first + 3]]
        for out, value in zip(outs[first : first + 3], adamw(*state, grad), strict=True):
            out[...] = value


def owners_update(owned, columns, kv, scale, states):
    shapes = tuple(jax.ShapeDtypeStruct(v.shape, v.dtype) for v in states)
    return call(
        functools.partial(adam_kernel, columns, kv, scale),
        shapes,
        2 * owned.size * PADDED_RANK,
        2 * owned.size + 8 * sum(v.size for v in states),
        in_specs=[VMEM_SPEC] * (1 + len(states)),
        out_specs=(VMEM_SPEC,) * len(states),
        name="owners_update",
    )(owned, *states)


def local(
    hidden,
    cotangent,
    frozen_key_value,
    adapter_down_factors,
    adapter_up_factors,
    down_master_copy,
    down_first_moment,
    down_second_moment,
    up_master_copy,
    up_first_moment,
    up_second_moment,
    adapter_of_token,
    adapter_rank_bucket,
    adapter_owner_slot,
    live_token_counts,
):
    n_tensor = lax.axis_size("tensor")
    n_chip = n_tensor // 2
    tokens = cotangent.shape[0]
    rows_own, width = hidden.shape
    columns = width // n_tensor
    n_slot = adapter_owner_slot.shape[0]

    blocks = hidden.reshape(rows_own, n_tensor, columns).transpose(1, 0, 2)
    hidden_columns = lax.all_to_all(blocks, "tensor", 0, 0, tiled=True).reshape(tokens, columns)

    masked, rows, pair_rows, slot_wide, factor_wide, place, up_own = prep(
        rows_own,
        live_token_counts,
        adapter_rank_bucket,
        adapter_owner_slot,
        adapter_of_token.reshape(1, tokens),
        cotangent,
        adapter_up_factors,
    )

    pair_rows = swap(pair_rows, 1, n_tensor)
    pair_frozen = swap(frozen_key_value, 1, n_tensor)
    slot_wide, pair_rows = lax.optimization_barrier((slot_wide, pair_rows))

    own = low_rank(hidden_columns, slot_wide, up_own, adapter_down_factors)
    own = own + swap(own, 1, n_tensor)
    weights = (sum_over_chips(own, n_tensor) * factor_wide).astype(jnp.bfloat16)
    packed = pack_rows(place, [hidden_columns, masked, weights], n_slot * CAP)
    packed, weights = lax.optimization_barrier((packed, weights))
    extra_ours, extra_theirs = extra_term(rows_own, weights, slot_wide, adapter_down_factors)
    owned = lax.all_to_all(
        packed.reshape(n_slot, CAP, -1), "dp", 0, 0, tiled=True
    ).reshape(n_slot * CAP, -1)

    total, *sent = pair_sum(
        rows_own,
        rows,
        pair_rows,
        extra_ours,
        swap(extra_theirs, 1, n_tensor),
        frozen_key_value,
        pair_frozen,
    )
    for step, value in enumerate(sent, 1):
        arrived = lax.ppermute(
            value, "tensor", [(i, (i + 2 * step) % n_tensor) for i in range(n_tensor)]
        )
        total = total + arrived.astype(jnp.float32)
    hidden_gradient = total.astype(jnp.bfloat16)

    owned, hidden_gradient = lax.optimization_barrier((owned, hidden_gradient))
    down_states = (down_master_copy.T, down_first_moment.T, down_second_moment.T)
    up_states = (up_master_copy, up_first_moment, up_second_moment)
    updated = owners_update(
        owned, columns, cotangent.shape[1], tokens, (*down_states, *up_states)
    )
    new_dm, new_dmo, new_ds = (value.T for value in updated[:3])
    new_um, new_umo, new_us = updated[3:]
    return (hidden_gradient, new_dm, new_dmo, new_ds, new_um, new_umo, new_us)


def solution(mesh):
    return jax.shard_map(
        local,
        mesh=mesh,
        in_specs=(
            P(("dp", "tensor"), None),
            P("dp", "tensor"),
            P(None, "tensor"),
            P("tensor", None),
            P(None, "tensor"),
            P("tensor", "dp"),
            P("tensor", "dp"),
            P("tensor", "dp"),
            P("dp", "tensor"),
            P("dp", "tensor"),
            P("dp", "tensor"),
            P("dp", None),
            P(),
            P(),
            P(),
        ),
        out_specs=(
            P(("dp", "tensor"), None),
            P("tensor", "dp"),
            P("tensor", "dp"),
            P("tensor", "dp"),
            P("dp", "tensor"),
            P("dp", "tensor"),
            P("dp", "tensor"),
        ),
        check_vma=False,
    )
```

```python
import functools

import jax
import jax.numpy as jnp
from jax import lax
from jax.experimental import pallas as pl
from jax.experimental.pallas import tpu as pltpu
from jax.sharding import PartitionSpec as P

RMIN = 8
PADDED_RANK = 64
CAP = 16


adapter_alpha_scale = 16.0
beta_one = 0.9
beta_two = 0.999
adam_eps = 1e-08
learn_rate = 0.0002
weight_decay = 0.1
first_fix = 0.9999734386011124
second_fix = 0.09520785288629038


def adamw(master, moment, second, grad):
    new_moment = beta_one * moment + (1.0 - beta_one) * grad
    new_second = beta_two * second + (1.0 - beta_two) * grad * grad
    update = new_moment / first_fix / (jnp.sqrt(new_second / second_fix) + adam_eps)
    new_master = master - learn_rate * (update + weight_decay * master)
    return (new_master, new_moment, new_second)


def contract_helper(left, right, left_dim, right_dim):
    return lax.dot_general(
        left, right, (((left_dim,), (right_dim,)), ((), ())), preferred_element_type=jnp.float32
    )


def swap(value, mask, count):
    return lax.ppermute(value, "tensor", [(i, i ^ mask) for i in range(count)])


def sum_over_chips(value, count):
    near = value + swap(value, 2, count)
    far = swap(value, 4, count) + swap(value, 6, count)
    return near + far


VMEM_LIMIT = 16 * 1024 * 1024
SMEM_SPEC = pl.BlockSpec(memory_space=pltpu.MemorySpace.SMEM)
VMEM_SPEC = pl.BlockSpec(memory_space=pltpu.MemorySpace.VMEM)
NT = (((1,), (1,)), ((), ()))
NN = (((1,), (0,)), ((), ()))


def call(kernel, out_shape, flops, moved, **options):
    return pl.pallas_call(
        kernel,
        out_shape=out_shape,
        compiler_params=pltpu.CompilerParams(vmem_limit_bytes=VMEM_LIMIT),
        cost_estimate=pl.CostEstimate(flops=flops, bytes_accessed=moved, transcendentals=0),
        **options,
    )


def dot(left, right, dims):
    return lax.dot_general(left, right, dims, preferred_element_type=jnp.float32)


def lane_slot(shape, first):
    return (lax.broadcasted_iota(jnp.int32, shape, 1) // PADDED_RANK + first).astype(jnp.float32)


def prep_kernel(rows_own, live_ref, bucket_ref, owner_ref, adapter_ref, cot_ref, up_ref,
                masked_ref, ours_ref, theirs_ref, slot_ref, factor_ref, place_ref, up_own_ref):
    tokens = cot_ref.shape[0]
    n_chip = tokens // rows_own // 2
    position = lax.axis_index("tensor")
    chip, core = position // 2, position % 2
    live = live_ref[lax.axis_index("dp")]
    token = lax.broadcasted_iota(jnp.int32, (tokens, 1), 0)
    masked = jnp.where(token < live, cot_ref[...].astype(jnp.float32), 0.0).astype(jnp.bfloat16)
    masked_ref[...] = masked
    for step in range(n_chip):
        block = (chip + step) % n_chip * 2
        for out, k in ((ours_ref, core), (theirs_ref, 1 - core)):
            start = pl.multiple_of((block + k) * rows_own, rows_own)
            ids = start + lax.broadcasted_iota(jnp.int32, (rows_own, 1), 0)
            rows = cot_ref[pl.ds(start, rows_own), :].astype(jnp.float32)
            out[pl.ds(step * rows_own, rows_own), :] = jnp.where(ids < live, rows, 0.0).astype(
                jnp.bfloat16
            )
    adapter = adapter_ref[...]
    slot = jnp.zeros_like(adapter)
    rank = jnp.zeros_like(adapter)
    for a in range(owner_ref.shape[0]):
        hit = adapter == a
        slot = jnp.where(hit, owner_ref[a], slot)
        rank = jnp.where(hit, lax.shift_left(RMIN, bucket_ref[a]), rank)
    slot_row = slot.astype(jnp.float32)
    rank_row = rank.astype(jnp.float32)
    down = lax.broadcasted_iota(jnp.int32, (tokens, tokens), 0)
    across = lax.broadcasted_iota(jnp.int32, (tokens, tokens), 1)
    diagonal = down == across
    slot_col = jnp.sum(jnp.where(diagonal, slot_row, 0.0), axis=1, keepdims=True)
    rank_col = jnp.sum(jnp.where(diagonal, rank_row, 0.0), axis=1, keepdims=True)
    earlier = jnp.where((slot_col == slot_row) & (down < across), 1.0, 0.0)
    place = slot_row * CAP + jnp.sum(earlier, axis=0, keepdims=True)
    place_ref[...] = place.astype(jnp.int32)
    lanes = factor_ref.shape[1]
    slot_wide = jnp.broadcast_to(slot_col, (tokens, lanes))
    slot_ref[...] = slot_wide
    kept = lax.broadcasted_iota(jnp.int32, (tokens, lanes), 1) % PADDED_RANK
    factor_ref[...] = jnp.where(
        kept.astype(jnp.float32) < rank_col, adapter_alpha_scale / rank_col, 0.0
    )
    chunk = 256
    acc = jnp.zeros((tokens, chunk), jnp.float32)
    for c in range(up_ref.shape[0] // chunk):
        part = dot(masked, up_ref[pl.ds(c * chunk, chunk), :], NT)
        hit = slot_col == lane_slot((1, chunk), c * chunk // PADDED_RANK)
        acc = acc + jnp.where(hit, part, 0.0)
    acc = acc[:, :128] + acc[:, 128:]
    up_own_ref[...] = acc[:, :PADDED_RANK] + acc[:, PADDED_RANK:]


def prep(rows_own, live, bucket, owner, adapter_row, cotangent, up_factors):
    tokens, kv = cotangent.shape
    shapes = (
        jax.ShapeDtypeStruct((tokens, kv), jnp.bfloat16),
        jax.ShapeDtypeStruct((tokens // 2, kv), jnp.bfloat16),
        jax.ShapeDtypeStruct((tokens // 2, kv), jnp.bfloat16),
        jax.ShapeDtypeStruct((tokens, 128), jnp.float32),
        jax.ShapeDtypeStruct((tokens, 128), jnp.float32),
        jax.ShapeDtypeStruct((1, tokens), jnp.int32),
        jax.ShapeDtypeStruct((tokens, PADDED_RANK), jnp.float32),
    )
    return call(
        functools.partial(prep_kernel, rows_own),
        shapes,
        2 * tokens * kv * up_factors.shape[0],
        up_factors.size * 2,
        in_specs=[SMEM_SPEC] * 3 + [VMEM_SPEC] * 3,
        out_specs=(VMEM_SPEC,) * len(shapes),
        name="prep",
    )(live, bucket, owner, adapter_row, cotangent, up_factors)


def pack_kernel(place_ref, *refs):
    parts, out_ref = refs[:-1], refs[-1]
    rows, tokens = out_ref.shape[0], place_ref.shape[1]
    down = lax.broadcasted_iota(jnp.int32, (rows, tokens), 0)
    pick = jnp.where(down == place_ref[...], 1.0, 0.0).astype(jnp.bfloat16)
    first = 0
    for part in parts:
        width = part.shape[1]
        out_ref[:, first : first + width] = dot(pick, part[...], NN).astype(jnp.bfloat16)
        first += width


def pack_rows(place, parts, rows):
    tokens, columns = place.shape[1], sum(v.shape[1] for v in parts)
    return call(
        pack_kernel,
        jax.ShapeDtypeStruct((rows, columns), jnp.bfloat16),
        2 * rows * columns * tokens,
        2 * (rows + tokens) * columns,
        in_specs=[VMEM_SPEC] * (len(parts) + 1),
        out_specs=VMEM_SPEC,
        name="pack",
    )(place, *parts)


CHUNK = 256


def down_kernel(hidden_ref, slot_ref, up_own_ref, factors_ref, ours_ref, theirs_ref, both_ref):
    slot = slot_ref[...]
    acc = jnp.zeros(slot.shape, jnp.float32)
    for first in range(0, factors_ref.shape[1], CHUNK):
        product = dot(hidden_ref[...], factors_ref[:, first : first + CHUNK], NN)
        for d in range(0, CHUNK, 128):
            hit = slot == lane_slot((1, 128), (first + d) // PADDED_RANK)
            acc = acc + jnp.where(hit, product[:, d : d + 128], 0.0)
    both_ref[:, :PADDED_RANK] = acc[:, :PADDED_RANK] + acc[:, PADDED_RANK:]
    both_ref[:, PADDED_RANK:] = up_own_ref[...]
    half = ours_ref.shape[0]
    core = lax.axis_index("tensor") % 2
    ours_ref[...] = both_ref[pl.ds(pl.multiple_of(core * half, half), half), :]
    theirs_ref[...] = both_ref[pl.ds(pl.multiple_of((1 - core) * half, half), half), :]


def low_rank(hidden_columns, slot_wide, up_own, factors):
    tokens = hidden_columns.shape[0]
    return call(
        down_kernel,
        (jax.ShapeDtypeStruct((tokens // 2, 2 * PADDED_RANK), jnp.float32),) * 2,
        2 * tokens * factors.size,
        2 * factors.size,
        in_specs=[VMEM_SPEC] * 4,
        out_specs=(VMEM_SPEC,) * 2,
        scratch_shapes=[pltpu.VMEM((tokens, 2 * PADDED_RANK), jnp.float32)],
        name="low_rank",
    )(hidden_columns, slot_wide, up_own, factors)


def extra_kernel(rows_own, weight_ref, slot_ref, factors_ref, ours_ref, theirs_ref, extra_ref):
    tokens = weight_ref.shape[0]
    n_chip = tokens // rows_own // 2
    slot = slot_ref[...]
    weight = weight_ref[:, PADDED_RANK:].astype(jnp.float32)
    double = jnp.concatenate([weight, weight], axis=1)
    for first in range(0, factors_ref.shape[1], CHUNK):
        pieces = []
        for d in range(0, CHUNK, 128):
            hit = slot == lane_slot((1, 128), (first + d) // PADDED_RANK)
            pieces.append(jnp.where(hit, double, 0.0).astype(jnp.bfloat16))
        placed = jnp.concatenate(pieces, axis=1)
        term = dot(placed, factors_ref[:, first : first + CHUNK], NT)
        if first == 0:
            extra_ref[...] = term
        else:
            extra_ref[...] += term
    position = lax.axis_index("tensor")
    chip, core = position // 2, position % 2
    for turn in range(n_chip):
        block = (chip + turn) % n_chip * 2
        for out, k in ((ours_ref, core), (theirs_ref, 1 - core)):
            start = pl.multiple_of((block + k) * rows_own, rows_own)
            out[pl.ds(turn * rows_own, rows_own), :] = extra_ref[pl.ds(start, rows_own), :]


def extra_term(rows_own, weights, slot_wide, factors):
    tokens, columns = weights.shape[0], factors.shape[0]
    half = jax.ShapeDtypeStruct((tokens // 2, columns), jnp.float32)
    return call(
        functools.partial(extra_kernel, rows_own),
        (half, half),
        2 * tokens * factors.size,
        2 * factors.size,
        in_specs=[VMEM_SPEC] * 3,
        out_specs=(VMEM_SPEC,) * 2,
        scratch_shapes=[pltpu.VMEM((tokens, columns), jnp.float32)],
        name="extra_term",
    )(weights, slot_wide, factors)


def pair_kernel(rows_own, rows_ref, pair_rows_ref, extra_ref, extra_pair_ref, frozen_ref,
                pair_frozen_ref, *outs):
    width = frozen_ref.shape[0]
    columns = extra_ref.shape[1]
    position = lax.axis_index("tensor")
    chip, core = position // 2, position % 2
    low = jnp.where(core == 0, extra_ref[...], extra_pair_ref[...])
    high = jnp.where(core == 0, extra_pair_ref[...], extra_ref[...])
    for block in range(width // columns):
        at = slice(block * columns, (block + 1) * columns)
        total = dot(rows_ref[...], frozen_ref[at, :], NT)
        total = total + dot(pair_rows_ref[...], pair_frozen_ref[at, :], NT)
        extra = low if block % 2 == 0 else high
        total = total + jnp.where(chip == block // 2, extra, 0.0)
        outs[0][:, at] = total[:rows_own, :]
        for i, out in enumerate(outs[1:], 1):
            out[:, at] = total[i * rows_own : (i + 1) * rows_own, :].astype(jnp.bfloat16)


def pair_sum(rows_own, rows, pair_rows, extra, extra_pair, frozen, pair_frozen):
    half, kv = rows.shape
    width = frozen.shape[0]
    sent = jax.ShapeDtypeStruct((rows_own, width), jnp.bfloat16)
    n_out = half // rows_own - 1
    return call(
        functools.partial(pair_kernel, rows_own),
        (jax.ShapeDtypeStruct((rows_own, width), jnp.float32),) + (sent,) * n_out,
        4 * half * width * kv,
        4 * kv * width + 4 * half * width,
        in_specs=[VMEM_SPEC] * 6,
        out_specs=(VMEM_SPEC,) * (n_out + 1),
        name="pair_sum",
    )(rows, pair_rows, extra, extra_pair, frozen, pair_frozen)


def adam_kernel(columns, kv, scale, owned_ref, *refs):
    states, outs = refs[:6], refs[6:]
    weights = owned_ref[:, columns + kv :].astype(jnp.float32)
    turned = jnp.transpose(weights).astype(jnp.bfloat16)
    grad_up = dot(turned[:PADDED_RANK], owned_ref[:, columns : columns + kv], NN) / scale
    grad_down = dot(turned[PADDED_RANK:], owned_ref[:, :columns], NN) / scale
    for first, grad in ((0, grad_down), (3, grad_up)):
        state = [ref[...] for ref in states[first : first + 3]]
        for out, value in zip(outs[first : first + 3], adamw(*state, grad), strict=True):
            out[...] = value


def owners_update(owned, columns, kv, scale, states):
    shapes = tuple(jax.ShapeDtypeStruct(v.shape, v.dtype) for v in states)
    return call(
        functools.partial(adam_kernel, columns, kv, scale),
        shapes,
        2 * owned.size * PADDED_RANK,
        2 * owned.size + 8 * sum(v.size for v in states),
        in_specs=[VMEM_SPEC] * (1 + len(states)),
        out_specs=(VMEM_SPEC,) * len(states),
        name="owners_update",
    )(owned, *states)


def local(
    hidden,
    cotangent,
    frozen_key_value,
    adapter_down_factors,
    adapter_up_factors,
    down_master_copy,
    down_first_moment,
    down_second_moment,
    up_master_copy,
    up_first_moment,
    up_second_moment,
    adapter_of_token,
    adapter_rank_bucket,
    adapter_owner_slot,
    live_token_counts,
):
    n_tensor = lax.axis_size("tensor")
    n_chip = n_tensor // 2
    tokens = cotangent.shape[0]
    rows_own, width = hidden.shape
    columns = width // n_tensor
    n_slot = adapter_owner_slot.shape[0]

    blocks = hidden.reshape(rows_own, n_tensor, columns).transpose(1, 0, 2)
    hidden_columns = lax.all_to_all(blocks, "tensor", 0, 0, tiled=True).reshape(tokens, columns)

    masked, rows, pair_rows, slot_wide, factor_wide, place, up_own = prep(
        rows_own,
        live_token_counts,
        adapter_rank_bucket,
        adapter_owner_slot,
        adapter_of_token.reshape(1, tokens),
        cotangent,
        adapter_up_factors,
    )

    pair_rows = swap(pair_rows, 1, n_tensor)
    pair_frozen = swap(frozen_key_value, 1, n_tensor)
    slot_wide, pair_rows = lax.optimization_barrier((slot_wide, pair_rows))

    own, theirs = low_rank(hidden_columns, slot_wide, up_own, adapter_down_factors)
    own = sum_over_chips(own + swap(theirs, 1, n_tensor), n_tensor)
    other = swap(own, 1, n_tensor)
    low_core = lax.axis_index("tensor") % 2 == 0
    summed = jnp.concatenate(
        [jnp.where(low_core, own, other), jnp.where(low_core, other, own)], axis=0
    )
    weights = (summed * factor_wide).astype(jnp.bfloat16)

    packed = pack_rows(place, [hidden_columns, masked, weights], n_slot * CAP)
    packed, weights = lax.optimization_barrier((packed, weights))
    extra_ours, extra_theirs = extra_term(rows_own, weights, slot_wide, adapter_down_factors)
    owned = lax.all_to_all(
        packed.reshape(n_slot, CAP, -1), "dp", 0, 0, tiled=True
    ).reshape(n_slot * CAP, -1)

    total, *sent = pair_sum(
        rows_own,
        rows,
        pair_rows,
        extra_ours,
        swap(extra_theirs, 1, n_tensor),
        frozen_key_value,
        pair_frozen,
    )
    for step, value in enumerate(sent, 1):
        arrived = lax.ppermute(
            value, "tensor", [(i, (i + 2 * step) % n_tensor) for i in range(n_tensor)]
        )
        total = total + arrived.astype(jnp.float32)
    hidden_gradient = total.astype(jnp.bfloat16)

    owned, hidden_gradient = lax.optimization_barrier((owned, hidden_gradient))
    down_states = (down_master_copy.T, down_first_moment.T, down_second_moment.T)
    up_states = (up_master_copy, up_first_moment, up_second_moment)
    updated = owners_update(
        owned, columns, cotangent.shape[1], tokens, (*down_states, *up_states)
    )
    new_dm, new_dmo, new_ds = (value.T for value in updated[:3])
    new_um, new_umo, new_us = updated[3:]
    return (hidden_gradient, new_dm, new_dmo, new_ds, new_um, new_umo, new_us)


def solution(mesh):
    return jax.shard_map(
        local,
        mesh=mesh,
        in_specs=(
            P(("dp", "tensor"), None),
            P("dp", "tensor"),
            P(None, "tensor"),
            P("tensor", None),
            P(None, "tensor"),
            P("tensor", "dp"),
            P("tensor", "dp"),
            P("tensor", "dp"),
            P("dp", "tensor"),
            P("dp", "tensor"),
            P("dp", "tensor"),
            P("dp", None),
            P(),
            P(),
            P(),
        ),
        out_specs=(
            P(("dp", "tensor"), None),
            P("tensor", "dp"),
            P("tensor", "dp"),
            P("tensor", "dp"),
            P("dp", "tensor"),
            P("dp", "tensor"),
            P("dp", "tensor"),
        ),
        check_vma=False,
    )
```
